32 devices in a mesh: dp: 2 (over x), row: 4 (over z), col: 4 (over y, core).
Axes of the slice: x: 2, y: 2, z: 4, core: 2. Of those that a mesh axis runs over, the one named last changes fastest.
Arguments:
- tokens: bfloat16 [4, 1024, 2048], P('dp', 'col', 'row'), may hold values from -6 to 6
- query_weight: bfloat16 [2048, 2048], P('row', 'col'), may hold values from -0.1875 to 0.1875
- key_weight: bfloat16 [2048, 2048], P('row', 'col'), may hold values from -0.1875 to 0.1875
- value_weight: bfloat16 [2048, 2048], P('row', 'col'), may hold values from -0.23201941 to 0.23201941
- out_weight: bfloat16 [2048, 2048], P('col', 'row'), may hold values from -0.75 to 0.75
- gate_weight: bfloat16 [2048, 8192], P('row', 'col'), may hold values from -0.23201941 to 0.23201941
- up_weight: bfloat16 [2048, 8192], P('row', 'col'), may hold values from -0.125 to 0.125
- down_weight: bfloat16 [8192, 2048], P('col', 'row'), may hold values from -0.0625 to 0.0625
- cotangent: bfloat16 [4, 1024, 2048], P('dp', 'col', 'row'), may hold values from -6 to 6
Outputs:
- layer_out: bfloat16 [4, 1024, 2048], P('dp', 'col', 'row')
- input_grad: float32 [4, 1024, 2048], P('dp', 'col', 'row')
- query_grad: float32 [2048, 2048], P('row', 'col')
- key_grad: float32 [2048, 2048], P('row', 'col')
- value_grad: float32 [2048, 2048], P('row', 'col')
- output_grad: float32 [2048, 2048], P('col', 'row')
- gate_grad: float32 [2048, 8192], P('row', 'col')
- up_grad: float32 [2048, 8192], P('row', 'col')
- down_grad: float32 [8192, 2048], P('col', 'row')
The draws below stay inside these ranges and needn't reach their ends.
All inputs are finite; a program needn't handle non-finite values.
Results may differ from the reference program's by a relative error of at most 0.03.
Values may be sent and summed in bfloat16 or wider, within the bound.
No kernel may reach another device: no remote copies, remote signals or barrier semaphores. Data moves between devices by JAX's collectives and lax.ppermute only.
A program may use at most 192 MiB of HBM per device.

```python
import jax
import jax.numpy as jnp
from jax import lax

HEADS = 16
HEAD_DIM = 128
D = 2048
FF = 8192
SEQ = 1024
SEQS = 4


def column_shifted(key, rows, columns):
    noise_key = jax.random.fold_in(key, 101)
    shift_key = jax.random.fold_in(key, 202)
    noise = jnp.clip(jax.random.normal(noise_key, (rows, columns), jnp.float32), -6.0, 6.0)
    shifts = jnp.clip(1.5 * jax.random.normal(shift_key, (1, columns), jnp.float32), -4.5, 4.5)
    return ((noise + shifts) * rows ** (-0.5)).astype(jnp.bfloat16)


def draw_value_weight(key, part):
    return column_shifted(key, D, D)


def draw_gate_weight(key, part):
    return column_shifted(key, D, FF)


def steps_of(key, dims, cuts, smallest, top_value):
    gain, own = 1.0, jax.random.fold_in(key, 6)
    for axis_at, parts in cuts:
        steps = jnp.exp(jax.random.uniform(jax.random.fold_in(own, axis_at), (parts,), jnp.float32, smallest / len(cuts), top_value / len(cuts)))
        gain = gain * jnp.repeat(steps, dims[axis_at] // parts).reshape([-1 if axis == axis_at else 1 for axis in range(len(dims))])
    return gain


def normal_values(key, extent, width, bound, split=(), dtype=jnp.bfloat16):
    drawn = jax.random.normal(key, extent, jnp.float32) * width
    if len(split) > 0:
        drawn = steps_of(key, extent, split, -0.22, 0.18) * drawn
    return jnp.clip(drawn, min=-bound, max=bound).astype(dtype)


def setup_inputs(seed: int = 0) -> dict:
    keys = jax.random.split(jax.random.key(seed), 10)
    return {
        "tokens": normal_values(keys[0], (SEQS, SEQ, D), 1.0, 6.0, ((0, 2), (1, 4), (2, 4))),
        "query_weight": normal_values(keys[1], (D, D), (D // 2) ** -0.5, 0.1875, ((0, 4), (1, 4))),
        "key_weight": normal_values(keys[2], (D, D), (D // 2) ** -0.5, 0.1875, ((0, 4), (1, 4))),
        "value_weight": draw_value_weight(jax.random.fold_in(keys[9], 71), 0),
        "out_weight": normal_values(keys[4], (D, D), (D // 32) ** -0.5, 0.75, ((0, 4), (1, 4))),
        "gate_weight": draw_gate_weight(jax.random.fold_in(keys[9], 71), 0),
        "up_weight": normal_values(keys[6], (D, FF), D ** -0.5, 0.125, ((0, 4), (1, 4))),
        "down_weight": normal_values(keys[7], (FF, D), FF ** -0.5, 0.0625, ((0, 4), (1, 4))),
        "cotangent": normal_values(keys[8], (SEQS, SEQ, D), 1.0, 6.0, ((0, 2), (1, 4), (2, 4))),
    }


epsilon = 1e-05
rope_base = 10000.0
masked_score = -1e+30

@jax.custom_vjp
def low(v):
    return lax.optimization_barrier(v.astype(jnp.bfloat16)).astype(jnp.float32)

@jax.custom_vjp
def low_back(v):
    return v

def low_keep(v):
    return (low(v), None)

def low_pass(kept, grad):
    return (grad,)

def back_keep(v):
    return (v, None)

def back_low(kept, grad):
    return (low(grad),)
low.defvjp(low_keep, low_pass)
low_back.defvjp(back_keep, back_low)

def matmul(left, right):
    return jnp.dot(left, right, precision=lax.Precision.HIGHEST)

def layer_norm(stream):
    average = lax.optimization_barrier(jnp.mean(stream, axis=-1, keepdims=True))
    centered = stream - average
    spread = lax.optimization_barrier(jnp.mean(centered * centered, axis=-1, keepdims=True))
    return centered * lax.rsqrt(spread + epsilon)

def rope_tables(length, head_depth):
    halfway = head_depth // 2
    position = jnp.arange(length).astype(jnp.float32)[:, None]
    frequency = rope_base ** (-(2.0 * jnp.arange(halfway).astype(jnp.float32)) / head_depth)
    angles = position * frequency[None, :]
    cosine = jnp.concatenate([jnp.cos(angles), jnp.cos(angles)], axis=1)
    sine_table = jnp.concatenate([jnp.sin(angles), jnp.sin(angles)], axis=1)
    return (cosine, sine_table)

def rope_apply(vector, cosine, sine_table):
    halfway = vector.shape[-1] // 2
    turned = jnp.concatenate([-vector[..., halfway:], vector[..., :halfway]], axis=-1)
    return vector * cosine + turned * sine_table

def head_attend(head_parts):
    queries, key_rows, values = head_parts
    length = queries.shape[0]
    scaling = queries.shape[1] ** (-0.5)
    scores = low_back(scaling * matmul(queries, key_rows.T))
    position = jnp.arange(length)
    scores = jnp.where(position[:, None] >= position[None, :], scores, masked_score)
    weights = jax.nn.softmax(scores, axis=-1)
    return matmul(low(weights), values)

def layer_forward(stream, query_weight, key_weight, value_weight, out_weight, gate_weight, up_weight, down_weight):
    length = stream.shape[0]
    cosine, sine_table = rope_tables(length, HEAD_DIM)
    normed_one = low(layer_norm(stream))
    query_sum = low_back(matmul(normed_one, query_weight)).reshape(length, HEADS, HEAD_DIM)
    key_sum = low_back(matmul(normed_one, key_weight)).reshape(length, HEADS, HEAD_DIM)
    value_sum = low(low_back(matmul(normed_one, value_weight))).reshape(length, HEADS, HEAD_DIM)
    queries = low(rope_apply(query_sum, cosine[:, None, :], sine_table[:, None, :]))
    key_rows = low(rope_apply(key_sum, cosine[:, None, :], sine_table[:, None, :]))
    attended = lax.map(jax.checkpoint(head_attend), (jnp.transpose(queries, (1, 0, 2)), jnp.transpose(key_rows, (1, 0, 2)), jnp.transpose(value_sum, (1, 0, 2))))
    heads_all = low(low_back(jnp.transpose(attended, (1, 0, 2)).reshape(length, HEADS * HEAD_DIM)))
    middle = stream + low_back(matmul(heads_all, out_weight))
    normed_two = low(layer_norm(middle))
    gate_sum = low_back(matmul(normed_two, gate_weight))
    up_sum = low_back(matmul(normed_two, up_weight))
    hidden = low(jax.nn.silu(gate_sum) * up_sum)
    return middle + low_back(matmul(hidden, down_weight))

def reference(tokens, query_weight, key_weight, value_weight, out_weight, gate_weight, up_weight, down_weight, cotangent):
    matrices = (query_weight.astype(jnp.float32), key_weight.astype(jnp.float32), value_weight.astype(jnp.float32), out_weight.astype(jnp.float32), gate_weight.astype(jnp.float32), up_weight.astype(jnp.float32), down_weight.astype(jnp.float32))

    def one_sequence(totals, sequence_pair):
        stream, slopes_in = sequence_pair
        result, pullback = jax.vjp(layer_forward, stream.astype(jnp.float32), matrices[0], matrices[1], matrices[2], matrices[3], matrices[4], matrices[5], matrices[6])
        gradients = pullback(slopes_in.astype(jnp.float32))
        totals = tuple((summed + fresh for summed, fresh in zip(totals, gradients[1:])))
        return (totals, (result.astype(jnp.bfloat16), gradients[0]))
    starting = tuple((jnp.zeros(matrix.shape, jnp.float32) for matrix in matrices))
    totals, (layer_out, input_grad) = lax.scan(one_sequence, starting, (tokens, cotangent))
    return (layer_out, input_grad, totals[0], totals[1], totals[2], totals[3], totals[4], totals[5], totals[6])
```

```python
import jax
import jax.numpy as jnp
from jax import lax
from jax.sharding import Mesh
from jax.sharding import PartitionSpec as P

HEAD_DIM = 128
BLOCK = 512
CORES = 2

epsilon = 1e-05
rope_base = 10000.0
masked_score = -1e30
low = jnp.bfloat16
wide = jnp.float32


def rope_tables(length, head_depth):
    halfway = head_depth // 2
    position = jnp.arange(length).astype(jnp.float32)[:, None]
    frequency = rope_base ** (-(2.0 * jnp.arange(halfway).astype(jnp.float32)) / head_depth)
    angles = position * frequency[None, :]
    cosine = jnp.concatenate([jnp.cos(angles), jnp.cos(angles)], axis=1)
    sine_table = jnp.concatenate([jnp.sin(angles), jnp.sin(angles)], axis=1)
    return (cosine, sine_table)


def rope_apply(vector, cosine, sine_table):
    halfway = vector.shape[-1] // 2
    turned = jnp.concatenate([-vector[..., halfway:], vector[..., :halfway]], axis=-1)
    return vector * cosine + turned * sine_table


def rope_undo(gradient, cosine, sine_table):
    halfway = gradient.shape[-1] // 2
    scaled = gradient * sine_table
    turned = jnp.concatenate([scaled[..., halfway:], -scaled[..., :halfway]], axis=-1)
    return gradient * cosine + turned


def dot(left, right):
    return jnp.dot(left, right, preferred_element_type=wide)


def dot_nt(left, right):
    return jnp.einsum("mk,nk->mn", left, right, preferred_element_type=wide)


def dot_tn(left, right):
    return jnp.einsum("km,kn->mn", left, right, preferred_element_type=wide)


def layer_norm(stream):
    average = jnp.mean(stream, axis=1, keepdims=True)
    centered = stream - average
    inverse = lax.rsqrt(jnp.mean(centered * centered, axis=1, keepdims=True) + epsilon)
    return centered * inverse, inverse


def norm_backward(normed, inverse, gradient):
    average = jnp.mean(gradient, axis=1, keepdims=True)
    crossed = jnp.mean(gradient * normed, axis=1, keepdims=True)
    return inverse * (gradient - average - normed * crossed)


def causal_mask(number, block_rows, finish):
    query_place = number * block_rows + jnp.arange(block_rows)
    key_place = jnp.arange(finish)
    return query_place[:, None] >= key_place[None, :]


def attend_forward(queries, key_rows, values, block_rows):
    scaling = queries.shape[1] ** (-0.5)
    outputs = []
    logsums = []
    for number in range(queries.shape[0] // block_rows):
        opening = number * block_rows
        finish = opening + block_rows
        scores = dot_nt(queries[opening:finish], key_rows[:finish]) * scaling
        scores = jnp.where(causal_mask(number, block_rows, finish), scores, masked_score)
        highest = jnp.max(scores, axis=1, keepdims=True)
        shifted = jnp.exp(scores - highest)
        totals = jnp.sum(shifted, axis=1, keepdims=True)
        logsums.append(highest + jnp.log(totals))
        weights = (shifted / totals).astype(low)
        outputs.append(dot(weights, values[:finish]))
    return (jnp.concatenate(outputs, axis=0), jnp.concatenate(logsums, axis=0))


def attend_backward(queries, key_rows, values, logsums, grad_low, block_rows):
    scaling = queries.shape[1] ** (-0.5)
    query_parts = []
    key_grad = jnp.zeros(key_rows.shape, wide)
    value_grad = jnp.zeros(values.shape, wide)
    for number in range(queries.shape[0] // block_rows):
        opening = number * block_rows
        finish = opening + block_rows
        query_block = queries[opening:finish]
        grad_block = grad_low[opening:finish]
        scores = dot_nt(query_block, key_rows[:finish]) * scaling
        scores = jnp.where(causal_mask(number, block_rows, finish), scores, masked_score)
        probable = jnp.exp(scores - logsums[opening:finish])
        weights = probable.astype(low)
        product = dot_nt(grad_block, values[:finish])
        slopes = probable * (product - jnp.sum(probable * product, axis=1, keepdims=True))
        slopes_low = slopes.astype(low)
        query_parts.append(dot(slopes_low, key_rows[:finish]) * scaling)
        key_grad = key_grad.at[:finish].add(dot_tn(slopes_low, query_block) * scaling)
        value_grad = value_grad.at[:finish].add(dot_tn(weights, grad_block))
    return (jnp.concatenate(query_parts, axis=0), key_grad, value_grad)


class Layout:
    def __init__(self, dp, rows):
        self.dp = dp
        self.rows = rows
        self.ring = 2 * rows
        place = lambda number: (number, 0) if number < rows else (2 * rows - 1 - number, 1)
        flat = [place(number)[0] * 2 + place(number)[1] for number in range(self.ring)]
        self.flat = flat
        self.onward = [(flat[i], flat[(i + 1) % self.ring]) for i in range(self.ring)]
        self.backward = [(b, a) for a, b in self.onward]

    def locate(self):
        self.d = lax.axis_index("dp")
        self.r = lax.axis_index("row")
        self.y = lax.axis_index("y")
        self.c = lax.axis_index("core")
        self.place = jnp.where(self.y == 0, self.r, self.ring - 1 - self.r)

    def swap_core(self, array):
        return lax.ppermute(array, "core", [(0, 1), (1, 0)])

    def ordered(self, mine, theirs):
        first = jnp.where(self.c == 0, mine, theirs)
        second = jnp.where(self.c == 0, theirs, mine)
        return jnp.stack([first, second])

    def exchange_rows(self, array):
        return lax.all_to_all(array, "row", 0, 0, tiled=True)

    def exchange_ring(self, array):
        by_flat = [0] * self.ring
        for place, flat in enumerate(self.flat):
            by_flat[flat] = place
        sent = jnp.stack([array[place] for place in by_flat])
        got = lax.all_to_all(sent, ("row", "y"), 0, 0, tiled=True)
        return jnp.stack([got[flat] for flat in self.flat])

    def flip(self, array):
        return jnp.where(self.y == 0, array, array[::-1])

    def to_shard(self, array):
        mine = lax.dynamic_index_in_dim(array, self.c, 0, keepdims=False)
        other = lax.dynamic_index_in_dim(array, 1 - self.c, 0, keepdims=False)
        both = self.ordered(mine, self.swap_core(other))
        tokens, width = 2 * array.shape[1], array.shape[2]
        pieces = self.flip(both.reshape(self.rows, tokens // self.rows, width))
        got = self.exchange_rows(pieces)
        return jnp.transpose(got, (1, 0, 2)).reshape(tokens // self.rows, self.rows * width)

    def from_shard(self, array):
        tokens, width = array.shape[0], array.shape[1] // self.rows
        pieces = jnp.transpose(array.reshape(tokens, self.rows, width), (1, 0, 2))
        got = self.flip(self.exchange_rows(pieces))
        both = got.reshape(CORES, self.rows * tokens // CORES, width)
        mine = lax.dynamic_index_in_dim(both, self.c, 0, keepdims=False)
        other = lax.dynamic_index_in_dim(both, 1 - self.c, 0, keepdims=False)
        return self.ordered(mine, self.swap_core(other))

    def gather_ring(self, shard):
        half = self.ring // 2
        slots = [None] * self.ring
        slots[half] = shard
        up = down = shard
        for step in range(1, half + 1):
            up = lax.ppermute(up, ("row", "y"), self.onward)
            slots[half - step] = up
            if step < half:
                down = lax.ppermute(down, ("row", "y"), self.backward)
                slots[half + step] = down
        return jnp.concatenate(slots, axis=0)

    def scatter_ring(self, partial):
        half = self.ring // 2
        rows = partial.shape[0] // self.ring
        part = lambda slot: partial[slot * rows : (slot + 1) * rows]
        up, down = part(self.ring - 1), part(0)
        for step in range(1, half + 1):
            down = lax.ppermute(down, ("row", "y"), self.backward)
            if step < half:
                down = (down.astype(wide) + part(step).astype(wide)).astype(low)
                up = lax.ppermute(up, ("row", "y"), self.onward)
                if step < half - 1:
                    up = (up.astype(wide) + part(self.ring - 1 - step).astype(wide)).astype(low)
        return part(half).astype(wide) + up.astype(wide) + down.astype(wide)

    def roll_to_order(self, array):
        rows = array.shape[0] // self.ring
        start = ((self.ring + self.ring // 2 - self.place) % self.ring) * rows
        return lax.dynamic_slice_in_dim(
            jnp.concatenate([array, array], axis=0), start, array.shape[0], 0
        )

    def roll_to_ring(self, array):
        rows = array.shape[0] // self.ring
        start = ((self.ring + self.place - self.ring // 2) % self.ring) * rows
        return lax.dynamic_slice_in_dim(
            jnp.concatenate([array, array], axis=0), start, array.shape[0], 0
        )

    def dp_turn(self, array, step):
        return lax.ppermute(
            array, "dp", [(i, (i + step) % self.dp) for i in range(self.dp)]
        )

    def dp_gather(self, array):
        shape = (array.shape[0], self.dp) + array.shape[1:]
        whole = jnp.zeros(shape, array.dtype)
        for step in range(self.dp):
            got = array if step == 0 else self.dp_turn(array, step)
            source = (self.d + self.dp - step) % self.dp
            whole = lax.dynamic_update_slice_in_dim(whole, got[:, None], source, 1)
        return whole

    def dp_scatter(self, array):
        total = lax.dynamic_index_in_dim(array, self.d, 1, keepdims=False).astype(wide)
        for step in range(1, self.dp):
            target = (self.d + step) % self.dp
            sent = lax.dynamic_index_in_dim(array, target, 1, keepdims=False)
            total = total + self.dp_turn(sent, step).astype(wide)
        return total.astype(low)

    def spread_weight(self, pieces):
        rows, n, m = pieces.shape
        parts = pieces.reshape(rows, self.dp, n // self.dp, m)
        mine = lax.dynamic_index_in_dim(parts, self.d, 1, keepdims=False)
        got = self.exchange_rows(mine)
        return self.dp_gather(got).reshape(rows, n, m)

    def collect_grad(self, own, other):
        rows, n, m = own.shape
        total = own + self.swap_core(other.astype(low)).astype(wide)
        parts = total.astype(low).reshape(rows, self.dp, n // self.dp, m)
        summed = self.dp_scatter(parts)
        got = self.exchange_rows(summed)
        return self.dp_gather(got).reshape(rows, n, m)


def on_device(
    layout,
    tokens,
    query_weight,
    key_weight,
    value_weight,
    out_weight,
    gate_weight,
    up_weight,
    down_weight,
    cotangent,
):
    layout.locate()
    rows, ring = layout.rows, layout.ring
    depth = HEAD_DIM

    stream = layout.to_shard(tokens).astype(wide)
    slope_low = layout.to_shard(cotangent)
    shard, width = stream.shape
    length = shard * ring
    normed_one, inverse_one = layer_norm(stream)
    rows_one = layout.gather_ring(normed_one.astype(low))

    block = query_weight.shape[0]
    heads_of = lambda weight: jnp.transpose(weight.reshape(block, rows, depth), (1, 0, 2))
    qkv_own = layout.spread_weight(
        jnp.concatenate([heads_of(query_weight), heads_of(key_weight), heads_of(value_weight)], axis=2)
    ).reshape(width, 3 * depth)
    qkv_other = layout.swap_core(qkv_own)

    hidden = gate_weight.shape[1] // rows
    units_of = lambda weight: jnp.transpose(weight.reshape(block, rows, hidden), (1, 0, 2))
    gu_own = layout.spread_weight(
        jnp.concatenate([units_of(gate_weight), units_of(up_weight)], axis=2)
    ).reshape(width, 2 * hidden)
    gu_other = layout.swap_core(gu_own)
    down_own = jnp.transpose(
        layout.spread_weight(down_weight.reshape(rows, hidden, block)), (1, 0, 2)
    ).reshape(hidden, width)
    down_other = layout.swap_core(down_own)

    out_mine = jnp.transpose(
        layout.exchange_rows(out_weight.reshape(rows, depth, block)), (1, 0, 2)
    ).reshape(depth, width)
    out_half = lax.all_gather(out_mine, ("row", "y"), axis=0, tiled=False)
    out_all = jnp.stack([out_half, layout.swap_core(out_half)], axis=1)
    flat = jnp.array(layout.flat)
    out_all = out_all[flat].reshape(ring * 2 * depth, width)

    cosine, sine_table = rope_tables(length, depth)
    qkv = layout.roll_to_order(
        jnp.concatenate([dot(rows_one, qkv_own), dot(rows_one, qkv_other)], axis=1)
    )
    head_parts = []
    for head in range(2):
        at = 3 * depth * head
        queries = rope_apply(qkv[:, at : at + depth], cosine, sine_table).astype(low)
        key_rows = rope_apply(qkv[:, at + depth : at + 2 * depth], cosine, sine_table).astype(low)
        values = qkv[:, at + 2 * depth : at + 3 * depth].astype(low)
        attended, logsums = attend_forward(queries, key_rows, values, BLOCK)
        head_parts.append((queries, key_rows, values, logsums, attended.astype(low)))
    heads = jnp.concatenate([part[4] for part in head_parts], axis=1)

    heads_shard = jnp.transpose(
        layout.exchange_ring(heads.reshape(ring, shard, 2 * depth)), (1, 0, 2)
    ).reshape(shard, ring * 2 * depth)
    middle = stream + dot(heads_shard, out_all)
    normed_two, inverse_two = layer_norm(middle)
    rows_two = layout.gather_ring(normed_two.astype(low))
    slope_all = layout.gather_ring(slope_low)

    def feed_forward(gu_weight, down_part):
        gate_up = dot(rows_two, gu_weight)
        gate_sum, up_sum = gate_up[:, :hidden], gate_up[:, hidden:]
        sigmoid = jax.nn.sigmoid(gate_sum)
        activated = gate_sum * sigmoid
        hidden_low = (activated * up_sum).astype(low)
        hidden_grad = dot_nt(slope_all, down_part)
        up_slope = (hidden_grad * activated).astype(low)
        gate_slope = (hidden_grad * up_sum * sigmoid * (1.0 + gate_sum * (1.0 - sigmoid))).astype(low)
        return hidden_low, jnp.concatenate([gate_slope, up_slope], axis=1)

    hidden_own, gu_slope_own = feed_forward(gu_own, down_own)
    hidden_other, gu_slope_other = feed_forward(gu_other, down_other)
    grad_two = layout.scatter_ring(
        (dot_nt(gu_slope_own, gu_own) + dot_nt(gu_slope_other, gu_other)).astype(low)
    )
    middle_grad = slope_low.astype(wide) + norm_backward(normed_two, inverse_two, grad_two)
    middle_low = middle_grad.astype(low)
    head_slope = dot_nt(middle_low, out_all).astype(low)
    head_grad = layout.exchange_ring(
        jnp.transpose(head_slope.reshape(shard, ring, 2 * depth), (1, 0, 2))
    ).reshape(length, 2 * depth)

    slopes = []
    for head in range(2):
        queries, key_rows, values, logsums, _ = head_parts[head]
        query_rot, key_rot, value_slope = attend_backward(
            queries, key_rows, values, logsums, head_grad[:, head * depth : (head + 1) * depth], BLOCK
        )
        slopes += [
            rope_undo(query_rot, cosine, sine_table).astype(low),
            rope_undo(key_rot, cosine, sine_table).astype(low),
            value_slope.astype(low),
        ]
    qkv_slope = layout.roll_to_ring(jnp.concatenate(slopes, axis=1))
    slope_own, slope_other = qkv_slope[:, : 3 * depth], qkv_slope[:, 3 * depth :]
    grad_one = layout.scatter_ring(
        (dot_nt(slope_own, qkv_own) + dot_nt(slope_other, qkv_other)).astype(low)
    )
    input_grad = layout.from_shard(
        middle_grad + norm_backward(normed_one, inverse_one, grad_one)
    )

    branch = layout.scatter_ring(
        (dot(hidden_own, down_own) + dot(hidden_other, down_other)).astype(low)
    )
    layer_out = layout.from_shard((middle + branch).astype(low))

    gu_grad = layout.collect_grad(
        dot_tn(rows_two, gu_slope_own).reshape(rows, block, 2 * hidden),
        dot_tn(rows_two, gu_slope_other).reshape(rows, block, 2 * hidden),
    )
    units_back = lambda grad: jnp.transpose(grad, (1, 0, 2)).reshape(block, rows * hidden).astype(wide)
    gate_grad = units_back(gu_grad[:, :, :hidden])
    up_grad = units_back(gu_grad[:, :, hidden:])
    by_block = lambda grad: jnp.transpose(grad.reshape(-1, rows, block), (1, 0, 2))
    down_grad = layout.collect_grad(
        by_block(dot_tn(hidden_own, slope_all)), by_block(dot_tn(hidden_other, slope_all))
    ).reshape(rows * hidden, block).astype(wide)
    middle_all = layout.gather_ring(middle_low)
    out_sum = by_block(dot_tn(layout.roll_to_ring(heads), middle_all))
    out_grad = layout.collect_grad(out_sum[:, :depth], out_sum[:, depth:])
    out_grad = out_grad.reshape(rows * depth, block).astype(wide)
    qkv_grad = layout.collect_grad(
        dot_tn(rows_one, slope_own).reshape(rows, block, 3 * depth),
        dot_tn(rows_one, slope_other).reshape(rows, block, 3 * depth),
    )
    heads_back = lambda grad: jnp.transpose(grad, (1, 0, 2)).reshape(block, rows * depth).astype(wide)
    query_grad = heads_back(qkv_grad[:, :, :depth])
    key_grad = heads_back(qkv_grad[:, :, depth : 2 * depth])
    value_grad = heads_back(qkv_grad[:, :, 2 * depth :])
    return (
        layer_out,
        input_grad,
        query_grad,
        key_grad,
        value_grad,
        out_grad,
        gate_grad,
        up_grad,
        down_grad,
    )


def solution(mesh):
    dp, rows, cols = (mesh.shape[name] for name in ("dp", "row", "col"))
    fine = Mesh(
        mesh.devices.reshape(dp, rows, cols // CORES, CORES), ("dp", "row", "y", "core")
    )
    layout = Layout(dp, rows)
    split = P("dp", ("y", "core"), "row")
    inward = P("row", ("y", "core"))
    outward = P(("y", "core"), "row")

    def program(*arrays):
        return on_device(layout, *arrays)

    return jax.shard_map(
        program,
        mesh=fine,
        in_specs=(split, inward, inward, inward, outward, inward, inward, outward, split),
        out_specs=(split, split, inward, inward, inward, outward, inward, inward, outward),
        check_vma=False,
    )
```

```python
import jax
import jax.numpy as jnp
from jax import lax
from jax.sharding import Mesh
from jax.sharding import PartitionSpec as P

HEAD_DIM = 128
BLOCK = 512
HALF = 2

epsilon = 1e-05
rope_base = 10000.0
masked_score = -1e30
low = jnp.bfloat16
wide = jnp.float32


def rope_tables(places, head_depth):
    halfway = head_depth // 2
    position = places.astype(jnp.float32)[:, None]
    frequency = rope_base ** (-(2.0 * jnp.arange(halfway).astype(jnp.float32)) / head_depth)
    angles = position * frequency[None, :]
    cosine = jnp.concatenate([jnp.cos(angles), jnp.cos(angles)], axis=1)
    sine_table = jnp.concatenate([jnp.sin(angles), jnp.sin(angles)], axis=1)
    return (cosine, sine_table)


def rope_apply(vector, cosine, sine_table):
    halfway = vector.shape[-1] // 2
    turned = jnp.concatenate([-vector[..., halfway:], vector[..., :halfway]], axis=-1)
    return vector * cosine + turned * sine_table


def rope_undo(gradient, cosine, sine_table):
    halfway = gradient.shape[-1] // 2
    scaled = gradient * sine_table
    turned = jnp.concatenate([scaled[..., halfway:], -scaled[..., :halfway]], axis=-1)
    return gradient * cosine + turned


def dot(left, right):
    return jnp.dot(left, right, preferred_element_type=wide)


def dot_nt(left, right):
    return jnp.einsum("mk,nk->mn", left, right, preferred_element_type=wide)


def dot_tn(left, right):
    return jnp.einsum("km,kn->mn", left, right, preferred_element_type=wide)


def layer_norm(stream):
    average = jnp.mean(stream, axis=1, keepdims=True)
    centered = stream - average
    inverse = lax.rsqrt(jnp.mean(centered * centered, axis=1, keepdims=True) + epsilon)
    return centered * inverse, inverse


def norm_backward(normed, inverse, gradient):
    average = jnp.mean(gradient, axis=1, keepdims=True)
    crossed = jnp.mean(gradient * normed, axis=1, keepdims=True)
    return inverse * (gradient - average - normed * crossed)


def attend_forward(queries, key_rows, values, places, block_rows):
    scaling = queries.shape[1] ** (-0.5)
    outputs = []
    logsums = []
    for opening in range(0, queries.shape[0], block_rows):
        finish = opening + block_rows
        scores = dot_nt(queries[opening:finish], key_rows) * scaling
        seen = places[opening:finish, None] >= places[None, :]
        scores = jnp.where(seen, scores, masked_score)
        highest = jnp.max(scores, axis=1, keepdims=True)
        shifted = jnp.exp(scores - highest)
        totals = jnp.sum(shifted, axis=1, keepdims=True)
        logsums.append(highest + jnp.log(totals))
        weights = (shifted / totals).astype(low)
        outputs.append(dot(weights, values))
    return (jnp.concatenate(outputs, axis=0), jnp.concatenate(logsums, axis=0))


def attend_backward(queries, key_rows, values, places, logsums, grad_low, block_rows):
    scaling = queries.shape[1] ** (-0.5)
    query_parts = []
    key_grad = jnp.zeros(key_rows.shape, wide)
    value_grad = jnp.zeros(values.shape, wide)
    for opening in range(0, queries.shape[0], block_rows):
        finish = opening + block_rows
        query_block = queries[opening:finish]
        grad_block = grad_low[opening:finish]
        scores = dot_nt(query_block, key_rows) * scaling
        seen = places[opening:finish, None] >= places[None, :]
        scores = jnp.where(seen, scores, masked_score)
        probable = jnp.exp(scores - logsums[opening:finish])
        weights = probable.astype(low)
        product = dot_nt(grad_block, values)
        slopes = probable * (product - jnp.sum(probable * product, axis=1, keepdims=True))
        slopes_low = slopes.astype(low)
        query_parts.append(dot(slopes_low, key_rows) * scaling)
        key_grad = key_grad + dot_tn(slopes_low, query_block) * scaling
        value_grad = value_grad + dot_tn(weights, grad_block)
    return (jnp.concatenate(query_parts, axis=0), key_grad, value_grad)


def swap(array, axis):
    return lax.ppermute(array, axis, [(0, 1), (1, 0)])


class Ring:
    def __init__(self, axes, line):
        self.axes = axes
        self.size = 2 * line
        self.half = line
        flat = [2 * n if n < line else 2 * (2 * line - 1 - n) + 1 for n in range(self.size)]
        self.upward = [(flat[i], flat[(i + 1) % self.size]) for i in range(self.size)]
        self.downward = [(b, a) for a, b in self.upward]

    def up(self, array):
        return lax.ppermute(array, self.axes, self.upward)

    def down(self, array):
        return lax.ppermute(array, self.axes, self.downward)

    def gather(self, shard):
        half, cut = self.half, shard.shape[0] // 2
        slots = [None] * self.size
        slots[half] = rising = falling = shard
        for step in range(1, half):
            slots[half - step] = rising = self.up(rising)
            slots[half + step] = falling = self.down(falling)
        slots[0] = jnp.concatenate([self.up(rising[:cut]), self.down(falling[cut:])], axis=0)
        return slots

    def scatter(self, parts):
        half, cut = self.half, parts[0].shape[0] // 2
        rising, falling = self.up(parts[0][:cut]), self.down(parts[0][cut:])
        for step in range(1, half):
            over, under = parts[self.size - step], parts[step]
            if step == 1:
                over = jnp.concatenate([add_low(over[:cut], rising), over[cut:]], axis=0)
                under = jnp.concatenate([under[:cut], add_low(under[cut:], falling)], axis=0)
            else:
                over, under = add_low(over, rising), add_low(under, falling)
            rising, falling = self.up(over), self.down(under)
        return parts[half].astype(wide) + rising.astype(wide) + falling.astype(wide)


def add_low(left, right):
    return (left.astype(wide) + right.astype(wide)).astype(low)


def split_rows(array, count):
    rows = array.shape[0] // count
    return [array[i * rows : (i + 1) * rows] for i in range(count)]


def gather_group(ring, shard):
    slots = ring.gather(shard)
    return jnp.concatenate(slots + [swap(slot, "core") for slot in slots], axis=0)


def scatter_group(ring, partial):
    own, other = split_rows(partial, HALF)
    return ring.scatter(split_rows(add_low(own, swap(other, "core")), ring.size))


def exchange_rows(array):
    return lax.all_to_all(array, ROW, 0, 0, tiled=True)


ROW = ("zhi", "zlo")


def to_shard(array):
    rows = lax.axis_size(ROW)
    seqs, tokens, width = array.shape
    pieces = array.reshape(rows, seqs * tokens // rows, width)
    got = exchange_rows(pieces)
    return jnp.transpose(got, (1, 0, 2)).reshape(pieces.shape[1], rows * width)


def from_shard(array, seqs):
    rows = lax.axis_size(ROW)
    tokens, width = array.shape[0], array.shape[1] // rows
    pieces = jnp.transpose(array.reshape(tokens, rows, width), (1, 0, 2))
    return exchange_rows(pieces).reshape(seqs, rows * tokens // seqs, width)


def pick(array, index, axis):
    return lax.dynamic_index_in_dim(array, index, axis, keepdims=False)


def in_order(mine, theirs, axis):
    at_first = lax.axis_index("x") == 0
    return jnp.stack(
        [jnp.where(at_first, mine, theirs), jnp.where(at_first, theirs, mine)], axis=axis
    )


def sum_grad(mine, theirs):
    total = add_low(mine, swap(theirs, "x"))
    if lax.axis_size("pair") > 1:
        total = lax.psum(total, "pair")
    rows = lax.axis_size(ROW)
    return exchange_rows(total.reshape(rows, total.shape[0] // rows, total.shape[1]))


def on_device(
    tokens,
    query_weight,
    key_weight,
    value_weight,
    out_weight,
    gate_weight,
    up_weight,
    down_weight,
    cotangent,
):
    depth = HEAD_DIM
    rows, line = lax.axis_size(ROW), lax.axis_size("zlo")
    x_index = lax.axis_index("x")
    small_ring = Ring(("zlo", "y"), line)
    large_ring = Ring(("zhi", "zlo", "y"), rows)
    seqs, width = tokens.shape[0], tokens.shape[2] * rows
    block = width // rows

    stream = to_shard(tokens).astype(wide)
    slope_low = to_shard(cotangent)
    shard = stream.shape[0]

    def heads_of(weight):
        return pick(weight.reshape(block, line, HALF, depth), x_index, 2)

    head_mats = [query_weight, key_weight, value_weight, out_weight.T]
    head_pieces = jnp.transpose(
        jnp.concatenate([heads_of(weight) for weight in head_mats], axis=2), (1, 0, 2)
    )
    head_pieces = jnp.concatenate([head_pieces] * (rows // line), axis=0)
    head_mine = exchange_rows(head_pieces).reshape(width, 4 * depth)
    head_weights = [head_mine, swap(head_mine, "x")]

    units = gate_weight.shape[1] // rows // HALF

    def units_of(weight):
        return jnp.transpose(pick(weight.reshape(block, rows, HALF, units), x_index, 2), (1, 0, 2))

    def spread(pieces):
        mine = exchange_rows(pieces).reshape(width, pieces.shape[2])
        theirs = swap(mine, "x")
        return jnp.concatenate([mine, theirs, swap(mine, "core"), swap(theirs, "core")], axis=1)

    gu_weight = spread(jnp.concatenate([units_of(gate_weight), units_of(up_weight)], axis=2))
    down_turned = spread(units_of(down_weight.T))

    place = jnp.arange(2 * small_ring.size)
    core = (lax.axis_index("core") + place // small_ring.size) % 2
    side, level = lax.axis_index("y"), lax.axis_index("zlo")
    here = jnp.where(side == 0, level, small_ring.size - 1 - level)
    spot = (here + place % small_ring.size + small_ring.half) % small_ring.size
    slot_side = spot // line
    slot_level = jnp.where(slot_side == 0, spot, small_ring.size - 1 - spot)
    first = ((2 * slot_side + core) * line + slot_level) * shard
    places = (first[:, None] + jnp.arange(shard)[None, :]).reshape(-1)
    cosine, sine_table = rope_tables(places, depth)

    normed_one, inverse_one = layer_norm(stream)
    rows_one = gather_group(small_ring, normed_one.astype(low))
    kept = []
    for weight in head_weights:
        qkv = dot(rows_one, weight[:, : 3 * depth])
        queries = rope_apply(qkv[:, :depth], cosine, sine_table).astype(low)
        key_rows = rope_apply(qkv[:, depth : 2 * depth], cosine, sine_table).astype(low)
        values = qkv[:, 2 * depth :].astype(low)
        attended, logsums = attend_forward(queries, key_rows, values, places, BLOCK)
        kept.append((queries, key_rows, values, logsums, attended.astype(low)))
    heads = jnp.concatenate([part[4] for part in kept], axis=1)
    out_turned = jnp.concatenate([weight[:, 3 * depth :] for weight in head_weights], axis=1)
    middle = stream + scatter_group(small_ring, dot_nt(heads, out_turned).astype(low))
    normed_two, inverse_two = layer_norm(middle)
    rows_two = jnp.concatenate(large_ring.gather(normed_two.astype(low)), axis=0)
    slope_all = jnp.concatenate(large_ring.gather(slope_low), axis=0)

    blocks = 2 * HALF
    gate_up = dot(rows_two, gu_weight).reshape(-1, blocks, 2, units)
    gate_sum, up_sum = (gate_up[:, :, i].reshape(-1, blocks * units) for i in range(2))
    sigmoid = jax.nn.sigmoid(gate_sum)
    activated = gate_sum * sigmoid
    hidden_low = (activated * up_sum).astype(low)
    hidden_grad = dot(slope_all, down_turned)
    up_slope = (hidden_grad * activated).astype(low)
    gate_slope = (hidden_grad * up_sum * sigmoid * (1.0 + gate_sum * (1.0 - sigmoid))).astype(low)
    gu_slope = jnp.stack(
        [part.reshape(-1, blocks, units) for part in (gate_slope, up_slope)], axis=2
    ).reshape(-1, 2 * blocks * units)
    grad_two = large_ring.scatter(
        split_rows(dot_nt(gu_slope, gu_weight).astype(low), large_ring.size)
    )
    middle_grad = slope_low.astype(wide) + norm_backward(normed_two, inverse_two, grad_two)
    middle_all = gather_group(small_ring, middle_grad.astype(low))

    head_grad = dot(middle_all, out_turned).astype(low)
    head_slopes = []
    for head in range(HALF):
        queries, key_rows, values, logsums, _ = kept[head]
        query_rot, key_rot, value_slope = attend_backward(
            queries, key_rows, values, places, logsums, head_grad[:, head * depth : (head + 1) * depth], BLOCK
        )
        parts = [
            rope_undo(query_rot, cosine, sine_table),
            rope_undo(key_rot, cosine, sine_table),
            value_slope,
        ]
        head_slopes.append(jnp.concatenate([part.astype(low) for part in parts], axis=1))
    grad_one = scatter_group(
        small_ring,
        sum(
            dot_nt(slope, weight[:, : 3 * depth])
            for slope, weight in zip(head_slopes, head_weights)
        ).astype(low),
    )
    input_grad = from_shard(middle_grad + norm_backward(normed_one, inverse_one, grad_one), seqs)

    branch = large_ring.scatter(
        split_rows(dot_nt(hidden_low, down_turned).astype(low), large_ring.size)
    )
    layer_out = from_shard((middle + branch).astype(low), seqs)

    def unit_grad(left, right, size):
        own = dot_tn(left, right[:, : 2 * size])
        other = dot_tn(left, right[:, 2 * size :]).astype(low)
        total = add_low(own, swap(other, "core"))
        mine = sum_grad(total[:, :size], total[:, size:])
        return in_order(mine, swap(mine, "x"), 2).astype(wide)

    def unit_columns(grad):
        return jnp.transpose(grad, (1, 0, 2, 3)).reshape(block, -1)

    gu_grad = unit_grad(rows_two, gu_slope, 2 * units)
    gate_grad = unit_columns(gu_grad[:, :, :, :units])
    up_grad = unit_columns(gu_grad[:, :, :, units:])
    down_grad = unit_columns(unit_grad(slope_all, hidden_low, units)).T

    head_sums = []
    for head in range(HALF):
        qkv_sum = dot_tn(rows_one, head_slopes[head])
        out_sum = dot_tn(middle_all, kept[head][4])
        head_sums.append(jnp.concatenate([qkv_sum, out_sum], axis=1).astype(low))
    head_all = sum_grad(head_sums[0], head_sums[1]).reshape(rows // line, line, block, 4 * depth)
    head_total = jnp.sum(head_all.astype(wide), axis=0).astype(low)
    head_total = in_order(head_total, swap(head_total, "x"), 2).astype(wide)
    head_total = jnp.transpose(head_total, (1, 0, 2, 3))
    head_grads = [
        head_total[..., i * depth : (i + 1) * depth].reshape(block, -1) for i in range(4)
    ]
    return (
        layer_out,
        input_grad,
        head_grads[0],
        head_grads[1],
        head_grads[2],
        head_grads[3].T,
        gate_grad,
        up_grad,
        down_grad,
    )


def solution(mesh):
    dp, rows, cols = (mesh.shape[name] for name in ("dp", "row", "col"))
    sizes = (dp // HALF, HALF, HALF, rows // HALF, cols // HALF, HALF)
    fine = Mesh(mesh.devices.reshape(sizes), ("pair", "x", "zhi", "zlo", "y", "core"))
    across, inner, tall = ("pair", "x"), ("y", "core"), ROW
    split = P(across, inner, tall)
    inward = P(tall, inner)
    outward = P(inner, tall)
    return jax.shard_map(
        on_device,
        mesh=fine,
        in_specs=(split, inward, inward, inward, outward, inward, inward, outward, split),
        out_specs=(split, split, inward, inward, inward, outward, inward, inward, outward),
        check_vma=False,
    )
```

```python
import functools

import jax
import jax.numpy as jnp
from jax import lax
from jax.experimental import pallas as pl
from jax.experimental.pallas import tpu as pltpu
from jax.sharding import Mesh
from jax.sharding import PartitionSpec as P

HEAD_DIM = 128
BLOCK = 512
HALF = 2

epsilon = 1e-05
rope_base = 10000.0
masked_score = -1e30
low = jnp.bfloat16
wide = jnp.float32


def rope_tables(places, head_depth):
    halfway = head_depth // 2
    position = places.astype(jnp.float32)[:, None]
    frequency = rope_base ** (-(2.0 * jnp.arange(halfway).astype(jnp.float32)) / head_depth)
    angles = position * frequency[None, :]
    cosine = jnp.concatenate([jnp.cos(angles), jnp.cos(angles)], axis=1)
    sine_table = jnp.concatenate([jnp.sin(angles), jnp.sin(angles)], axis=1)
    return (cosine, sine_table)


def dot(left, right):
    return jnp.dot(left, right, preferred_element_type=wide)


def dot_nt(left, right):
    return jnp.einsum("mk,nk->mn", left, right, preferred_element_type=wide)


def dot_tn(left, right):
    return jnp.einsum("km,kn->mn", left, right, preferred_element_type=wide)


def layer_norm(stream):
    average = jnp.mean(stream, axis=1, keepdims=True)
    centered = stream - average
    inverse = lax.rsqrt(jnp.mean(centered * centered, axis=1, keepdims=True) + epsilon)
    return centered * inverse, inverse


def norm_backward(normed, inverse, gradient):
    average = jnp.mean(gradient, axis=1, keepdims=True)
    crossed = jnp.mean(gradient * normed, axis=1, keepdims=True)
    return inverse * (gradient - average - normed * crossed)


def turn(array):
    return pltpu.roll(array, array.shape[1] // 2, 1)


def rope_sign(depth):
    return jnp.where(lax.broadcasted_iota(jnp.int32, (1, depth), 1) < depth // 2, -1.0, 1.0)


def attend_kernel(rows_ref, weight_ref, cosine_ref, sine_ref, column_ref, line_ref, qkv_ref, heads_ref, logsum_ref):
    depth = heads_ref.shape[1]
    qkv = dot(rows_ref[...], weight_ref[:, : 3 * depth])
    cosine, sine = cosine_ref[...], sine_ref[...] * rope_sign(depth)
    rope = lambda w: (w * cosine + turn(w) * sine).astype(low)
    queries, key_rows = rope(qkv[:, :depth]), rope(qkv[:, depth : 2 * depth])
    values = qkv[:, 2 * depth :].astype(low)
    qkv_ref[...] = jnp.concatenate([queries, key_rows, values], axis=1)
    for at in range(0, queries.shape[0], BLOCK):
        part = slice(at, at + BLOCK)
        scores = dot_last(queries[part], key_rows) * depth**-0.5
        scores = jnp.where(column_ref[part] >= line_ref[...], scores, masked_score)
        highest = jnp.max(scores, axis=1, keepdims=True)
        shifted = jnp.exp(scores - highest)
        totals = jnp.sum(shifted, axis=1, keepdims=True)
        logsum_ref[part] = highest + jnp.log(totals)
        weights = (shifted * (1.0 / totals)).astype(low)
        heads_ref[part] = dot(weights, values).astype(low)


def attend_back_kernel(
    middle_ref, weight_ref, cosine_ref, sine_ref, column_ref, line_ref, qkv_ref, logsum_ref, slope_ref
):
    depth = cosine_ref.shape[1]
    scaling = depth**-0.5
    queries, key_rows, values = (qkv_ref[:, i * depth : (i + 1) * depth] for i in range(3))
    head_grad = dot(middle_ref[...], weight_ref[:, 3 * depth :]).astype(low)
    query_parts = []
    key_grad = value_grad = None
    for at in range(0, queries.shape[0], BLOCK):
        part = slice(at, at + BLOCK)
        scores = dot_last(queries[part], key_rows) * scaling
        scores = jnp.where(column_ref[part] >= line_ref[...], scores, masked_score)
        probable = jnp.exp(scores - logsum_ref[part])
        product = dot_last(head_grad[part], values)
        slopes = probable * (product - jnp.sum(probable * product, axis=1, keepdims=True))
        slopes = slopes.astype(low)
        query_parts.append(dot(slopes, key_rows) * scaling)
        key_part = dot_first(slopes, queries[part]) * scaling
        value_part = dot_first(probable.astype(low), head_grad[part])
        key_grad = key_part if at == 0 else key_grad + key_part
        value_grad = value_part if at == 0 else value_grad + value_part
    cosine, sine = cosine_ref[...], sine_ref[...]
    undo = lambda g: (g * cosine - turn(g * sine) * rope_sign(depth)).astype(low)
    slope_ref[:, :depth] = undo(jnp.concatenate(query_parts, axis=0))
    slope_ref[:, depth : 2 * depth] = undo(key_grad)
    slope_ref[:, 2 * depth :] = value_grad.astype(low)


def project_kernel(columns, *refs):
    lefts, weights, out_ref = refs[: len(refs) // 2], refs[len(refs) // 2 : -1], refs[-1]
    out_ref[...] = sum(
        dot_last(left[...], weight[:, columns]) for left, weight in zip(lefts, weights)
    ).astype(low)


def assemble_kernel(x_ref, mine_ref, theirs_ref, query_ref, key_ref, value_ref, out_ref):
    line, block, depth = mine_ref.shape[0], mine_ref.shape[1], HEAD_DIM
    for i in range(line):
        for source, turned in ((mine_ref, x_ref[0]), (theirs_ref, 1 - x_ref[0])):
            place = pl.ds(pl.multiple_of((HALF * i + turned) * depth, depth), depth)
            for n, target in enumerate((query_ref, key_ref, value_ref)):
                target[:, place] = source[i, :, n * depth : (n + 1) * depth].astype(wide)
            out_ref[place, :] = source[i, :, 3 * depth :].astype(wide).T


def assemble(mine, theirs):
    line, block, _ = mine.shape
    shape = jax.ShapeDtypeStruct((block, block), wide)
    whole = pl.BlockSpec(memory_space=pltpu.VMEM)
    return pl.pallas_call(
        assemble_kernel,
        in_specs=[pl.BlockSpec(memory_space=pltpu.SMEM), whole, whole],
        out_specs=[whole] * 4,
        out_shape=[shape] * 4,
        name="assemble",
    )(lax.axis_index("x")[None].astype(jnp.int32), mine, theirs)


def call_whole(kernel, name, shapes, *arrays):
    whole = pl.BlockSpec(memory_space=pltpu.VMEM)
    return pl.pallas_call(
        kernel,
        in_specs=[whole] * len(arrays),
        out_specs=[whole] * len(shapes),
        out_shape=shapes,
        compiler_params=pltpu.CompilerParams(vmem_limit_bytes=48 * 1024 * 1024),
        cost_estimate=pl.CostEstimate(flops=1, transcendentals=0, bytes_accessed=1),
        name=name,
    )(*arrays)


def dot_last(left, right):
    return lax.dot_general(left, right, (((1,), (1,)), ((), ())), preferred_element_type=wide)


def dot_first(left, right):
    return lax.dot_general(left, right, (((0,), (0,)), ((), ())), preferred_element_type=wide)


def swap(array, axis):
    return lax.ppermute(array, axis, [(0, 1), (1, 0)])


class Ring:
    def __init__(self, axes, line):
        self.axes = axes
        self.size = 2 * line
        self.half = line
        flat = [2 * n if n < line else 2 * (2 * line - 1 - n) + 1 for n in range(self.size)]
        self.upward = [(flat[i], flat[(i + 1) % self.size]) for i in range(self.size)]
        self.downward = [(b, a) for a, b in self.upward]

    def up(self, array):
        return lax.ppermute(array, self.axes, self.upward)

    def down(self, array):
        return lax.ppermute(array, self.axes, self.downward)

    def place(self):
        level, side = lax.axis_index(self.axes[:-1]), lax.axis_index(self.axes[-1])
        return jnp.where(side == 0, level, self.size - 1 - level)

    def gather(self, shard, waits={}):
        half, cut = self.half, shard.shape[0] // 2
        slots = [None] * self.size
        slots[half] = rising = falling = shard
        for step in range(1, half + 1):
            rising, falling = after((rising, falling), waits.get(step))
            if step == half:
                break
            slots[half - step] = rising = self.up(rising)
            slots[half + step] = falling = self.down(falling)
        slots[0] = jnp.concatenate([self.up(rising[:cut]), self.down(falling[cut:])], axis=0)
        return slots

    def scatter(self, parts, waits={}):
        half, cut = self.half, parts[0].shape[0] // 2
        rising, falling = self.up(parts[0][:cut]), self.down(parts[0][cut:])
        for step in range(1, half):
            over, under = parts[self.size - step], parts[step]
            if step == 1:
                over = jnp.concatenate([add_low(over[:cut], rising), over[cut:]], axis=0)
                under = jnp.concatenate([under[:cut], add_low(under[cut:], falling)], axis=0)
            else:
                over, under = add_low(over, rising), add_low(under, falling)
            over, under = after((over, under), waits.get(step))
            rising, falling = self.up(over), self.down(under)
        return parts[half].astype(wide) + rising.astype(wide) + falling.astype(wide)


def add_low(left, right):
    return (left.astype(wide) + right.astype(wide)).astype(low)


def split_rows(array, count):
    rows = array.shape[0] // count
    return [array[i * rows : (i + 1) * rows] for i in range(count)]


def gather_group(ring, shard, waits={}):
    slots = ring.gather(shard, waits)
    return jnp.concatenate(slots + [swap(slot, "core") for slot in slots], axis=0)


def scatter_group(ring, partial, waits={}):
    own, other = split_rows(partial, HALF)
    return ring.scatter(split_rows(add_low(own, swap(other, "core")), ring.size), waits)


def exchange_rows(array):
    return lax.all_to_all(array, ROW, 0, 0, tiled=True)


ROW = ("zhi", "zlo")


def to_shards(*arrays):
    rows = lax.axis_size(ROW)
    seqs, tokens, width = arrays[0].shape
    pieces = [array.reshape(rows, seqs * tokens // rows, width) for array in arrays]
    got = jnp.transpose(exchange_rows(jnp.concatenate(pieces, axis=1)), (1, 0, 2))
    return split_rows(got.reshape(-1, rows * width), len(arrays))


def from_shards(arrays, seqs):
    rows, count = lax.axis_size(ROW), len(arrays)
    tokens, width = arrays[0].shape[0], arrays[0].shape[1] // rows
    stacked = jnp.concatenate(arrays, axis=0).reshape(count * tokens, rows, width)
    got = exchange_rows(jnp.transpose(stacked, (1, 0, 2)))
    return [
        got[:, i * tokens : (i + 1) * tokens].reshape(seqs, rows * tokens // seqs, width)
        for i in range(count)
    ]


def after(arrays, others):
    if others is None:
        return arrays
    return lax.optimization_barrier((arrays, others))[0]


def choose(first, second):
    return jnp.where(lax.axis_index("x") == 0, first, second)


def spread(pieces):
    mine = exchange_rows(pieces)
    return [mine, swap(mine, "x")]


def sum_pair(mine, theirs):
    total = add_low(mine, swap(theirs, "x"))
    if lax.axis_size("pair") > 1:
        total = lax.psum(total, "pair")
    return total


def in_order(mine):
    theirs = swap(mine, "x")
    return choose(mine, theirs), choose(theirs, mine)


def by_block(array, count):
    return jnp.transpose(array.reshape(array.shape[0], count, -1), (1, 0, 2))


def from_block(array):
    return jnp.transpose(array, (1, 0, 2)).reshape(array.shape[1], -1)


def pack_kernel(x_ref, query, key, value, out, gate, up, down, head, gu, down_out):
    head[0] = jnp.concatenate([query[...], key[...], value[...], out[...].T], axis=1)
    gu[0] = jnp.concatenate([gate[...], up[...]], axis=1)
    down_out[0] = down[...]


def pack(query, key, value, out, gate, up, down, rows, line):
    depth, block = HEAD_DIM, query.shape[0]
    units = gate.shape[1] // rows // HALF
    head_at = lambda r, x: HALF * (r % line) + x[0]
    head_in = pl.BlockSpec((block, depth), lambda r, x: (0, head_at(r, x)))
    out_in = pl.BlockSpec((depth, block), lambda r, x: (head_at(r, x), 0))
    unit_in = pl.BlockSpec((block, units), lambda r, x: (0, HALF * r + x[0]))
    down_in = pl.BlockSpec((units, block), lambda r, x: (HALF * r + x[0], 0))
    shapes = [(block, 4 * depth), (block, 2 * units), (units, block)]
    return pl.pallas_call(
        pack_kernel,
        grid_spec=pltpu.PrefetchScalarGridSpec(
            num_scalar_prefetch=1,
            grid=(rows,),
            in_specs=[head_in, head_in, head_in, out_in, unit_in, unit_in, down_in],
            out_specs=[pl.BlockSpec((1,) + shape, lambda r, x: (r, 0, 0)) for shape in shapes],
        ),
        out_shape=[jax.ShapeDtypeStruct((rows,) + shape, low) for shape in shapes],
        name="pack_weights",
    )(lax.axis_index("x")[None].astype(jnp.int32), query, key, value, out, gate, up, down)


def mlp_kernel(blocks, rows_ref, slope_ref, *refs):
    weights, downs = refs[:blocks], refs[blocks : 2 * blocks]
    hidden_ref, gu_slope_ref, grad_ref = refs[2 * blocks :]
    parts, units, span = downs[0].shape
    rows = rows_ref[...]
    total = None
    for i in range(blocks):
        weight = weights[i][...]
        gate_up = dot(rows, weight)
        gate, up = gate_up[:, :units], gate_up[:, units:]
        sigmoid = 1.0 / (1.0 + jnp.exp(-gate))
        activated = gate * sigmoid
        hidden_ref[:, i * units : (i + 1) * units] = (activated * up).astype(low)
        hidden_grad = sum(
            dot_last(slope_ref[:, k * span : (k + 1) * span], downs[i][k]) for k in range(parts)
        )
        gate_slope = hidden_grad * up * sigmoid * (1.0 + gate * (1.0 - sigmoid))
        gu_slope = jnp.concatenate([gate_slope, hidden_grad * activated], axis=1).astype(low)
        gu_slope_ref[:, 2 * i * units : 2 * (i + 1) * units] = gu_slope
        part = dot_last(gu_slope, weight)
        total = part if total is None else total + part
    grad_ref[...] = total.astype(low)


def down_kernel(place_ref, hidden_ref, *refs):
    downs, out_ref = refs[:-1], refs[-1]
    parts, units, span = downs[0].shape
    for k in range(parts):
        out_ref[0, 0, :, k * span : (k + 1) * span] = sum(
            dot(hidden_ref[:, i * units : (i + 1) * units], down[k]) for i, down in enumerate(downs)
        ).astype(low)


def down_project(ring, hidden, downs, width):
    tile = hidden.shape[0] // ring.size

    def target(i, place):
        spot = (place[0] + i + ring.half) % ring.size
        side = spot // ring.half
        row = jnp.where(side == 0, spot, ring.size - 1 - spot)
        return (jnp.where(side == place[0] // ring.half, 0, 1), row, 0, 0)

    whole = lambda array: pl.BlockSpec(
        array.shape, lambda i, place: (0, 0, 0), pipeline_mode=pl.Buffered(buffer_count=1)
    )
    return pl.pallas_call(
        down_kernel,
        grid_spec=pltpu.PrefetchScalarGridSpec(
            num_scalar_prefetch=1,
            grid=(ring.size,),
            in_specs=[pl.BlockSpec((tile, hidden.shape[1]), lambda i, place: (i, 0))]
            + [whole(down) for down in downs],
            out_specs=pl.BlockSpec((1, 1, tile, width), target),
        ),
        out_shape=jax.ShapeDtypeStruct((HALF, ring.half, tile, width), low),
        compiler_params=pltpu.CompilerParams(vmem_limit_bytes=48 * 1024 * 1024),
        name="down_project",
    )(ring.place()[None].astype(jnp.int32), hidden, *downs)


def call_rows(kernel, name, arrays, held, sizes, tile=256):
    count = arrays[0].shape[0]
    row_block = lambda columns: pl.BlockSpec((tile, columns), lambda i: (i, 0))
    whole = lambda array: pl.BlockSpec(
        array.shape, lambda i: (0,) * array.ndim, pipeline_mode=pl.Buffered(buffer_count=1)
    )
    return pl.pallas_call(
        kernel,
        grid=(count // tile,),
        in_specs=[row_block(array.shape[1]) for array in arrays] + [whole(array) for array in held],
        out_specs=[row_block(size) for size in sizes],
        out_shape=[jax.ShapeDtypeStruct((count, size), low) for size in sizes],
        compiler_params=pltpu.CompilerParams(vmem_limit_bytes=48 * 1024 * 1024),
        name=name,
    )(*arrays, *held)


def on_device(
    tokens,
    query_weight,
    key_weight,
    value_weight,
    out_weight,
    gate_weight,
    up_weight,
    down_weight,
    cotangent,
):
    depth = HEAD_DIM
    rows, line = lax.axis_size(ROW), lax.axis_size("zlo")
    small_ring = Ring(("zlo", "y"), line)
    large_ring = Ring(("zhi", "zlo", "y"), rows)
    seqs, width = tokens.shape[0], tokens.shape[2] * rows
    block = width // rows
    units = gate_weight.shape[1] // rows // HALF
    flat = lambda got: got.reshape(width, got.shape[2])

    heads_weight, gu_pieces, down_pieces = pack(
        query_weight, key_weight, value_weight, out_weight, gate_weight, up_weight, down_weight, rows, line
    )
    stream_low, slope_low = to_shards(tokens, cotangent)
    stream = stream_low.astype(wide)
    shard = stream.shape[0]
    heads_weight = [flat(got) for got in spread(after(heads_weight, stream_low))]

    place = jnp.arange(2 * small_ring.size)
    core = (lax.axis_index("core") + place // small_ring.size) % 2
    spot = (small_ring.place() + place % small_ring.size + small_ring.half) % small_ring.size
    slot_side = spot // line
    slot_level = jnp.where(slot_side == 0, spot, small_ring.size - 1 - spot)
    first = ((2 * slot_side + core) * line + slot_level) * shard
    places = (first[:, None] + jnp.arange(shard)[None, :]).reshape(-1)
    cosine, sine_table = rope_tables(places, depth)

    normed_one, inverse_one = layer_norm(stream)
    rows_one = gather_group(small_ring, normed_one.astype(low))
    slope_slots = large_ring.gather(after(slope_low, (heads_weight[0], rows_one)), {4: heads_weight[1]})
    slope_all = jnp.concatenate(slope_slots, axis=0)

    gu_weight = [flat(got) for got in spread(after(gu_pieces, heads_weight[0]))]
    down = spread(after(down_pieces, gu_weight[0]))

    rows_one = after(rows_one, slope_slots[2:7])
    length = rows_one.shape[0]
    seen = (cosine, sine_table, places[:, None], places[None, :])
    qkv_shape = jax.ShapeDtypeStruct((length, 3 * depth), low)
    kept = []
    for weight in heads_weight:
        shapes = [qkv_shape, jax.ShapeDtypeStruct((length, depth), low), jax.ShapeDtypeStruct((length, 1), wide)]
        kept.append(call_whole(attend_kernel, "attend", shapes, rows_one, weight, *seen))
    heads = after([part[1] for part in kept], (slope_slots[1], slope_slots[7]))
    project = functools.partial(project_kernel, slice(3 * depth, 4 * depth))
    (out_part,) = call_rows(project, "out_project", heads, heads_weight, (width,))
    middle = stream + scatter_group(small_ring, out_part)
    normed_two, inverse_two = layer_norm(after(middle, (slope_slots[0], gu_weight[0])))
    waits = {2: down[0], 3: gu_weight[1]}
    rows_two = jnp.concatenate(large_ring.gather(normed_two.astype(low), waits), axis=0)
    gu_weight += [swap(part, "core") for part in gu_weight]
    down += [swap(part, "core") for part in down]

    sizes = (4 * units, 8 * units, width)
    hidden_low, gu_slope, grad_part = call_rows(
        functools.partial(mlp_kernel, len(down)), "feed_forward", [rows_two, slope_all], gu_weight + down, sizes
    )
    gu_own = dot_tn(rows_two, gu_slope[:, : 4 * units])
    gu_other = dot_tn(rows_two, gu_slope[:, 4 * units :]).astype(low)
    gu_total = add_low(gu_own, swap(gu_other, "core"))
    gu_sum = sum_pair(gu_total[:, : 2 * units], gu_total[:, 2 * units :])

    grad_two = large_ring.scatter(split_rows(grad_part, large_ring.size), {2: gu_total})
    middle_grad = slope_low.astype(wide) + norm_backward(normed_two, inverse_two, grad_two)
    middle_all = gather_group(small_ring, middle_grad.astype(low), {2: gu_sum})

    late_hidden, late_slope = after((hidden_low, slope_all), grad_two)
    down_own = dot_tn(late_hidden[:, : 2 * units], late_slope)
    down_other = dot_tn(late_hidden[:, 2 * units :], late_slope).astype(low)
    down_total = add_low(down_own, swap(down_other, "core"))
    down_sum = sum_pair(down_total[:units], down_total[units:])
    branch_part = down_project(large_ring, late_hidden, down, width)
    branch_half = add_low(branch_part[0], swap(branch_part[1], "y"))
    gu_got = exchange_rows(gu_sum.reshape(rows, block, 2 * units))
    down_got = exchange_rows(by_block(after(down_sum, gu_got), rows))
    branch_got = exchange_rows(after(branch_half, down_got))

    head_slopes, head_sums = [None] * HALF, [None] * HALF
    for head in reversed(range(HALF)):
        qkv, attended, logsums = kept[head]
        (slope,) = call_whole(
            attend_back_kernel, "attend_back", [qkv_shape], middle_all, heads_weight[head], *seen, qkv, logsums
        )
        sums = [dot_tn(rows_one, slope), dot_tn(middle_all, attended)]
        head_slopes[head] = slope
        head_sums[head] = jnp.concatenate(sums, axis=1).astype(low)
    project = functools.partial(project_kernel, slice(0, 3 * depth))
    (grad_part,) = call_rows(project, "qkv_back", head_slopes, heads_weight, (width,))
    grad_one = scatter_group(small_ring, grad_part, {1: branch_half})
    input_low = (middle_grad + norm_backward(normed_one, inverse_one, grad_one)).astype(low)
    head_total = sum_pair(*head_sums).reshape(rows, block, 4 * depth)
    head_got = exchange_rows(after(head_total, branch_got)).reshape(rows // line, line, block, 4 * depth)
    head_mine = jnp.sum(head_got.astype(wide), axis=0).astype(low)
    query_grad, key_grad, value_grad, out_grad = assemble(head_mine, swap(head_mine, "x"))
    branch = jnp.sum(branch_got.astype(wide), axis=0)
    output_low = (middle + branch).astype(low)
    layer_out, input_grad = from_shards(after((output_low, input_low), head_got), seqs)
    input_grad = input_grad.astype(wide)

    def unit_columns(first, second):
        parts = [part[i] for i in range(rows) for part in (first, second)]
        return jnp.concatenate(parts, axis=1).astype(wide)

    gu_grads = in_order(gu_got)
    gate_grad = unit_columns(*(part[:, :, :units] for part in gu_grads))
    up_grad = unit_columns(*(part[:, :, units:] for part in gu_grads))
    down_grad = jnp.stack(in_order(down_got), axis=1).reshape(-1, block).astype(wide)

    return (
        layer_out,
        input_grad,
        query_grad,
        key_grad,
        value_grad,
        out_grad,
        gate_grad,
        up_grad,
        down_grad,
    )


def solution(mesh):
    dp, rows, cols = (mesh.shape[name] for name in ("dp", "row", "col"))
    sizes = (dp // HALF, HALF, HALF, rows // HALF, cols // HALF, HALF)
    fine = Mesh(mesh.devices.reshape(sizes), ("pair", "x", "zhi", "zlo", "y", "core"))
    across, inner, tall = ("pair", "x"), ("y", "core"), ROW
    split = P(across, inner, tall)
    inward = P(tall, inner)
    outward = P(inner, tall)
    return jax.shard_map(
        on_device,
        mesh=fine,
        in_specs=(split, inward, inward, inward, outward, inward, inward, outward, split),
        out_specs=(split, split, inward, inward, inward, outward, inward, inward, outward),
        check_vma=False,
    )
```

```python
import functools

import jax
import jax.numpy as jnp
from jax import lax
from jax.experimental import pallas as pl
from jax.experimental.pallas import tpu as pltpu
from jax.sharding import Mesh
from jax.sharding import PartitionSpec as P

HEAD_DIM = 128
BLOCK = 512
HALF = 2

epsilon = 1e-05
rope_base = 10000.0
masked_score = -1e30
low = jnp.bfloat16
CHEAP = pl.CostEstimate(flops=1, transcendentals=0, bytes_accessed=1)
wide = jnp.float32


def rope_tables(places, head_depth):
    halfway = head_depth // 2
    position = places.astype(jnp.float32)[:, None]
    frequency = rope_base ** (-(2.0 * jnp.arange(halfway).astype(jnp.float32)) / head_depth)
    angles = position * frequency[None, :]
    cosine = jnp.concatenate([jnp.cos(angles), jnp.cos(angles)], axis=1)
    sine_table = jnp.concatenate([jnp.sin(angles), jnp.sin(angles)], axis=1)
    return (cosine, sine_table)


def dot(left, right):
    return jnp.dot(left, right, preferred_element_type=wide)


def layer_norm(stream):
    average = jnp.mean(stream, axis=1, keepdims=True)
    centered = stream - average
    inverse = lax.rsqrt(jnp.mean(centered * centered, axis=1, keepdims=True) + epsilon)
    return centered * inverse, inverse


def norm_backward(normed, inverse, gradient):
    average = jnp.mean(gradient, axis=1, keepdims=True)
    crossed = jnp.mean(gradient * normed, axis=1, keepdims=True)
    return inverse * (gradient - average - normed * crossed)


def turn(array):
    return pltpu.roll(array, array.shape[1] // 2, 1)


def rope_sign(depth):
    return jnp.where(lax.broadcasted_iota(jnp.int32, (1, depth), 1) < depth // 2, -1.0, 1.0)


def attend_kernel(rows_ref, weight_ref, cosine_ref, sine_ref, column_ref, line_ref, qkv_ref, heads_ref, logsum_ref):
    depth = heads_ref.shape[1]
    qkv = dot(rows_ref[...], weight_ref[:, : 3 * depth])
    cosine, sine = cosine_ref[...], sine_ref[...] * rope_sign(depth)
    rope = lambda w: (w * cosine + turn(w) * sine).astype(low)
    queries, key_rows = rope(qkv[:, :depth]), rope(qkv[:, depth : 2 * depth])
    values = qkv[:, 2 * depth :].astype(low)
    qkv_ref[...] = jnp.concatenate([queries, key_rows, values], axis=1)
    for at in range(0, queries.shape[0], BLOCK):
        part = slice(at, at + BLOCK)
        scores = dot_last(queries[part], key_rows) * depth**-0.5
        scores = jnp.where(column_ref[part] >= line_ref[...], scores, masked_score)
        highest = jnp.max(scores, axis=1, keepdims=True)
        shifted = jnp.exp(scores - highest)
        totals = jnp.sum(shifted, axis=1, keepdims=True)
        logsum_ref[part] = highest + jnp.log(totals)
        weights = (shifted * (1.0 / totals)).astype(low)
        heads_ref[part] = dot(weights, values).astype(low)


def attend_back_kernel(
    middle_ref, weight_ref, cosine_ref, sine_ref, column_ref, line_ref, qkv_ref, logsum_ref, slope_ref
):
    depth = cosine_ref.shape[1]
    scaling = depth**-0.5
    queries, key_rows, values = (qkv_ref[:, i * depth : (i + 1) * depth] for i in range(3))
    head_grad = dot(middle_ref[...], weight_ref[:, 3 * depth :]).astype(low)
    query_parts = []
    key_grad = value_grad = None
    for at in range(0, queries.shape[0], BLOCK):
        part = slice(at, at + BLOCK)
        scores = dot_last(queries[part], key_rows) * scaling
        scores = jnp.where(column_ref[part] >= line_ref[...], scores, masked_score)
        probable = jnp.exp(scores - logsum_ref[part])
        product = dot_last(head_grad[part], values)
        slopes = probable * (product - jnp.sum(probable * product, axis=1, keepdims=True))
        slopes = slopes.astype(low)
        query_parts.append(dot(slopes, key_rows) * scaling)
        key_part = dot_first(slopes, queries[part]) * scaling
        value_part = dot_first(probable.astype(low), head_grad[part])
        key_grad = key_part if at == 0 else key_grad + key_part
        value_grad = value_part if at == 0 else value_grad + value_part
    cosine, sine = cosine_ref[...], sine_ref[...]
    undo = lambda g: (g * cosine - turn(g * sine) * rope_sign(depth)).astype(low)
    slope_ref[:, :depth] = undo(jnp.concatenate(query_parts, axis=0))
    slope_ref[:, depth : 2 * depth] = undo(key_grad)
    slope_ref[:, 2 * depth :] = value_grad.astype(low)


def project_kernel(columns, *refs):
    lefts, weights = refs[: len(refs) // 2 - 1], refs[len(refs) // 2 - 1 : -2]
    part = sum(dot_last(left[...], weight[:, columns]) for left, weight in zip(lefts, weights)).astype(low)
    first = 2 * pl.program_id(0) < pl.num_programs(0)

    @pl.when(first)
    def _():
        refs[-2][...] = part

    @pl.when(jnp.logical_not(first))
    def _():
        refs[-1][...] = part


def project(name, columns, lefts, weights, tile=256):
    count, width = lefts[0].shape[0], weights[0].shape[0]
    last = count // tile // HALF - 1
    whole = lambda array: pl.BlockSpec(array.shape, lambda i: (0, 0), pipeline_mode=pl.Buffered(buffer_count=1))
    return pl.pallas_call(
        functools.partial(project_kernel, columns),
        grid=(count // tile,),
        in_specs=[pl.BlockSpec((tile, left.shape[1]), lambda i: (i, 0)) for left in lefts]
        + [whole(weight) for weight in weights],
        out_specs=[
            pl.BlockSpec((tile, width), lambda i: (jnp.minimum(i, last), 0)),
            pl.BlockSpec((tile, width), lambda i: (jnp.maximum(i - last - 1, 0), 0)),
        ],
        out_shape=[jax.ShapeDtypeStruct((count // HALF, width), low)] * HALF,
        compiler_params=pltpu.CompilerParams(vmem_limit_bytes=48 * 1024 * 1024),
        cost_estimate=CHEAP,
        name=name,
    )(*lefts, *weights)


def head_sum_kernel(rows_ref, middle_ref, slope_ref, attended_ref, out_ref):
    parts = [dot_first(rows_ref[...], slope_ref[...]), dot_first(middle_ref[...], attended_ref[...])]
    out_ref[0] = jnp.concatenate(parts, axis=1).astype(low)


def gu_sum_kernel(blocks, rows_ref, slope_ref, *out_refs):
    rows = rows_ref[...]
    for block, out_ref in zip(blocks, out_refs):
        size = out_ref.shape[2]
        out_ref[0] = dot_first(rows, slope_ref[:, block * size : (block + 1) * size]).astype(low)


def down_sum_kernel(blocks, slope_ref, hidden_ref, *out_refs):
    slope = slope_ref[...]
    for block, out_ref in zip(blocks, out_refs):
        units = out_ref.shape[1]
        out_ref[0] = dot_first(hidden_ref[:, block * units : (block + 1) * units], slope).astype(low)


def call_blocks(kernel, name, cut, held, shapes):
    count, (length, width) = shapes[0][0], cut[0].shape
    return pl.pallas_call(
        kernel,
        grid=(count,),
        in_specs=[pl.BlockSpec((length, width // count), lambda i: (0, i))] * len(cut)
        + [pl.BlockSpec(array.shape, lambda i: (0, 0)) for array in held],
        out_specs=[pl.BlockSpec((1,) + shape[1:], lambda i: (i, 0, 0)) for shape in shapes],
        out_shape=[jax.ShapeDtypeStruct(shape, low) for shape in shapes],
        compiler_params=pltpu.CompilerParams(vmem_limit_bytes=48 * 1024 * 1024),
        cost_estimate=CHEAP,
        name=name,
    )(*cut, *held)


def assemble_kernel(x_ref, mine_ref, theirs_ref, query_ref, key_ref, value_ref, out_ref):
    line, block, depth = mine_ref.shape[0], mine_ref.shape[1], HEAD_DIM
    for i in range(line):
        for source, turned in ((mine_ref, x_ref[0]), (theirs_ref, 1 - x_ref[0])):
            place = pl.ds(pl.multiple_of((HALF * i + turned) * depth, depth), depth)
            for n, target in enumerate((query_ref, key_ref, value_ref)):
                target[:, place] = source[i, :, n * depth : (n + 1) * depth].astype(wide)
            out_ref[place, :] = source[i, :, 3 * depth :].astype(wide).T


def assemble(mine, theirs):
    line, block, _ = mine.shape
    shape = jax.ShapeDtypeStruct((block, block), wide)
    whole = pl.BlockSpec(memory_space=pltpu.VMEM)
    return pl.pallas_call(
        assemble_kernel,
        in_specs=[pl.BlockSpec(memory_space=pltpu.SMEM), whole, whole],
        out_specs=[whole] * 4,
        out_shape=[shape] * 4,
        cost_estimate=CHEAP,
        name="assemble",
    )(lax.axis_index("x")[None].astype(jnp.int32), mine, theirs)


def assemble_units_kernel(x_ref, gu_mine, down_mine, gu_theirs, down_theirs, gate_ref, up_ref, down_ref):
    units = down_mine.shape[1]
    mine, theirs = gu_mine[0].astype(wide), gu_theirs[0].astype(wide)
    first = jnp.where(x_ref[0] == 0, mine, theirs)
    second = jnp.where(x_ref[0] == 0, theirs, mine)
    gate_ref[...] = jnp.concatenate([first[:, :units], second[:, :units]], axis=1)
    up_ref[...] = jnp.concatenate([first[:, units:], second[:, units:]], axis=1)
    mine, theirs = down_mine[0].astype(wide), down_theirs[0].astype(wide)
    down_ref[:units] = jnp.where(x_ref[0] == 0, mine, theirs)
    down_ref[units:] = jnp.where(x_ref[0] == 0, theirs, mine)


def assemble_units(*arrays):
    rows, units, size = arrays[1].shape
    share = HALF * units
    arrived = [pl.BlockSpec((1,) + array.shape[1:], lambda i, x: (i, 0, 0)) for array in arrays]
    columns = pl.BlockSpec((size, share), lambda i, x: (0, i))
    wide_shape = jax.ShapeDtypeStruct((size, rows * share), wide)
    return pl.pallas_call(
        assemble_units_kernel,
        grid_spec=pltpu.PrefetchScalarGridSpec(
            num_scalar_prefetch=1,
            grid=(rows,),
            in_specs=arrived,
            out_specs=[columns, columns, pl.BlockSpec((share, size), lambda i, x: (i, 0))],
        ),
        out_shape=[wide_shape, wide_shape, jax.ShapeDtypeStruct((rows * share, size), wide)],
        compiler_params=pltpu.CompilerParams(vmem_limit_bytes=48 * 1024 * 1024),
        cost_estimate=CHEAP,
        name="assemble_units",
    )(lax.axis_index("x")[None].astype(jnp.int32), *arrays)


def call_whole(kernel, name, shapes, *arrays):
    whole = pl.BlockSpec(memory_space=pltpu.VMEM)
    return pl.pallas_call(
        kernel,
        in_specs=[whole] * len(arrays),
        out_specs=[whole] * len(shapes),
        out_shape=shapes,
        compiler_params=pltpu.CompilerParams(vmem_limit_bytes=48 * 1024 * 1024),
        cost_estimate=CHEAP,
        name=name,
    )(*arrays)


def dot_last(left, right):
    return lax.dot_general(left, right, (((1,), (1,)), ((), ())), preferred_element_type=wide)


def dot_first(left, right):
    return lax.dot_general(left, right, (((0,), (0,)), ((), ())), preferred_element_type=wide)


def swap(array, axis):
    return lax.ppermute(array, axis, [(0, 1), (1, 0)])


class Ring:
    def __init__(self, axes, line):
        self.axes = axes
        self.size = 2 * line
        self.half = line
        flat = [2 * n if n < line else 2 * (2 * line - 1 - n) + 1 for n in range(self.size)]
        self.upward = [(flat[i], flat[(i + 1) % self.size]) for i in range(self.size)]
        self.downward = [(b, a) for a, b in self.upward]

    def up(self, array):
        return lax.ppermute(array, self.axes, self.upward)

    def down(self, array):
        return lax.ppermute(array, self.axes, self.downward)

    def place(self):
        level, side = lax.axis_index(self.axes[:-1]), lax.axis_index(self.axes[-1])
        return jnp.where(side == 0, level, self.size - 1 - level)

    def slot(self, place, other, level):
        side = place // self.half
        spot = jnp.where((side == 0) != other, level, self.size - 1 - level)
        return (spot - place + self.half + self.size) % self.size

    def gather(self, shard, waits={}):
        half, cut = self.half, shard.shape[0] // 2
        slots = [None] * self.size
        slots[half] = rising = falling = shard
        for step in range(1, half + 1):
            rising, falling = after((rising, falling), waits.get(step))
            if step == half:
                break
            slots[half - step] = rising = self.up(rising)
            slots[half + step] = falling = self.down(falling)
        slots[0] = jnp.concatenate([self.up(rising[:cut]), self.down(falling[cut:])], axis=0)
        return slots

    def scatter_start(self, parts):
        cut = parts[0].shape[0] // 2
        return self.up(parts[0][:cut]), self.down(parts[0][cut:])

    def scatter_step(self, parts, step, moving):
        rising, falling = moving
        cut = rising.shape[0]
        over, under = parts[self.size - step], parts[step]
        if step == 1:
            over = jnp.concatenate([add_low(over[:cut], rising), over[cut:]], axis=0)
            under = jnp.concatenate([under[:cut], add_low(under[cut:], falling)], axis=0)
        else:
            over, under = add_low(over, rising), add_low(under, falling)
        return self.up(over), self.down(under)

    def scatter_end(self, parts, moving):
        return sum(part.astype(wide) for part in (parts[self.half],) + moving)

    def scatter(self, parts):
        moving = self.scatter_start(parts)
        for step in range(1, self.half):
            moving = self.scatter_step(parts, step, moving)
        return self.scatter_end(parts, moving)


def add_low(left, right):
    return (left.astype(wide) + right.astype(wide)).astype(low)


def split_rows(array, count):
    rows = array.shape[0] // count
    return [array[i * rows : (i + 1) * rows] for i in range(count)]


def gather_group(ring, slots):
    return jnp.concatenate(slots + [swap(slot, "core") for slot in slots], axis=0)


def scatter_group(ring, own, other, awaited=None):
    total = after(add_low(own, swap(other, "core")), awaited)
    return ring.scatter(split_rows(total, ring.size))


def exchange_rows(array):
    return lax.all_to_all(array, ROW, 0, 0, tiled=True)


ROW = ("zhi", "zlo")


def to_shard(blocks):
    return jnp.transpose(blocks, (1, 0, 2)).reshape(blocks.shape[1], -1)


def from_shards(arrays, seqs):
    rows, count = lax.axis_size(ROW), len(arrays)
    tokens, width = arrays[0].shape[0], arrays[0].shape[1] // rows
    stacked = jnp.concatenate(arrays, axis=0).reshape(count * tokens, rows, width)
    got = exchange_rows(jnp.transpose(stacked, (1, 0, 2)))
    return [
        got[:, i * tokens : (i + 1) * tokens].reshape(seqs, rows * tokens // seqs, width)
        for i in range(count)
    ]


def together(*arrays):
    return lax.optimization_barrier(arrays)


def after(arrays, others):
    if others is None:
        return arrays
    return lax.optimization_barrier((arrays, others))[0]


def sum_pairs(array):
    return lax.psum(array, "pair") if lax.axis_size("pair") > 1 else array


def pack_kernel(x_ref, query, key, value, out, gate, up, down, head, hidden):
    head[0] = jnp.concatenate([query[...], key[...], value[...], out[...].T], axis=1)
    hidden[0] = jnp.concatenate([jnp.concatenate([gate[...], up[...]], axis=1), down[...]], axis=0)


def pack(query, key, value, out, gate, up, down, rows, line):
    depth, block = HEAD_DIM, query.shape[0]
    units = gate.shape[1] // rows // HALF
    head_at = lambda r, x: HALF * (r % line) + x[0]
    head_in = pl.BlockSpec((block, depth), lambda r, x: (0, head_at(r, x)))
    out_in = pl.BlockSpec((depth, block), lambda r, x: (head_at(r, x), 0))
    unit_in = pl.BlockSpec((block, units), lambda r, x: (0, HALF * r + x[0]))
    down_in = pl.BlockSpec((units, block), lambda r, x: (HALF * r + x[0], 0))
    shapes = [(block, 4 * depth), (block + units, block)]
    return pl.pallas_call(
        pack_kernel,
        grid_spec=pltpu.PrefetchScalarGridSpec(
            num_scalar_prefetch=1,
            grid=(rows,),
            in_specs=[head_in, head_in, head_in, out_in, unit_in, unit_in, down_in],
            out_specs=[pl.BlockSpec((1,) + shape, lambda r, x: (r, 0, 0)) for shape in shapes],
        ),
        out_shape=[jax.ShapeDtypeStruct((rows,) + shape, low) for shape in shapes],
        name="pack_weights",
    )(lax.axis_index("x")[None].astype(jnp.int32), query, key, value, out, gate, up, down)


def mlp_kernel(place_ref, *refs):
    tiles, weights = refs[:4], refs[4:-5]
    hidden_ref, gu_slope_ref, grad_ref, rows_ref, slope_ref = refs[-5:]
    parts, height, span = weights[0].shape
    units = height - span
    rows_ref[...] = jnp.concatenate([tiles[0][...], tiles[2][...]], axis=0)
    slope_ref[...] = jnp.concatenate([tiles[1][...], tiles[3][...]], axis=0)
    cuts = [slice(k * span, (k + 1) * span) for k in range(parts)]
    totals = [None] * parts
    for i, weight in enumerate(weights):
        gate_up = sum(dot(rows_ref[:, cut], weight[k, :span]) for k, cut in enumerate(cuts))
        gate, up = gate_up[:, :units], gate_up[:, units:]
        sigmoid = 1.0 / (1.0 + jnp.exp(-gate))
        activated = gate * sigmoid
        hidden_ref[:, i * units : (i + 1) * units] = (activated * up).astype(low)
        hidden_grad = sum(dot_last(slope_ref[:, cut], weight[k, span:]) for k, cut in enumerate(cuts))
        gate_slope = hidden_grad * up * sigmoid * (1.0 + gate * (1.0 - sigmoid))
        gu_slope = jnp.concatenate([gate_slope, hidden_grad * activated], axis=1).astype(low)
        gu_slope_ref[:, 2 * i * units : 2 * (i + 1) * units] = gu_slope
        for k in range(parts):
            part = dot_last(gu_slope, weight[k, :span])
            totals[k] = part if i == 0 else totals[k] + part
    for k, cut in enumerate(cuts):
        grad_ref[:, cut] = totals[k].astype(low)


def feed_forward(ring, both, weights):
    count, width = both.shape[0] // HALF, both.shape[1]
    parts, height, span = weights[0].shape
    blocks, units, tile = len(weights), height - span, count // ring.size
    pair = lambda size: pl.BlockSpec((HALF * tile, size), lambda i, place: (i, 0))
    single = lambda n: pl.BlockSpec((tile, width), lambda i, place: (4 * i + n, 0))
    whole = lambda array: pl.BlockSpec(
        array.shape, lambda i, place: (0, 0, 0), pipeline_mode=pl.Buffered(buffer_count=1)
    )
    sizes = (blocks * units, 2 * blocks * units, width, width, width)
    return pl.pallas_call(
        mlp_kernel,
        grid_spec=pltpu.PrefetchScalarGridSpec(
            num_scalar_prefetch=1,
            grid=(ring.half,),
            in_specs=[single(n) for n in range(4)] + [whole(weight) for weight in weights],
            out_specs=[pair(size) for size in sizes],
        ),
        out_shape=[jax.ShapeDtypeStruct((count, size), low) for size in sizes],
        compiler_params=pltpu.CompilerParams(vmem_limit_bytes=48 * 1024 * 1024),
        cost_estimate=CHEAP,
        name="feed_forward",
    )(ring.place()[None].astype(jnp.int32), *[both] * 4, *weights)


def down_kernel(place_ref, hidden_ref, *refs):
    weights, out_ref = refs[:-1], refs[-1]
    parts, height, span = weights[0].shape
    units = height - span
    for k in range(parts):
        out_ref[:, k * span : (k + 1) * span] = sum(
            dot(hidden_ref[:, i * units : (i + 1) * units], weight[k, span:]) for i, weight in enumerate(weights)
        ).astype(low)


def down_project(ring, hidden, downs, width, other):
    tile = hidden.shape[0] // ring.size
    whole = lambda array: pl.BlockSpec(
        array.shape, lambda i, place: (0, 0, 0), pipeline_mode=pl.Buffered(buffer_count=1)
    )
    return pl.pallas_call(
        down_kernel,
        grid_spec=pltpu.PrefetchScalarGridSpec(
            num_scalar_prefetch=1,
            grid=(ring.half,),
            in_specs=[pl.BlockSpec((tile, hidden.shape[1]), lambda i, place: (ring.slot(place[0], other, i), 0))]
            + [whole(down) for down in downs],
            out_specs=pl.BlockSpec((tile, width), lambda i, place: (i, 0)),
        ),
        out_shape=jax.ShapeDtypeStruct((hidden.shape[0] // HALF, width), low),
        compiler_params=pltpu.CompilerParams(vmem_limit_bytes=48 * 1024 * 1024),
        cost_estimate=CHEAP,
        name="down_project",
    )(ring.place()[None].astype(jnp.int32), hidden, *downs)


def on_device(
    tokens,
    query_weight,
    key_weight,
    value_weight,
    out_weight,
    gate_weight,
    up_weight,
    down_weight,
    cotangent,
):
    depth = HEAD_DIM
    rows, line = lax.axis_size(ROW), lax.axis_size("zlo")
    small_ring = Ring(("zlo", "y"), line)
    large_ring = Ring(("zhi", "zlo", "y"), rows)
    seqs, width = tokens.shape[0], tokens.shape[2] * rows
    block = width // rows
    units = gate_weight.shape[1] // rows // HALF

    shard = seqs * tokens.shape[1] // rows
    pieces = [array.reshape(rows, shard, block) for array in (tokens, cotangent)]
    weights = (query_weight, key_weight, value_weight, out_weight, gate_weight, up_weight, down_weight)
    head_pieces, hidden_pieces = pack(*weights, rows, line)
    got = exchange_rows(jnp.concatenate(pieces, axis=1))
    got, head_pieces, hidden_pieces = together(got, head_pieces, hidden_pieces)
    stream = to_shard(got[:, :shard]).astype(wide)
    slope_low = to_shard(got[:, shard:])

    head_mine = exchange_rows(head_pieces)

    place = jnp.arange(2 * small_ring.size)
    core = (lax.axis_index("core") + place // small_ring.size) % 2
    spot = (small_ring.place() + place % small_ring.size + small_ring.half) % small_ring.size
    slot_side = spot // line
    slot_level = jnp.where(slot_side == 0, spot, small_ring.size - 1 - spot)
    first = ((2 * slot_side + core) * line + slot_level) * shard
    places = (first[:, None] + jnp.arange(shard)[None, :]).reshape(-1)
    cosine, sine_table = rope_tables(places, depth)

    normed_one, inverse_one = layer_norm(stream)
    rows_one = gather_group(small_ring, small_ring.gather(normed_one.astype(low)))
    rows_one, head_mine, hidden_pieces = together(rows_one, head_mine, hidden_pieces)
    heads_weight = [head_mine.reshape(width, 4 * depth)]
    heads_weight.append(swap(heads_weight[0], "x"))

    hidden_mine = exchange_rows(hidden_pieces)
    hidden_theirs = swap(hidden_mine, "x")
    length = rows_one.shape[0]
    seen = (cosine, sine_table, places[:, None], places[None, :])
    qkv_shape = jax.ShapeDtypeStruct((length, 3 * depth), low)
    kept = []
    for weight in heads_weight:
        shapes = [qkv_shape, jax.ShapeDtypeStruct((length, depth), low), jax.ShapeDtypeStruct((length, 1), wide)]
        kept.append(call_whole(attend_kernel, "attend", shapes, rows_one, weight, *seen))
    heads = [part[1] for part in kept]
    out_parts = project("out_project", slice(3 * depth, 4 * depth), heads, heads_weight)
    middle = stream + scatter_group(small_ring, *out_parts, hidden_mine)
    normed_two, inverse_two = layer_norm(middle)
    both = jnp.concatenate([normed_two.astype(low), slope_low], axis=0)
    both = jnp.concatenate(large_ring.gather(both, {4: hidden_theirs}), axis=0)
    hidden_weight = [hidden_mine, hidden_theirs, swap(hidden_mine, "core"), swap(hidden_theirs, "core")]
    hidden_low, gu_slope, grad_part, rows_two, slope_all = feed_forward(large_ring, both, hidden_weight)

    def gu_sums(i, left):
        kernel = functools.partial(gu_sum_kernel, (i, i + 2))
        return call_blocks(kernel, "gu_sum", [left], [gu_slope], [(rows, block, 2 * units)] * 2)

    def down_sums(i, left):
        kernel = functools.partial(down_sum_kernel, (i, i + 2))
        return call_blocks(kernel, "down_sum", [left], [hidden_low], [(rows, units, block)] * 2)

    parts = split_rows(grad_part, large_ring.size)
    moving = large_ring.scatter_start(parts)
    gu_own, gu_other = gu_sums(1, rows_two)
    moving, gu_own, gu_other, rows_two, slope_all, parts = together(
        moving, gu_own, gu_other, rows_two, slope_all, parts
    )
    moving = large_ring.scatter_step(parts, 1, moving)
    gu_other = swap(gu_other, "core")
    gu_mine, gu_mine_other = gu_sums(0, rows_two)
    moving, gu_own, gu_other, gu_mine, gu_mine_other, slope_all = together(
        moving, gu_own, gu_other, gu_mine, gu_mine_other, slope_all
    )

    def chunk(own, other, k, n):
        return swap(add_low(own[k : k + n], other[k : k + n]), "x")

    chunks = [chunk(gu_own, gu_other, 0, 1)]
    moving = large_ring.scatter_step(parts, 2, moving)
    down_own, down_other = down_sums(1, slope_all)
    moving, chunks, gu_own, gu_other, gu_mine_other, down_own, down_other, slope_all = together(
        moving, chunks, gu_own, gu_other, gu_mine_other, down_own, down_other, slope_all
    )
    chunks.append(chunk(gu_own, gu_other, 1, 1))
    moving = large_ring.scatter_step(parts, 3, moving)
    gu_mine_other = swap(gu_mine_other, "core")
    down_other = swap(down_other, "core")
    down_mine, down_mine_other = down_sums(0, slope_all)
    moving, chunks, gu_own, gu_other, gu_mine_other, down_other, down_mine, down_mine_other, hidden_low = together(
        moving, chunks, gu_own, gu_other, gu_mine_other, down_other, down_mine, down_mine_other, hidden_low
    )
    grad_two = large_ring.scatter_end(parts, moving)
    middle_grad = slope_low.astype(wide) + norm_backward(normed_two, inverse_two, grad_two)

    chunks.append(chunk(gu_own, gu_other, 2, 1))
    middle_low = middle_grad.astype(low)
    slots = [None, small_ring.up(middle_low), middle_low, small_ring.down(middle_low)]
    branch_other = down_project(large_ring, hidden_low, hidden_weight, width, True)
    slots[1:], chunks, gu_own, gu_other, down_mine_other, branch_other, gu_mine = together(
        slots[1:], chunks, gu_own, gu_other, down_mine_other, branch_other, gu_mine
    )
    chunks.append(chunk(gu_own, gu_other, 3, 1))
    cut = shard // 2
    slots[0] = jnp.concatenate([small_ring.up(slots[1][:cut]), small_ring.down(slots[3][cut:])], axis=0)
    down_mine_other = swap(down_mine_other, "core")
    gu_mine = add_low(gu_mine, gu_mine_other)
    slots, chunks, down_mine_other, down_own, down_other, gu_mine = together(
        slots, chunks, down_mine_other, down_own, down_other, gu_mine
    )
    down_chunks = [chunk(down_own, down_other, 0, rows // 2)]
    middle_all = gather_group(small_ring, slots)
    gu_total = sum_pairs(add_low(gu_mine, jnp.concatenate(chunks, axis=0)))
    gu_got = exchange_rows(gu_total)
    middle_all, down_chunks, down_own, down_other, branch_other = together(
        middle_all, down_chunks, down_own, down_other, branch_other
    )

    def head_back(head):
        qkv, attended, logsums = kept[head]
        arrays = (middle_all, heads_weight[head], *seen, qkv, logsums)
        (slope,) = call_whole(attend_back_kernel, "attend_back", [qkv_shape], *arrays)
        shape = (rows, block, 4 * depth)
        return slope, call_blocks(head_sum_kernel, "head_sum", [rows_one, middle_all], [slope, attended], [shape])[0]

    down_chunks.append(chunk(down_own, down_other, rows // 2, rows // 2))
    branch_other = split_rows(branch_other, HALF)
    branch_other[0] = swap(branch_other[0], "y")
    theirs_slope, theirs_sum = head_back(1)
    middle_all, theirs_slope, theirs_sum, down_chunks, branch_other, hidden_low = together(
        middle_all, theirs_slope, theirs_sum, down_chunks, branch_other, hidden_low
    )
    branch_other[1] = swap(branch_other[1], "y")
    head_first = swap(theirs_sum[: rows // 2], "x")
    mine_slope, mine_sum = head_back(0)
    back_parts = project("qkv_back", slice(0, 3 * depth), [mine_slope, theirs_slope], heads_weight)
    down_total = add_low(add_low(down_mine, down_mine_other), jnp.concatenate(down_chunks, axis=0))
    back_parts, mine_sum, head_first, theirs_sum, branch_other, gu_got, down_total, hidden_low = together(
        back_parts, mine_sum, head_first, theirs_sum, branch_other, gu_got, down_total, hidden_low
    )
    down_got = exchange_rows(sum_pairs(down_total))
    head_second = swap(theirs_sum[rows // 2 :], "x")
    back_total = add_low(back_parts[0], swap(back_parts[1], "core"))
    back_slots = split_rows(back_total, small_ring.size)
    moving = small_ring.scatter_start(back_slots)
    branch_own = down_project(large_ring, hidden_low, hidden_weight, width, False)
    branch_half = add_low(branch_own, jnp.concatenate(branch_other, axis=0)).reshape(rows, shard, width)
    moving, back_slots, down_got, branch_half, head_second, gu_got = together(
        moving, back_slots, down_got, branch_half, head_second, gu_got
    )
    branch_got = exchange_rows(branch_half)
    gu_theirs = swap(gu_got, "x")
    moving = small_ring.scatter_step(back_slots, 1, moving)
    head_total = sum_pairs(add_low(mine_sum, jnp.concatenate([head_first, head_second], axis=0)))
    moving, head_total, branch_got, gu_theirs, down_got = together(moving, head_total, branch_got, gu_theirs, down_got)
    head_got = exchange_rows(head_total)
    down_theirs = swap(down_got, "x")
    grad_one = small_ring.scatter_end(back_slots, moving)
    input_low = (middle_grad + norm_backward(normed_one, inverse_one, grad_one)).astype(low)
    output_low = (middle + jnp.sum(branch_got.astype(wide), axis=0)).astype(low)
    head_got, down_theirs, input_low, output_low, gu_got, down_got, gu_theirs = together(
        head_got, down_theirs, input_low, output_low, gu_got, down_got, gu_theirs
    )
    head_got = head_got.reshape(rows // line, line, block, 4 * depth)
    head_mine = jnp.sum(head_got.astype(wide), axis=0).astype(low)
    head_theirs = swap(head_mine, "x")
    layer_out, input_grad = from_shards((output_low, input_low), seqs)
    gate_grad, up_grad, down_grad = assemble_units(gu_got, down_got, gu_theirs, down_theirs)
    layer_out, input_grad, head_mine, head_theirs = together(layer_out, input_grad, head_mine, head_theirs)
    input_grad = input_grad.astype(wide)
    query_grad, key_grad, value_grad, out_grad = assemble(head_mine, head_theirs)

    return (
        layer_out,
        input_grad,
        query_grad,
        key_grad,
        value_grad,
        out_grad,
        gate_grad,
        up_grad,
        down_grad,
    )


def solution(mesh):
    dp, rows, cols = (mesh.shape[name] for name in ("dp", "row", "col"))
    sizes = (dp // HALF, HALF, HALF, rows // HALF, cols // HALF, HALF)
    fine = Mesh(mesh.devices.reshape(sizes), ("pair", "x", "zhi", "zlo", "y", "core"))
    across, inner, tall = ("pair", "x"), ("y", "core"), ROW
    split = P(across, inner, tall)
    inward = P(tall, inner)
    outward = P(inner, tall)
    return jax.shard_map(
        on_device,
        mesh=fine,
        in_specs=(split, inward, inward, inward, outward, inward, inward, outward, split),
        out_specs=(split, split, inward, inward, inward, outward, inward, inward, outward),
        check_vma=False,
    )
```

```python
import functools

import jax
import jax.numpy as jnp
from jax import lax
from jax.experimental import pallas as pl
from jax.experimental.pallas import tpu as pltpu
from jax.sharding import Mesh
from jax.sharding import PartitionSpec as P

HEAD_DIM = 128
BLOCK = 512
HALF = 2

epsilon = 1e-05
rope_base = 10000.0
masked_score = -1e30
low = jnp.bfloat16
CHEAP = pl.CostEstimate(flops=1, transcendentals=0, bytes_accessed=1)
wide = jnp.float32


def rope_tables(places, head_depth):
    halfway = head_depth // 2
    position = places.astype(jnp.float32)[:, None]
    frequency = rope_base ** (-(2.0 * jnp.arange(halfway).astype(jnp.float32)) / head_depth)
    angles = position * frequency[None, :]
    cosine = jnp.concatenate([jnp.cos(angles), jnp.cos(angles)], axis=1)
    sine_table = jnp.concatenate([jnp.sin(angles), jnp.sin(angles)], axis=1)
    return (cosine, sine_table)


def dot(left, right):
    return jnp.dot(left, right, preferred_element_type=wide)


def layer_norm(stream):
    average = jnp.mean(stream, axis=1, keepdims=True)
    centered = stream - average
    inverse = lax.rsqrt(jnp.mean(centered * centered, axis=1, keepdims=True) + epsilon)
    return centered * inverse, inverse


def norm_backward(normed, inverse, gradient):
    average = jnp.mean(gradient, axis=1, keepdims=True)
    crossed = jnp.mean(gradient * normed, axis=1, keepdims=True)
    return inverse * (gradient - average - normed * crossed)


def turn(array):
    return pltpu.roll(array, array.shape[1] // 2, 1)


def rope_sign(depth):
    return jnp.where(lax.broadcasted_iota(jnp.int32, (1, depth), 1) < depth // 2, -1.0, 1.0)


def attend_kernel(own_ref, other_ref, weight_ref, cosine_ref, sine_ref, column_ref, line_ref, qkv_ref, heads_ref, logsum_ref):
    depth = heads_ref.shape[1]
    weight = weight_ref[:, : 3 * depth]
    qkv = jnp.concatenate([dot(own_ref[...], weight), dot(other_ref[...], weight)], axis=0)
    cosine, sine = cosine_ref[...], sine_ref[...] * rope_sign(depth)
    rope = lambda w: (w * cosine + turn(w) * sine).astype(low)
    queries, key_rows = rope(qkv[:, :depth]), rope(qkv[:, depth : 2 * depth])
    values = qkv[:, 2 * depth :].astype(low)
    qkv_ref[...] = jnp.concatenate([queries, key_rows, values], axis=1)
    for at in range(0, queries.shape[0], BLOCK):
        part = slice(at, at + BLOCK)
        scores = dot_last(queries[part], key_rows) * depth**-0.5
        scores = jnp.where(column_ref[part] >= line_ref[...], scores, masked_score)
        highest = jnp.max(scores, axis=1, keepdims=True)
        shifted = jnp.exp(scores - highest)
        totals = jnp.sum(shifted, axis=1, keepdims=True)
        logsum_ref[part] = highest + jnp.log(totals)
        weights = (shifted * (1.0 / totals)).astype(low)
        heads_ref[part] = dot(weights, values).astype(low)


def attend_back_kernel(
    own_ref, other_ref, weight_ref, cosine_ref, sine_ref, column_ref, line_ref, qkv_ref, logsum_ref, slope_ref
):
    depth = cosine_ref.shape[1]
    scaling = depth**-0.5
    queries, key_rows, values = (qkv_ref[:, i * depth : (i + 1) * depth] for i in range(3))
    weight = weight_ref[:, 3 * depth :]
    head_grad = jnp.concatenate([dot(own_ref[...], weight), dot(other_ref[...], weight)], axis=0).astype(low)
    query_parts = []
    key_grad = value_grad = None
    for at in range(0, queries.shape[0], BLOCK):
        part = slice(at, at + BLOCK)
        scores = dot_last(queries[part], key_rows) * scaling
        scores = jnp.where(column_ref[part] >= line_ref[...], scores, masked_score)
        probable = jnp.exp(scores - logsum_ref[part])
        product = dot_last(head_grad[part], values)
        slopes = probable * (product - jnp.sum(probable * product, axis=1, keepdims=True))
        slopes = slopes.astype(low)
        query_parts.append(dot(slopes, key_rows) * scaling)
        key_part = dot_first(slopes, queries[part]) * scaling
        value_part = dot_first(probable.astype(low), head_grad[part])
        key_grad = key_part if at == 0 else key_grad + key_part
        value_grad = value_part if at == 0 else value_grad + value_part
    cosine, sine = cosine_ref[...], sine_ref[...]
    undo = lambda g: (g * cosine - turn(g * sine) * rope_sign(depth)).astype(low)
    slope_ref[:, :depth] = undo(jnp.concatenate(query_parts, axis=0))
    slope_ref[:, depth : 2 * depth] = undo(key_grad)
    slope_ref[:, 2 * depth :] = value_grad.astype(low)


def project_kernel(columns, *refs):
    lefts, weights = refs[: len(refs) // 2 - 1], refs[len(refs) // 2 - 1 : -2]
    part = sum(dot_last(left[...], weight[:, columns]) for left, weight in zip(lefts, weights)).astype(low)
    first = 2 * pl.program_id(0) < pl.num_programs(0)

    @pl.when(first)
    def _():
        refs[-2][...] = part

    @pl.when(jnp.logical_not(first))
    def _():
        refs[-1][...] = part


def project(name, columns, lefts, weights, tile=256):
    count, width = lefts[0].shape[0], weights[0].shape[0]
    last = count // tile // HALF - 1
    whole = lambda array: pl.BlockSpec(array.shape, lambda i: (0, 0), pipeline_mode=pl.Buffered(buffer_count=1))
    return pl.pallas_call(
        functools.partial(project_kernel, columns),
        grid=(count // tile,),
        in_specs=[pl.BlockSpec((tile, left.shape[1]), lambda i: (i, 0)) for left in lefts]
        + [whole(weight) for weight in weights],
        out_specs=[
            pl.BlockSpec((tile, width), lambda i: (jnp.minimum(i, last), 0)),
            pl.BlockSpec((tile, width), lambda i: (jnp.maximum(i - last - 1, 0), 0)),
        ],
        out_shape=[jax.ShapeDtypeStruct((count // HALF, width), low)] * HALF,
        compiler_params=pltpu.CompilerParams(vmem_limit_bytes=48 * 1024 * 1024),
        cost_estimate=CHEAP,
        name=name,
    )(*lefts, *weights)


def head_sum_kernel(rows_own, rows_other, middle_own, middle_other, slope_ref, attended_ref, out_ref):
    half = rows_own.shape[0]

    def product(own, other, right):
        return dot_first(own[...], right[:half]) + dot_first(other[...], right[half:])

    parts = [product(rows_own, rows_other, slope_ref), product(middle_own, middle_other, attended_ref)]
    out_ref[0] = jnp.concatenate(parts, axis=1).astype(low)


def gu_sum_kernel(blocks, first_rows, second_rows, first_slope, second_slope, *out_refs):
    first, second = first_rows[...], second_rows[...]
    for block, out_ref in zip(blocks, out_refs):
        size = out_ref.shape[2]
        cut = slice(block * size, (block + 1) * size)
        out_ref[0] = (dot_first(first, first_slope[:, cut]) + dot_first(second, second_slope[:, cut])).astype(low)


def down_sum_kernel(blocks, first_slope, second_slope, first_hidden, second_hidden, *out_refs):
    first, second = first_slope[...], second_slope[...]
    for block, out_ref in zip(blocks, out_refs):
        units = out_ref.shape[1]
        cut = slice(block * units, (block + 1) * units)
        out_ref[0] = (dot_first(first_hidden[:, cut], first) + dot_first(second_hidden[:, cut], second)).astype(low)


def call_blocks(kernel, name, cut, held, shapes):
    count = shapes[0][0]
    return pl.pallas_call(
        kernel,
        grid=(count,),
        in_specs=[pl.BlockSpec((array.shape[0], array.shape[1] // count), lambda i: (0, i)) for array in cut]
        + [pl.BlockSpec(array.shape, lambda i: (0, 0)) for array in held],
        out_specs=[pl.BlockSpec((1,) + shape[1:], lambda i: (i, 0, 0)) for shape in shapes],
        out_shape=[jax.ShapeDtypeStruct(shape, low) for shape in shapes],
        compiler_params=pltpu.CompilerParams(vmem_limit_bytes=48 * 1024 * 1024),
        cost_estimate=CHEAP,
        name=name,
    )(*cut, *held)


def assemble_kernel(x_ref, mine_ref, theirs_ref, query_ref, key_ref, value_ref, out_ref):
    line, block, depth = mine_ref.shape[0], mine_ref.shape[1], HEAD_DIM
    for i in range(line):
        for source, turned in ((mine_ref, x_ref[0]), (theirs_ref, 1 - x_ref[0])):
            place = pl.ds(pl.multiple_of((HALF * i + turned) * depth, depth), depth)
            for n, target in enumerate((query_ref, key_ref, value_ref)):
                target[:, place] = source[i, :, n * depth : (n + 1) * depth].astype(wide)
            out_ref[place, :] = source[i, :, 3 * depth :].astype(wide).T


def assemble(mine, theirs):
    line, block, _ = mine.shape
    shape = jax.ShapeDtypeStruct((block, block), wide)
    whole = pl.BlockSpec(memory_space=pltpu.VMEM)
    return pl.pallas_call(
        assemble_kernel,
        in_specs=[pl.BlockSpec(memory_space=pltpu.SMEM), whole, whole],
        out_specs=[whole] * 4,
        out_shape=[shape] * 4,
        cost_estimate=CHEAP,
        name="assemble",
    )(lax.axis_index("x")[None].astype(jnp.int32), mine, theirs)


def assemble_units_kernel(x_ref, mine_ref, theirs_ref, gate_ref, up_ref, down_ref):
    size, units = gate_ref.shape[0], down_ref.shape[0] // HALF
    mine, theirs = mine_ref[0].astype(wide), theirs_ref[0].astype(wide)
    first = jnp.where(x_ref[0] == 0, mine, theirs)
    second = jnp.where(x_ref[0] == 0, theirs, mine)
    gate_ref[...] = jnp.concatenate([first[:size, :units], second[:size, :units]], axis=1)
    up_ref[...] = jnp.concatenate([first[:size, units:], second[:size, units:]], axis=1)
    down_ref[...] = jnp.concatenate([first[size:], second[size:]], axis=0)


def assemble_units(mine, theirs):
    rows, height, size = mine.shape
    share = HALF * (height - size)
    arrived = pl.BlockSpec((1, height, size), lambda i, x: (i, 0, 0))
    columns = pl.BlockSpec((size, share), lambda i, x: (0, i))
    wide_shape = jax.ShapeDtypeStruct((size, rows * share), wide)
    return pl.pallas_call(
        assemble_units_kernel,
        grid_spec=pltpu.PrefetchScalarGridSpec(
            num_scalar_prefetch=1,
            grid=(rows,),
            in_specs=[arrived, arrived],
            out_specs=[columns, columns, pl.BlockSpec((share, size), lambda i, x: (i, 0))],
        ),
        out_shape=[wide_shape, wide_shape, jax.ShapeDtypeStruct((rows * share, size), wide)],
        compiler_params=pltpu.CompilerParams(vmem_limit_bytes=48 * 1024 * 1024),
        cost_estimate=CHEAP,
        name="assemble_units",
    )(lax.axis_index("x")[None].astype(jnp.int32), mine, theirs)


def call_whole(kernel, name, shapes, *arrays):
    whole = pl.BlockSpec(memory_space=pltpu.VMEM)
    return pl.pallas_call(
        kernel,
        in_specs=[whole] * len(arrays),
        out_specs=[whole] * len(shapes),
        out_shape=shapes,
        compiler_params=pltpu.CompilerParams(vmem_limit_bytes=48 * 1024 * 1024),
        cost_estimate=CHEAP,
        name=name,
    )(*arrays)


def dot_last(left, right):
    return lax.dot_general(left, right, (((1,), (1,)), ((), ())), preferred_element_type=wide)


def dot_first(left, right):
    return lax.dot_general(left, right, (((0,), (0,)), ((), ())), preferred_element_type=wide)


def swap(array, axis):
    return lax.ppermute(array, axis, [(0, 1), (1, 0)])


class Ring:
    def __init__(self, axes, line):
        self.axes = axes
        self.size = 2 * line
        self.half = line
        flat = [2 * n if n < line else 2 * (2 * line - 1 - n) + 1 for n in range(self.size)]
        self.upward = [(flat[i], flat[(i + 1) % self.size]) for i in range(self.size)]
        self.downward = [(b, a) for a, b in self.upward]

    def up(self, array):
        return lax.ppermute(array, self.axes, self.upward)

    def down(self, array):
        return lax.ppermute(array, self.axes, self.downward)

    def place(self):
        level, side = lax.axis_index(self.axes[:-1]), lax.axis_index(self.axes[-1])
        return jnp.where(side == 0, level, self.size - 1 - level)

    def gather(self, shard, waits={}):
        half, cut = self.half, shard.shape[0] // 2
        slots = [None] * self.size
        slots[half] = rising = falling = shard
        for step in range(1, half + 1):
            rising, falling = after((rising, falling), waits.get(step))
            if step == half:
                break
            slots[half - step] = rising = self.up(rising)
            slots[half + step] = falling = self.down(falling)
        slots[0] = jnp.concatenate([self.up(rising[:cut]), self.down(falling[cut:])], axis=0)
        return slots

    def scatter_start(self, parts):
        cut = parts[0].shape[0] // 2
        return self.up(parts[0][:cut]), self.down(parts[0][cut:])

    def scatter_step(self, parts, step, moving):
        rising, falling = moving
        cut = rising.shape[0]
        over, under = parts[self.size - step], parts[step]
        if step == 1:
            over = jnp.concatenate([add_low(over[:cut], rising), over[cut:]], axis=0)
            under = jnp.concatenate([under[:cut], add_low(under[cut:], falling)], axis=0)
        else:
            over, under = add_low(over, rising), add_low(under, falling)
        return self.up(over), self.down(under)

    def scatter_end(self, parts, moving):
        return sum(part.astype(wide) for part in (parts[self.half],) + moving)

    def scatter(self, parts):
        moving = self.scatter_start(parts)
        for step in range(1, self.half):
            moving = self.scatter_step(parts, step, moving)
        return self.scatter_end(parts, moving)


def add_low(left, right):
    return (left.astype(wide) + right.astype(wide)).astype(low)


def split_rows(array, count):
    rows = array.shape[0] // count
    return [array[i * rows : (i + 1) * rows] for i in range(count)]


def gather_group(slots):
    own = jnp.concatenate(slots, axis=0)
    return [own, swap(own, "core")]


def scatter_group(ring, own, other, awaited=None):
    total = after(add_low(own, swap(other, "core")), awaited)
    return ring.scatter(split_rows(total, ring.size))


def exchange_rows(array):
    return lax.all_to_all(array, ROW, 0, 0, tiled=True)


ROW = ("zhi", "zlo")


def to_shard(blocks):
    return jnp.transpose(blocks, (1, 0, 2)).reshape(blocks.shape[1], -1)


def from_shards(arrays, seqs):
    rows, count = lax.axis_size(ROW), len(arrays)
    tokens, width = arrays[0].shape[0], arrays[0].shape[1] // rows
    stacked = jnp.concatenate(arrays, axis=0).reshape(count * tokens, rows, width)
    got = exchange_rows(jnp.transpose(stacked, (1, 0, 2)))
    return [
        got[:, i * tokens : (i + 1) * tokens].reshape(seqs, rows * tokens // seqs, width)
        for i in range(count)
    ]


def together(*arrays):
    return lax.optimization_barrier(arrays)


def after(arrays, others):
    if others is None:
        return arrays
    return lax.optimization_barrier((arrays, others))[0]


def sum_pairs(array):
    return lax.psum(array, "pair") if lax.axis_size("pair") > 1 else array


def pack_kernel(x_ref, query, key, value, out, gate, up, down, head, hidden):
    head[0] = jnp.concatenate([query[...], key[...], value[...], out[...].T], axis=1)
    hidden[0] = jnp.concatenate([jnp.concatenate([gate[...], up[...]], axis=1), down[...]], axis=0)


def pack(query, key, value, out, gate, up, down, rows, line):
    depth, block = HEAD_DIM, query.shape[0]
    units = gate.shape[1] // rows // HALF
    head_at = lambda r, x: HALF * (r % line) + x[0]
    head_in = pl.BlockSpec((block, depth), lambda r, x: (0, head_at(r, x)))
    out_in = pl.BlockSpec((depth, block), lambda r, x: (head_at(r, x), 0))
    unit_in = pl.BlockSpec((block, units), lambda r, x: (0, HALF * r + x[0]))
    down_in = pl.BlockSpec((units, block), lambda r, x: (HALF * r + x[0], 0))
    shapes = [(block, 4 * depth), (block + units, block)]
    return pl.pallas_call(
        pack_kernel,
        grid_spec=pltpu.PrefetchScalarGridSpec(
            num_scalar_prefetch=1,
            grid=(rows,),
            in_specs=[head_in, head_in, head_in, out_in, unit_in, unit_in, down_in],
            out_specs=[pl.BlockSpec((1,) + shape, lambda r, x: (r, 0, 0)) for shape in shapes],
        ),
        out_shape=[jax.ShapeDtypeStruct((rows,) + shape, low) for shape in shapes],
        name="pack_weights",
    )(lax.axis_index("x")[None].astype(jnp.int32), query, key, value, out, gate, up, down)


def mlp_kernel(*refs):
    tiles, weights = refs[:4], refs[4:-5]
    hidden_ref, gu_slope_ref, both_ref, rows_ref, slope_ref = refs[-5:]
    parts, height, span = weights[0].shape
    units = height - span
    rows_ref[...] = jnp.concatenate([tiles[0][...], tiles[2][...]], axis=0)
    slope_ref[...] = jnp.concatenate([tiles[1][...], tiles[3][...]], axis=0)
    cuts = [slice(k * span, (k + 1) * span) for k in range(parts)]
    totals, branches = [None] * parts, [None] * parts
    for i, weight in enumerate(weights):
        gate_up = sum(dot(rows_ref[:, cut], weight[k, :span]) for k, cut in enumerate(cuts))
        gate, up = gate_up[:, :units], gate_up[:, units:]
        sigmoid = 1.0 / (1.0 + jnp.exp(-gate))
        activated = gate * sigmoid
        hidden = (activated * up).astype(low)
        hidden_ref[:, i * units : (i + 1) * units] = hidden
        hidden_grad = sum(dot_last(slope_ref[:, cut], weight[k, span:]) for k, cut in enumerate(cuts))
        gate_slope = hidden_grad * up * sigmoid * (1.0 + gate * (1.0 - sigmoid))
        gu_slope = jnp.concatenate([gate_slope, hidden_grad * activated], axis=1).astype(low)
        gu_slope_ref[:, 2 * i * units : 2 * (i + 1) * units] = gu_slope
        for k in range(parts):
            part, branch = dot_last(gu_slope, weight[k, :span]), dot(hidden, weight[k, span:])
            totals[k] = part if i == 0 else totals[k] + part
            branches[k] = branch if i == 0 else branches[k] + branch
    tile = tiles[0].shape[0]
    for k, cut in enumerate(cuts):
        for n in range(HALF):
            tokens = slice(n * tile, (n + 1) * tile)
            both_ref[2 * n * tile : (2 * n + 1) * tile, cut] = totals[k][tokens].astype(low)
            both_ref[(2 * n + 1) * tile : 2 * (n + 1) * tile, cut] = branches[k][tokens].astype(low)


def feed_forward(both, weights, tile):
    count, width = both.shape[0] // HALF, both.shape[1]
    parts, height, span = weights[0].shape
    blocks, units = len(weights), height - span
    steps = count // (HALF * tile)
    single = lambda n: pl.BlockSpec((tile, width), lambda i: (4 * i + n, 0))
    whole = lambda array: pl.BlockSpec(array.shape, lambda i: (0, 0, 0), pipeline_mode=pl.Buffered(buffer_count=1))
    shapes = [(count, size) for size in (blocks * units, 2 * blocks * units, width, width, width)]
    shapes[2] = both.shape
    return pl.pallas_call(
        mlp_kernel,
        grid=(steps,),
        in_specs=[single(n) for n in range(4)] + [whole(weight) for weight in weights],
        out_specs=[pl.BlockSpec((shape[0] // steps, shape[1]), lambda i: (i, 0)) for shape in shapes],
        out_shape=[jax.ShapeDtypeStruct(shape, low) for shape in shapes],
        compiler_params=pltpu.CompilerParams(vmem_limit_bytes=48 * 1024 * 1024),
        cost_estimate=CHEAP,
        name="feed_forward",
    )(*[both] * 4, *weights)


def on_device(
    tokens,
    query_weight,
    key_weight,
    value_weight,
    out_weight,
    gate_weight,
    up_weight,
    down_weight,
    cotangent,
):
    depth = HEAD_DIM
    rows, line = lax.axis_size(ROW), lax.axis_size("zlo")
    small_ring = Ring(("zlo", "y"), line)
    large_ring = Ring(("zhi", "zlo", "y"), rows)
    seqs, width = tokens.shape[0], tokens.shape[2] * rows
    block = width // rows
    units = gate_weight.shape[1] // rows // HALF

    shard = seqs * tokens.shape[1] // rows
    pieces = [array.reshape(rows, shard, block) for array in (tokens, cotangent)]
    weights = (query_weight, key_weight, value_weight, out_weight, gate_weight, up_weight, down_weight)
    head_pieces, hidden_pieces = pack(*weights, rows, line)
    got = exchange_rows(jnp.concatenate(pieces, axis=1))
    got, head_pieces, hidden_pieces = together(got, head_pieces, hidden_pieces)
    stream = to_shard(got[:, :shard]).astype(wide)
    slope_low = to_shard(got[:, shard:])

    head_mine = exchange_rows(head_pieces)

    place = jnp.arange(2 * small_ring.size)
    core = (lax.axis_index("core") + place // small_ring.size) % 2
    spot = (small_ring.place() + place % small_ring.size + small_ring.half) % small_ring.size
    slot_side = spot // line
    slot_level = jnp.where(slot_side == 0, spot, small_ring.size - 1 - spot)
    first = ((2 * slot_side + core) * line + slot_level) * shard
    places = (first[:, None] + jnp.arange(shard)[None, :]).reshape(-1)
    cosine, sine_table = rope_tables(places, depth)

    normed_one, inverse_one = layer_norm(stream)
    rows_one = gather_group(small_ring.gather(normed_one.astype(low)))
    rows_one, head_mine, hidden_pieces = together(rows_one, head_mine, hidden_pieces)
    heads_weight = [head_mine.reshape(width, 4 * depth)]
    heads_weight.append(swap(heads_weight[0], "x"))

    hidden_mine = exchange_rows(hidden_pieces)
    hidden_theirs = swap(hidden_mine, "x")
    length = HALF * rows_one[0].shape[0]
    seen = (cosine, sine_table, places[:, None], places[None, :])
    qkv_shape = jax.ShapeDtypeStruct((length, 3 * depth), low)
    kept = []
    for weight in heads_weight:
        shapes = [qkv_shape, jax.ShapeDtypeStruct((length, depth), low), jax.ShapeDtypeStruct((length, 1), wide)]
        kept.append(call_whole(attend_kernel, "attend", shapes, *rows_one, weight, *seen))
    heads = [part[1] for part in kept]
    out_parts = project("out_project", slice(3 * depth, 4 * depth), heads, heads_weight)
    middle = stream + scatter_group(small_ring, *out_parts, hidden_mine)
    normed_two, inverse_two = layer_norm(middle)
    both = jnp.concatenate([normed_two.astype(low), slope_low], axis=0)
    slots, size = [None] * large_ring.size, large_ring.half
    slots[size] = rising = falling = both
    for step in range(1, size):
        if step == size - 1:
            rising, falling, hidden_theirs = together(rising, falling, hidden_theirs)
            hidden_weight = [hidden_mine, hidden_theirs, swap(hidden_mine, "core"), swap(hidden_theirs, "core")]
            inner = jnp.concatenate(slots[2:6], axis=0)
            inner_parts = feed_forward(inner, hidden_weight, shard)
        slots[size - step] = rising = large_ring.up(rising)
        slots[size + step] = falling = large_ring.down(falling)
    rising, falling, inner_parts, hidden_weight = together(rising, falling, inner_parts, hidden_weight)
    slots[size - step], slots[size + step] = rising, falling
    slots[0] = jnp.concatenate([large_ring.up(rising[:shard]), large_ring.down(falling[shard:])], axis=0)
    outer = jnp.concatenate([*slots[6:], *slots[:2]], axis=0)
    outer_parts = feed_forward(outer, hidden_weight, shard)
    hidden_low, gu_slope, both_parts, rows_two, slope_all = map(list, zip(inner_parts, outer_parts))

    def gu_sums(i, left):
        kernel = functools.partial(gu_sum_kernel, (i, i + 2))
        return call_blocks(kernel, "gu_sum", left, gu_slope, [(rows, block, 2 * units)] * 2)

    def down_sums(i, left):
        kernel = functools.partial(down_sum_kernel, (i, i + 2))
        return call_blocks(kernel, "down_sum", left, hidden_low, [(rows, units, block)] * 2)

    def slot_parts(inner, outer):
        inner, outer = split_rows(inner, 4), split_rows(outer, 4)
        return outer[2:] + inner + outer[:2]

    moving = large_ring.scatter_start(slot_parts(*both_parts))
    gu_own, gu_other = gu_sums(1, rows_two)
    moving, gu_own, gu_other, rows_two, slope_all, both_parts = together(
        moving, gu_own, gu_other, rows_two, slope_all, both_parts
    )
    parts = slot_parts(*both_parts)
    moving = large_ring.scatter_step(parts, 1, moving)
    gu_other = swap(gu_other, "core")
    gu_mine, gu_mine_other = gu_sums(0, rows_two)
    down_own, down_other = down_sums(1, slope_all)
    moving, gu_own, gu_other, gu_mine, gu_mine_other, slope_all, down_own, down_other = together(
        moving, gu_own, gu_other, gu_mine, gu_mine_other, slope_all, down_own, down_other
    )

    def chunk(own, other, k, n):
        return swap(add_low(own[k : k + n], other[k : k + n]), "x")

    chunks = [chunk(gu_own, gu_other, 0, rows // 2)]
    moving = large_ring.scatter_step(parts, 2, moving)
    down_other, gu_mine_other = swap(down_other, "core"), swap(gu_mine_other, "core")
    down_mine, down_mine_other = down_sums(0, slope_all)
    moving, chunks, gu_own, gu_other, gu_mine, gu_mine_other, down_own, down_other, down_mine_other = together(
        moving, chunks, gu_own, gu_other, gu_mine, gu_mine_other, down_own, down_other, down_mine_other
    )
    chunks.append(chunk(gu_own, gu_other, rows // 2, rows // 2))
    moving = large_ring.scatter_step(parts, 3, moving)
    down_mine_other = swap(down_mine_other, "core")
    gu_mine = add_low(gu_mine, gu_mine_other)
    moving, chunks, gu_mine, down_mine, down_mine_other, down_own, down_other = together(
        moving, chunks, gu_mine, down_mine, down_mine_other, down_own, down_other
    )
    grad_two, branch = split_rows(large_ring.scatter_end(parts, moving), HALF)
    middle_grad = slope_low.astype(wide) + norm_backward(normed_two, inverse_two, grad_two)
    output_low = (middle + branch).astype(low)

    down_chunks = [chunk(down_own, down_other, 0, rows // 2)]
    middle_low = middle_grad.astype(low)
    slots = [None, small_ring.up(middle_low), middle_low, small_ring.down(middle_low)]
    down_mine = add_low(down_mine, down_mine_other)
    slots[1:], down_chunks, down_own, down_other, down_mine, chunks, gu_mine = together(
        slots[1:], down_chunks, down_own, down_other, down_mine, chunks, gu_mine
    )
    down_chunks.append(chunk(down_own, down_other, rows // 2, rows // 2))
    cut = shard // 2
    slots[0] = jnp.concatenate([small_ring.up(slots[1][:cut]), small_ring.down(slots[3][cut:])], axis=0)
    gu_total = add_low(gu_mine, jnp.concatenate(chunks, axis=0))
    slots, down_chunks, gu_total = together(slots, down_chunks, gu_total)
    down_total = add_low(down_mine, jnp.concatenate(down_chunks, axis=0))
    unit_got = exchange_rows(sum_pairs(jnp.concatenate([gu_total, down_total], axis=1)))
    middle_all = gather_group(slots)

    def head_back(head):
        qkv, attended, logsums = kept[head]
        arrays = (*middle_all, heads_weight[head], *seen, qkv, logsums)
        (slope,) = call_whole(attend_back_kernel, "attend_back", [qkv_shape], *arrays)
        shape = (rows, block, 4 * depth)
        return slope, call_blocks(head_sum_kernel, "head_sum", rows_one + middle_all, [slope, attended], [shape])[0]

    theirs_slope, theirs_sum = head_back(1)
    middle_all, theirs_slope, theirs_sum = together(middle_all, theirs_slope, theirs_sum)
    head_chunks = [swap(theirs_sum[: rows // 2], "x")]
    mine_slope, mine_sum = head_back(0)
    back_parts = project("qkv_back", slice(0, 3 * depth), [mine_slope, theirs_slope], heads_weight)
    back_parts, mine_sum, head_chunks, theirs_sum = together(back_parts, mine_sum, head_chunks, theirs_sum)
    head_chunks.append(swap(theirs_sum[rows // 2 :], "x"))
    back_total = add_low(back_parts[0], swap(back_parts[1], "core"))
    back_total, mine_sum, head_chunks, unit_got = together(back_total, mine_sum, head_chunks, unit_got)

    head_got = exchange_rows(sum_pairs(add_low(mine_sum, jnp.concatenate(head_chunks, axis=0))))
    unit_theirs = swap(unit_got, "x")
    grad_one = small_ring.scatter(split_rows(back_total, small_ring.size))
    input_low = (middle_grad + norm_backward(normed_one, inverse_one, grad_one)).astype(low)
    head_got, unit_theirs, input_low, output_low, unit_got = together(
        head_got, unit_theirs, input_low, output_low, unit_got
    )
    head_got = head_got.reshape(rows // line, line, block, 4 * depth)
    head_mine = jnp.sum(head_got.astype(wide), axis=0).astype(low)
    head_theirs = swap(head_mine, "x")
    layer_out, input_grad = from_shards((output_low, input_low), seqs)
    gate_grad, up_grad, down_grad = assemble_units(unit_got, unit_theirs)
    layer_out, input_grad, head_mine, head_theirs = together(layer_out, input_grad, head_mine, head_theirs)
    input_grad = input_grad.astype(wide)
    query_grad, key_grad, value_grad, out_grad = assemble(head_mine, head_theirs)

    return (
        layer_out,
        input_grad,
        query_grad,
        key_grad,
        value_grad,
        out_grad,
        gate_grad,
        up_grad,
        down_grad,
    )


def solution(mesh):
    dp, rows, cols = (mesh.shape[name] for name in ("dp", "row", "col"))
    sizes = (dp // HALF, HALF, HALF, rows // HALF, cols // HALF, HALF)
    fine = Mesh(mesh.devices.reshape(sizes), ("pair", "x", "zhi", "zlo", "y", "core"))
    across, inner, tall = ("pair", "x"), ("y", "core"), ROW
    split = P(across, inner, tall)
    inward = P(tall, inner)
    outward = P(inner, tall)
    return jax.shard_map(
        on_device,
        mesh=fine,
        in_specs=(split, inward, inward, inward, outward, inward, inward, outward, split),
        out_specs=(split, split, inward, inward, inward, outward, inward, inward, outward),
        check_vma=False,
    )
```

```python
import functools

import jax
import jax.numpy as jnp
from jax import lax
from jax.experimental import pallas as pl
from jax.experimental.pallas import tpu as pltpu
from jax.sharding import Mesh
from jax.sharding import PartitionSpec as P

HEAD_DIM = 128
BLOCK = 512
HALF = 2

epsilon = 1e-05
rope_base = 10000.0
masked_score = -1e30
low = jnp.bfloat16
CHEAP = pl.CostEstimate(flops=1, transcendentals=0, bytes_accessed=1)
wide = jnp.float32


def rope_tables(places, head_depth):
    halfway = head_depth // 2
    position = places.astype(jnp.float32)[:, None]
    frequency = rope_base ** (-(2.0 * jnp.arange(halfway).astype(jnp.float32)) / head_depth)
    angles = position * frequency[None, :]
    cosine = jnp.concatenate([jnp.cos(angles), jnp.cos(angles)], axis=1)
    sine_table = jnp.concatenate([jnp.sin(angles), jnp.sin(angles)], axis=1)
    return (cosine, sine_table)


def dot(left, right):
    return jnp.dot(left, right, preferred_element_type=wide)


def layer_norm(stream):
    average = jnp.mean(stream, axis=1, keepdims=True)
    centered = stream - average
    inverse = lax.rsqrt(jnp.mean(centered * centered, axis=1, keepdims=True) + epsilon)
    return centered * inverse, inverse


def norm_backward(normed, inverse, gradient):
    average = jnp.mean(gradient, axis=1, keepdims=True)
    crossed = jnp.mean(gradient * normed, axis=1, keepdims=True)
    return inverse * (gradient - average - normed * crossed)


def turn(array):
    return pltpu.roll(array, array.shape[1] // 2, 1)


def rope_sign(depth):
    return jnp.where(lax.broadcasted_iota(jnp.int32, (1, depth), 1) < depth // 2, -1.0, 1.0)


def attend_kernel(own_ref, other_ref, weight_ref, cosine_ref, sine_ref, column_ref, line_ref, qkv_ref, heads_ref, logsum_ref):
    depth = heads_ref.shape[1]
    weight = weight_ref[:, : 3 * depth]
    qkv = jnp.concatenate([dot(own_ref[...], weight), dot(other_ref[...], weight)], axis=0)
    cosine, sine = cosine_ref[...], sine_ref[...] * rope_sign(depth)
    rope = lambda w: (w * cosine + turn(w) * sine).astype(low)
    queries, key_rows = rope(qkv[:, :depth]), rope(qkv[:, depth : 2 * depth])
    values = qkv[:, 2 * depth :].astype(low)
    qkv_ref[...] = jnp.concatenate([queries, key_rows, values], axis=1)
    for at in range(0, queries.shape[0], BLOCK):
        part = slice(at, at + BLOCK)
        scores = dot_last(queries[part], key_rows) * depth**-0.5
        scores = jnp.where(column_ref[part] >= line_ref[...], scores, masked_score)
        highest = jnp.max(scores, axis=1, keepdims=True)
        shifted = jnp.exp(scores - highest)
        totals = jnp.sum(shifted, axis=1, keepdims=True)
        logsum_ref[part] = highest + jnp.log(totals)
        weights = (shifted * (1.0 / totals)).astype(low)
        heads_ref[part] = dot(weights, values).astype(low)


def attend_back_kernel(
    own_ref, other_ref, weight_ref, cosine_ref, sine_ref, column_ref, line_ref, qkv_ref, logsum_ref, slope_ref
):
    depth = cosine_ref.shape[1]
    scaling = depth**-0.5
    queries, key_rows, values = (qkv_ref[:, i * depth : (i + 1) * depth] for i in range(3))
    weight = weight_ref[:, 3 * depth :]
    head_grad = jnp.concatenate([dot(own_ref[...], weight), dot(other_ref[...], weight)], axis=0).astype(low)
    query_parts = []
    key_grad = value_grad = None
    for at in range(0, queries.shape[0], BLOCK):
        part = slice(at, at + BLOCK)
        scores = dot_last(queries[part], key_rows) * scaling
        scores = jnp.where(column_ref[part] >= line_ref[...], scores, masked_score)
        probable = jnp.exp(scores - logsum_ref[part])
        product = dot_last(head_grad[part], values)
        slopes = probable * (product - jnp.sum(probable * product, axis=1, keepdims=True))
        slopes = slopes.astype(low)
        query_parts.append(dot(slopes, key_rows) * scaling)
        key_part = dot_first(slopes, queries[part]) * scaling
        value_part = dot_first(probable.astype(low), head_grad[part])
        key_grad = key_part if at == 0 else key_grad + key_part
        value_grad = value_part if at == 0 else value_grad + value_part
    cosine, sine = cosine_ref[...], sine_ref[...]
    undo = lambda g: (g * cosine - turn(g * sine) * rope_sign(depth)).astype(low)
    slope_ref[:, :depth] = undo(jnp.concatenate(query_parts, axis=0))
    slope_ref[:, depth : 2 * depth] = undo(key_grad)
    slope_ref[:, 2 * depth :] = value_grad.astype(low)


def project_kernel(columns, *refs):
    lefts, weights = refs[: len(refs) // 2 - 1], refs[len(refs) // 2 - 1 : -2]
    part = sum(dot_last(left[...], weight[:, columns]) for left, weight in zip(lefts, weights)).astype(low)
    first = 2 * pl.program_id(0) < pl.num_programs(0)

    @pl.when(first)
    def _():
        refs[-2][...] = part

    @pl.when(jnp.logical_not(first))
    def _():
        refs[-1][...] = part


def project(name, columns, lefts, weights, tile=256):
    count, width = lefts[0].shape[0], weights[0].shape[0]
    last = count // tile // HALF - 1
    whole = lambda array: pl.BlockSpec(array.shape, lambda i: (0, 0), pipeline_mode=pl.Buffered(buffer_count=1))
    return pl.pallas_call(
        functools.partial(project_kernel, columns),
        grid=(count // tile,),
        in_specs=[pl.BlockSpec((tile, left.shape[1]), lambda i: (i, 0)) for left in lefts]
        + [whole(weight) for weight in weights],
        out_specs=[
            pl.BlockSpec((tile, width), lambda i: (jnp.minimum(i, last), 0)),
            pl.BlockSpec((tile, width), lambda i: (jnp.maximum(i - last - 1, 0), 0)),
        ],
        out_shape=[jax.ShapeDtypeStruct((count // HALF, width), low)] * HALF,
        compiler_params=pltpu.CompilerParams(vmem_limit_bytes=12 * 1024 * 1024),
        cost_estimate=CHEAP,
        name=name,
    )(*lefts, *weights)


def head_sum_kernel(rows_own, rows_other, middle_own, middle_other, slope_ref, attended_ref, out_ref):
    half = rows_own.shape[0]

    def product(own, other, right):
        return dot_first(own[...], right[:half]) + dot_first(other[...], right[half:])

    parts = [product(rows_own, rows_other, slope_ref), product(middle_own, middle_other, attended_ref)]
    out_ref[0] = jnp.concatenate(parts, axis=1).astype(low)


def gu_sum_kernel(blocks, parts, *refs):
    rows, slopes, out_refs = refs[:parts], refs[parts : 2 * parts], refs[2 * parts :]
    rows = [part[...] for part in rows]
    for block, out_ref in zip(blocks, out_refs):
        size = out_ref.shape[2]
        cut = slice(block * size, (block + 1) * size)
        out_ref[0] = sum(dot_first(left, right[:, cut]) for left, right in zip(rows, slopes)).astype(low)


def down_sum_kernel(blocks, parts, *refs):
    slopes, hiddens, out_refs = refs[:parts], refs[parts : 2 * parts], refs[2 * parts :]
    slopes = [part[...] for part in slopes]
    for block, out_ref in zip(blocks, out_refs):
        units = out_ref.shape[1]
        cut = slice(block * units, (block + 1) * units)
        out_ref[0] = sum(dot_first(left[:, cut], right) for left, right in zip(hiddens, slopes)).astype(low)


def call_blocks(kernel, name, cut, held, shapes):
    count = shapes[0][0]
    return pl.pallas_call(
        kernel,
        grid=(count,),
        in_specs=[pl.BlockSpec((array.shape[0], array.shape[1] // count), lambda i: (0, i)) for array in cut]
        + [pl.BlockSpec(array.shape, lambda i: (0, 0)) for array in held],
        out_specs=[pl.BlockSpec((1,) + shape[1:], lambda i: (i, 0, 0)) for shape in shapes],
        out_shape=[jax.ShapeDtypeStruct(shape, low) for shape in shapes],
        compiler_params=pltpu.CompilerParams(vmem_limit_bytes=12 * 1024 * 1024),
        cost_estimate=CHEAP,
        name=name,
    )(*cut, *held)


def assemble_kernel(x_ref, mine_ref, theirs_ref, query_ref, key_ref, value_ref, out_ref):
    line, block, depth = mine_ref.shape[0], mine_ref.shape[1], HEAD_DIM
    for i in range(line):
        for source, turned in ((mine_ref, x_ref[0]), (theirs_ref, 1 - x_ref[0])):
            place = pl.ds(pl.multiple_of((HALF * i + turned) * depth, depth), depth)
            for n, target in enumerate((query_ref, key_ref, value_ref)):
                target[:, place] = source[i, :, n * depth : (n + 1) * depth].astype(wide)
            out_ref[place, :] = source[i, :, 3 * depth :].astype(wide).T


def assemble(mine, theirs):
    line, block, _ = mine.shape
    shape = jax.ShapeDtypeStruct((block, block), wide)
    whole = pl.BlockSpec(memory_space=pltpu.VMEM)
    return pl.pallas_call(
        assemble_kernel,
        in_specs=[pl.BlockSpec(memory_space=pltpu.SMEM), whole, whole],
        out_specs=[whole] * 4,
        out_shape=[shape] * 4,
        cost_estimate=CHEAP,
        name="assemble",
    )(lax.axis_index("x")[None].astype(jnp.int32), mine, theirs)


def assemble_units_kernel(x_ref, mine_ref, theirs_ref, gate_ref, up_ref, down_ref):
    size, units = gate_ref.shape[0], down_ref.shape[0] // HALF
    mine, theirs = mine_ref[0].astype(wide), theirs_ref[0].astype(wide)
    first = jnp.where(x_ref[0] == 0, mine, theirs)
    second = jnp.where(x_ref[0] == 0, theirs, mine)
    gate_ref[...] = jnp.concatenate([first[:size, :units], second[:size, :units]], axis=1)
    up_ref[...] = jnp.concatenate([first[:size, units:], second[:size, units:]], axis=1)
    down_ref[...] = jnp.concatenate([first[size:], second[size:]], axis=0)


def assemble_units(mine, theirs):
    rows, height, size = mine.shape
    share = HALF * (height - size)
    arrived = pl.BlockSpec((1, height, size), lambda i, x: (i, 0, 0))
    columns = pl.BlockSpec((size, share), lambda i, x: (0, i))
    wide_shape = jax.ShapeDtypeStruct((size, rows * share), wide)
    return pl.pallas_call(
        assemble_units_kernel,
        grid_spec=pltpu.PrefetchScalarGridSpec(
            num_scalar_prefetch=1,
            grid=(rows,),
            in_specs=[arrived, arrived],
            out_specs=[columns, columns, pl.BlockSpec((share, size), lambda i, x: (i, 0))],
        ),
        out_shape=[wide_shape, wide_shape, jax.ShapeDtypeStruct((rows * share, size), wide)],
        compiler_params=pltpu.CompilerParams(vmem_limit_bytes=10 * 1024 * 1024),
        cost_estimate=CHEAP,
        name="assemble_units",
    )(lax.axis_index("x")[None].astype(jnp.int32), mine, theirs)


def call_whole(kernel, name, shapes, *arrays):
    whole = pl.BlockSpec(memory_space=pltpu.VMEM)
    return pl.pallas_call(
        kernel,
        in_specs=[whole] * len(arrays),
        out_specs=[whole] * len(shapes),
        out_shape=shapes,
        compiler_params=pltpu.CompilerParams(vmem_limit_bytes=18 * 1024 * 1024),
        cost_estimate=CHEAP,
        name=name,
    )(*arrays)


def dot_last(left, right):
    return lax.dot_general(left, right, (((1,), (1,)), ((), ())), preferred_element_type=wide)


def dot_first(left, right):
    return lax.dot_general(left, right, (((0,), (0,)), ((), ())), preferred_element_type=wide)


def swap(array, axis):
    return lax.ppermute(array, axis, [(0, 1), (1, 0)])


class Ring:
    def __init__(self, axes, line):
        self.axes = axes
        self.size = 2 * line
        self.half = line
        flat = [2 * n if n < line else 2 * (2 * line - 1 - n) + 1 for n in range(self.size)]
        self.upward = [(flat[i], flat[(i + 1) % self.size]) for i in range(self.size)]
        self.downward = [(b, a) for a, b in self.upward]

    def up(self, array):
        return lax.ppermute(array, self.axes, self.upward)

    def down(self, array):
        return lax.ppermute(array, self.axes, self.downward)

    def place(self):
        level, side = lax.axis_index(self.axes[:-1]), lax.axis_index(self.axes[-1])
        return jnp.where(side == 0, level, self.size - 1 - level)

    def gather(self, shard, waits={}):
        half, cut = self.half, shard.shape[0] // 2
        slots = [None] * self.size
        slots[half] = rising = falling = shard
        for step in range(1, half + 1):
            rising, falling = after((rising, falling), waits.get(step))
            if step == half:
                break
            slots[half - step] = rising = self.up(rising)
            slots[half + step] = falling = self.down(falling)
        slots[0] = jnp.concatenate([self.up(rising[:cut]), self.down(falling[cut:])], axis=0)
        return slots

    def scatter_start(self, parts):
        cut = parts[0].shape[0] // 2
        return self.up(parts[0][:cut]), self.down(parts[0][cut:])

    def scatter_step(self, parts, step, moving):
        rising, falling = moving
        cut = rising.shape[0]
        over, under = parts[self.size - step], parts[step]
        if step == 1:
            over = jnp.concatenate([add_low(over[:cut], rising), over[cut:]], axis=0)
            under = jnp.concatenate([under[:cut], add_low(under[cut:], falling)], axis=0)
        else:
            over, under = add_low(over, rising), add_low(under, falling)
        return self.up(over), self.down(under)

    def scatter_end(self, parts, moving):
        return sum(part.astype(wide) for part in (parts[self.half],) + moving)

    def scatter(self, parts):
        moving = self.scatter_start(parts)
        for step in range(1, self.half):
            moving = self.scatter_step(parts, step, moving)
        return self.scatter_end(parts, moving)


def add_low(left, right):
    return (left.astype(wide) + right.astype(wide)).astype(low)


def split_rows(array, count):
    rows = array.shape[0] // count
    return [array[i * rows : (i + 1) * rows] for i in range(count)]


def gather_group(slots):
    own = jnp.concatenate(slots, axis=0)
    return [own, swap(own, "core")]


def scatter_group(ring, own, other, awaited=None):
    total = after(add_low(own, swap(other, "core")), awaited)
    return ring.scatter(split_rows(total, ring.size))


def exchange_rows(array):
    return lax.all_to_all(array, ROW, 0, 0, tiled=True)


ROW = ("zhi", "zlo")


def to_shard(blocks):
    return jnp.transpose(blocks, (1, 0, 2)).reshape(blocks.shape[1], -1)


def from_shards(arrays, seqs):
    rows, count = lax.axis_size(ROW), len(arrays)
    tokens, width = arrays[0].shape[0], arrays[0].shape[1] // rows
    stacked = jnp.concatenate(arrays, axis=0).reshape(count * tokens, rows, width)
    got = exchange_rows(jnp.transpose(stacked, (1, 0, 2)))
    return [
        got[:, i * tokens : (i + 1) * tokens].reshape(seqs, rows * tokens // seqs, width)
        for i in range(count)
    ]


def together(*arrays):
    return lax.optimization_barrier(arrays)


def after(arrays, others):
    if others is None:
        return arrays
    return lax.optimization_barrier((arrays, others))[0]


def sum_pairs(array):
    return lax.psum(array, "pair") if lax.axis_size("pair") > 1 else array


def pack_kernel(x_ref, slope, query, key, value, out, gate, up, down, head, hidden):
    weight = jnp.concatenate([query[...], key[...], value[...], out[...].T], axis=1)
    head[0] = jnp.concatenate([weight, slope[0]], axis=0)
    hidden[0] = jnp.concatenate([jnp.concatenate([gate[...], up[...]], axis=1), down[...]], axis=0)


def pack(slope, query, key, value, out, gate, up, down, line):
    rows, shard, _ = slope.shape
    depth, block = HEAD_DIM, query.shape[0]
    units = gate.shape[1] // rows // HALF
    head_at = lambda r, x: HALF * (r % line) + x[0]
    head_in = pl.BlockSpec((block, depth), lambda r, x: (0, head_at(r, x)))
    out_in = pl.BlockSpec((depth, block), lambda r, x: (head_at(r, x), 0))
    unit_in = pl.BlockSpec((block, units), lambda r, x: (0, HALF * r + x[0]))
    down_in = pl.BlockSpec((units, block), lambda r, x: (HALF * r + x[0], 0))
    slope_in = pl.BlockSpec((1, shard, block), lambda r, x: (r, 0, 0))
    shapes = [(block + shard, 4 * depth), (block + units, block)]
    return pl.pallas_call(
        pack_kernel,
        grid_spec=pltpu.PrefetchScalarGridSpec(
            num_scalar_prefetch=1,
            grid=(rows,),
            in_specs=[slope_in, head_in, head_in, head_in, out_in, unit_in, unit_in, down_in],
            out_specs=[pl.BlockSpec((1,) + shape, lambda r, x: (r, 0, 0)) for shape in shapes],
        ),
        out_shape=[jax.ShapeDtypeStruct((rows,) + shape, low) for shape in shapes],
        name="pack_weights",
    )(lax.axis_index("x")[None].astype(jnp.int32), slope, query, key, value, out, gate, up, down)


def mlp_kernel(*refs):
    tiles, weights = refs[:4], refs[4:-5]
    hidden_ref, gu_slope_ref, both_ref, rows_ref, slope_ref = refs[-5:]
    parts, height, span = weights[0].shape
    units = height - span
    rows_ref[...] = jnp.concatenate([tiles[0][...], tiles[2][...]], axis=0)
    slope_ref[...] = jnp.concatenate([tiles[1][...], tiles[3][...]], axis=0)
    cuts = [slice(k * span, (k + 1) * span) for k in range(parts)]
    totals, branches = [None] * parts, [None] * parts
    for i, weight in enumerate(weights):
        gate_up = sum(dot(rows_ref[:, cut], weight[k, :span]) for k, cut in enumerate(cuts))
        gate, up = gate_up[:, :units], gate_up[:, units:]
        sigmoid = 1.0 / (1.0 + jnp.exp(-gate))
        activated = gate * sigmoid
        hidden = (activated * up).astype(low)
        hidden_ref[:, i * units : (i + 1) * units] = hidden
        hidden_grad = sum(dot_last(slope_ref[:, cut], weight[k, span:]) for k, cut in enumerate(cuts))
        gate_slope = hidden_grad * up * sigmoid * (1.0 + gate * (1.0 - sigmoid))
        gu_slope = jnp.concatenate([gate_slope, hidden_grad * activated], axis=1).astype(low)
        gu_slope_ref[:, 2 * i * units : 2 * (i + 1) * units] = gu_slope
        for k in range(parts):
            part, branch = dot_last(gu_slope, weight[k, :span]), dot(hidden, weight[k, span:])
            totals[k] = part if i == 0 else totals[k] + part
            branches[k] = branch if i == 0 else branches[k] + branch
    tile = tiles[0].shape[0]
    for k, cut in enumerate(cuts):
        for n in range(HALF):
            tokens = slice(n * tile, (n + 1) * tile)
            both_ref[2 * n * tile : (2 * n + 1) * tile, cut] = totals[k][tokens].astype(low)
            both_ref[(2 * n + 1) * tile : 2 * (n + 1) * tile, cut] = branches[k][tokens].astype(low)


def feed_forward(both, weights, tile):
    count, width = both.shape[0] // HALF, both.shape[1]
    parts, height, span = weights[0].shape
    blocks, units = len(weights), height - span
    steps = count // (HALF * tile)
    single = lambda n: pl.BlockSpec((tile, width), lambda i: (4 * i + n, 0))
    whole = lambda array: pl.BlockSpec(array.shape, lambda i: (0, 0, 0), pipeline_mode=pl.Buffered(buffer_count=1))
    shapes = [(count, size) for size in (blocks * units, 2 * blocks * units, width, width, width)]
    shapes[2] = both.shape
    return pl.pallas_call(
        mlp_kernel,
        grid=(steps,),
        in_specs=[single(n) for n in range(4)] + [whole(weight) for weight in weights],
        out_specs=[pl.BlockSpec((shape[0] // steps, shape[1]), lambda i: (i, 0)) for shape in shapes],
        out_shape=[jax.ShapeDtypeStruct(shape, low) for shape in shapes],
        compiler_params=pltpu.CompilerParams(vmem_limit_bytes=30 * 1024 * 1024),
        cost_estimate=CHEAP,
        name="feed_forward",
    )(*[both] * 4, *weights)


def on_device(
    tokens,
    query_weight,
    key_weight,
    value_weight,
    out_weight,
    gate_weight,
    up_weight,
    down_weight,
    cotangent,
):
    depth = HEAD_DIM
    rows, line = lax.axis_size(ROW), lax.axis_size("zlo")
    small_ring = Ring(("zlo", "y"), line)
    large_ring = Ring(("zhi", "zlo", "y"), rows)
    seqs, width = tokens.shape[0], tokens.shape[2] * rows
    block = width // rows
    units = gate_weight.shape[1] // rows // HALF

    shard = seqs * tokens.shape[1] // rows
    pieces = [array.reshape(rows, shard, block) for array in (tokens, cotangent)]
    weights = (query_weight, key_weight, value_weight, out_weight, gate_weight, up_weight, down_weight)
    head_pieces, hidden_pieces = pack(pieces[1], *weights, line)
    got = exchange_rows(pieces[0])
    got, head_pieces, hidden_pieces = together(got, head_pieces, hidden_pieces)
    stream = to_shard(got).astype(wide)
    head_got = exchange_rows(head_pieces)

    place = jnp.arange(2 * small_ring.size)
    core = (lax.axis_index("core") + place // small_ring.size) % 2
    spot = (small_ring.place() + place % small_ring.size + small_ring.half) % small_ring.size
    slot_side = spot // line
    slot_level = jnp.where(slot_side == 0, spot, small_ring.size - 1 - spot)
    first = ((2 * slot_side + core) * line + slot_level) * shard
    places = (first[:, None] + jnp.arange(shard)[None, :]).reshape(-1)
    cosine, sine_table = rope_tables(places, depth)

    normed_one, inverse_one = layer_norm(stream)
    rows_slots = small_ring.gather(normed_one.astype(low))
    rows_slots, head_got, hidden_pieces = together(rows_slots, head_got, hidden_pieces)
    rows_one = gather_group(rows_slots)
    heads_weight = [head_got[:, :block].reshape(width, 4 * depth)]
    heads_weight.append(swap(heads_weight[0], "x"))
    slope_low = to_shard(head_got[:, block:])

    hidden_mine = exchange_rows(hidden_pieces)
    hidden_theirs = swap(hidden_mine, "x")
    length = HALF * rows_one[0].shape[0]
    seen = (cosine, sine_table, places[:, None], places[None, :])
    qkv_shape = jax.ShapeDtypeStruct((length, 3 * depth), low)
    kept = []
    for weight in heads_weight:
        shapes = [qkv_shape, jax.ShapeDtypeStruct((length, depth), low), jax.ShapeDtypeStruct((length, 1), wide)]
        kept.append(call_whole(attend_kernel, "attend", shapes, *rows_one, weight, *seen))
    heads = [part[1] for part in kept]
    out_parts = project("out_project", slice(3 * depth, 4 * depth), heads, heads_weight)
    middle = stream + scatter_group(small_ring, *out_parts, hidden_mine)
    normed_two, inverse_two = layer_norm(middle)
    both = jnp.concatenate([normed_two.astype(low), slope_low], axis=0)
    slots, size = [None] * large_ring.size, large_ring.half
    slots[size] = rising = falling = both
    for step in range(1, size):
        if step == size - 1:
            rising, falling, hidden_theirs = together(rising, falling, hidden_theirs)
            hidden_weight = [hidden_mine, hidden_theirs, swap(hidden_mine, "core"), swap(hidden_theirs, "core")]
            token_parts = [feed_forward(jnp.concatenate(slots[2:4], axis=0), hidden_weight, shard)]
        slots[size - step] = rising = large_ring.up(rising)
        slots[size + step] = falling = large_ring.down(falling)
    rising, falling, token_parts, hidden_weight, slots[4:6] = together(
        rising, falling, token_parts, hidden_weight, slots[4:6]
    )
    slots[size - step], slots[size + step] = rising, falling
    last = large_ring.up(rising[:shard]), large_ring.down(falling[shard:])
    token_parts.append(feed_forward(jnp.concatenate(slots[4:6], axis=0), hidden_weight, shard))
    last, token_parts, hidden_weight = together(last, token_parts, hidden_weight)
    slots[0] = jnp.concatenate(last, axis=0)
    token_parts.append(feed_forward(jnp.concatenate([*slots[6:], *slots[:2]], axis=0), hidden_weight, shard))
    hidden_low, gu_slope, both_parts, rows_two, slope_all = map(list, zip(*token_parts))

    def gu_sums(i, left):
        kernel = functools.partial(gu_sum_kernel, (i, i + 2), len(left))
        return call_blocks(kernel, "gu_sum", left, gu_slope, [(rows, block, 2 * units)] * 2)

    def down_sums(i, left):
        kernel = functools.partial(down_sum_kernel, (i, i + 2), len(left))
        return call_blocks(kernel, "down_sum", left, hidden_low, [(rows, units, block)] * 2)

    def slot_parts(first, second, third):
        third = split_rows(third, 4)
        return third[2:] + split_rows(first, 2) + split_rows(second, 2) + third[:2]

    moving = large_ring.scatter_start(slot_parts(*both_parts))
    gu_own, gu_other = gu_sums(1, rows_two)
    moving, gu_own, gu_other, rows_two, slope_all, both_parts = together(
        moving, gu_own, gu_other, rows_two, slope_all, both_parts
    )
    parts = slot_parts(*both_parts)
    moving = large_ring.scatter_step(parts, 1, moving)
    gu_other = swap(gu_other, "core")
    gu_mine, gu_mine_other = gu_sums(0, rows_two)
    down_own, down_other = down_sums(1, slope_all)
    gu_theirs = [add_low(own, other) for own, other in zip(split_rows(gu_own, HALF), split_rows(gu_other, HALF))]
    moving, gu_theirs, gu_mine, gu_mine_other, slope_all, down_own, down_other = together(
        moving, gu_theirs, gu_mine, gu_mine_other, slope_all, down_own, down_other
    )

    chunks = [swap(gu_theirs[0], "x")]
    moving = large_ring.scatter_step(parts, 2, moving)
    down_other, gu_mine_other = swap(down_other, "core"), swap(gu_mine_other, "core")
    down_mine, down_mine_other = down_sums(0, slope_all)
    down_theirs = [
        add_low(own, other) for own, other in zip(split_rows(down_own, HALF), split_rows(down_other, HALF))
    ]
    moving, chunks, gu_theirs, gu_mine, gu_mine_other, down_theirs, down_mine_other = together(
        moving, chunks, gu_theirs, gu_mine, gu_mine_other, down_theirs, down_mine_other
    )
    chunks.append(swap(gu_theirs[1], "x"))
    moving = large_ring.scatter_step(parts, 3, moving)
    down_mine_other = swap(down_mine_other, "core")
    gu_mine = add_low(gu_mine, gu_mine_other)
    moving, chunks, gu_mine, down_mine, down_mine_other, down_theirs = together(
        moving, chunks, gu_mine, down_mine, down_mine_other, down_theirs
    )
    grad_two, branch = split_rows(large_ring.scatter_end(parts, moving), HALF)
    middle_grad = slope_low.astype(wide) + norm_backward(normed_two, inverse_two, grad_two)
    output_low = (middle + branch).astype(low)

    down_chunks = [swap(down_theirs[0], "x")]
    middle_low = middle_grad.astype(low)
    slots = [None, small_ring.up(middle_low), middle_low, small_ring.down(middle_low)]
    down_mine = add_low(down_mine, down_mine_other)
    slots[1:], down_chunks, down_theirs, down_mine, chunks, gu_mine = together(
        slots[1:], down_chunks, down_theirs, down_mine, chunks, gu_mine
    )
    down_chunks.append(swap(down_theirs[1], "x"))
    cut = shard // 2
    slots[0] = jnp.concatenate([small_ring.up(slots[1][:cut]), small_ring.down(slots[3][cut:])], axis=0)
    gu_total = add_low(gu_mine, jnp.concatenate(chunks, axis=0))
    slots, down_chunks, gu_total = together(slots, down_chunks, gu_total)
    down_total = add_low(down_mine, jnp.concatenate(down_chunks, axis=0))
    unit_got = exchange_rows(sum_pairs(jnp.concatenate([gu_total, down_total], axis=1)))
    middle_all = gather_group(slots)

    def head_back(head):
        qkv, attended, logsums = kept[head]
        arrays = (*middle_all, heads_weight[head], *seen, qkv, logsums)
        (slope,) = call_whole(attend_back_kernel, "attend_back", [qkv_shape], *arrays)
        shape = (rows, block, 4 * depth)
        return slope, call_blocks(head_sum_kernel, "head_sum", rows_one + middle_all, [slope, attended], [shape])[0]

    theirs_slope, theirs_sum = head_back(1)
    middle_all, theirs_slope, theirs_sum = together(middle_all, theirs_slope, theirs_sum)
    head_chunks = [swap(theirs_sum[: rows // 2], "x")]
    mine_slope, mine_sum = head_back(0)
    back_parts = project("qkv_back", slice(0, 3 * depth), [mine_slope, theirs_slope], heads_weight)
    back_parts, mine_sum, head_chunks, theirs_sum = together(back_parts, mine_sum, head_chunks, theirs_sum)
    head_chunks.append(swap(theirs_sum[rows // 2 :], "x"))
    back_total = add_low(back_parts[0], swap(back_parts[1], "core"))
    back_total, mine_sum, head_chunks, unit_got = together(back_total, mine_sum, head_chunks, unit_got)

    head_got = exchange_rows(sum_pairs(add_low(mine_sum, jnp.concatenate(head_chunks, axis=0))))
    unit_theirs = swap(unit_got, "x")
    grad_one = small_ring.scatter(split_rows(back_total, small_ring.size))
    input_low = (middle_grad + norm_backward(normed_one, inverse_one, grad_one)).astype(low)
    head_got, unit_theirs, input_low, output_low, unit_got = together(
        head_got, unit_theirs, input_low, output_low, unit_got
    )
    head_got = head_got.reshape(rows // line, line, block, 4 * depth)
    head_mine = jnp.sum(head_got.astype(wide), axis=0).astype(low)
    head_theirs = swap(head_mine, "x")
    layer_out, input_grad = from_shards((output_low, input_low), seqs)
    gate_grad, up_grad, down_grad = assemble_units(unit_got, unit_theirs)
    layer_out, input_grad, head_mine, head_theirs = together(layer_out, input_grad, head_mine, head_theirs)
    input_grad = input_grad.astype(wide)
    query_grad, key_grad, value_grad, out_grad = assemble(head_mine, head_theirs)

    return (
        layer_out,
        input_grad,
        query_grad,
        key_grad,
        value_grad,
        out_grad,
        gate_grad,
        up_grad,
        down_grad,
    )


def solution(mesh):
    dp, rows, cols = (mesh.shape[name] for name in ("dp", "row", "col"))
    sizes = (dp // HALF, HALF, HALF, rows // HALF, cols // HALF, HALF)
    fine = Mesh(mesh.devices.reshape(sizes), ("pair", "x", "zhi", "zlo", "y", "core"))
    across, inner, tall = ("pair", "x"), ("y", "core"), ROW
    split = P(across, inner, tall)
    inward = P(tall, inner)
    outward = P(inner, tall)
    return jax.shard_map(
        on_device,
        mesh=fine,
        in_specs=(split, inward, inward, inward, outward, inward, inward, outward, split),
        out_specs=(split, split, inward, inward, inward, outward, inward, inward, outward),
        check_vma=False,
    )
```

```python
import functools

import jax
import jax.numpy as jnp
from jax import lax
from jax.experimental import pallas as pl
from jax.experimental.pallas import tpu as pltpu
from jax.sharding import Mesh
from jax.sharding import PartitionSpec as P

HEAD_DIM = 128
BLOCK = 512
HALF = 2

epsilon = 1e-05
rope_base = 10000.0
masked_score = -1e30
low = jnp.bfloat16
CHEAP = pl.CostEstimate(flops=1, transcendentals=0, bytes_accessed=1)
wide = jnp.float32


def rope_tables(places, head_depth):
    halfway = head_depth // 2
    position = places.astype(jnp.float32)[:, None]
    frequency = rope_base ** (-(2.0 * jnp.arange(halfway).astype(jnp.float32)) / head_depth)
    angles = position * frequency[None, :]
    cosine = jnp.concatenate([jnp.cos(angles), jnp.cos(angles)], axis=1)
    sine_table = jnp.concatenate([jnp.sin(angles), jnp.sin(angles)], axis=1)
    return (cosine, sine_table)


def dot(left, right):
    return jnp.dot(left, right, preferred_element_type=wide)


def layer_norm(stream):
    average = jnp.mean(stream, axis=1, keepdims=True)
    centered = stream - average
    inverse = lax.rsqrt(jnp.mean(centered * centered, axis=1, keepdims=True) + epsilon)
    return centered * inverse, inverse


def norm_backward(normed, inverse, gradient):
    average = jnp.mean(gradient, axis=1, keepdims=True)
    crossed = jnp.mean(gradient * normed, axis=1, keepdims=True)
    return inverse * (gradient - average - normed * crossed)


def turn(array):
    return pltpu.roll(array, array.shape[1] // 2, 1)


def rope_sign(depth):
    return jnp.where(lax.broadcasted_iota(jnp.int32, (1, depth), 1) < depth // 2, -1.0, 1.0)


def attend_kernel(own_ref, other_ref, weight_ref, cosine_ref, sine_ref, column_ref, line_ref, qkv_ref, heads_ref, logsum_ref):
    depth = heads_ref.shape[1]
    weight = weight_ref[:, : 3 * depth]
    qkv = jnp.concatenate([dot(own_ref[...], weight), dot(other_ref[...], weight)], axis=0)
    cosine, sine = cosine_ref[...], sine_ref[...] * rope_sign(depth)
    rope = lambda w: (w * cosine + turn(w) * sine).astype(low)
    queries, key_rows = rope(qkv[:, :depth]), rope(qkv[:, depth : 2 * depth])
    values = qkv[:, 2 * depth :].astype(low)
    qkv_ref[...] = jnp.concatenate([queries, key_rows, values], axis=1)
    for at in range(0, queries.shape[0], BLOCK):
        part = slice(at, at + BLOCK)
        scores = dot_last(queries[part], key_rows) * depth**-0.5
        scores = jnp.where(column_ref[part] >= line_ref[...], scores, masked_score)
        highest = jnp.max(scores, axis=1, keepdims=True)
        shifted = jnp.exp(scores - highest)
        totals = jnp.sum(shifted, axis=1, keepdims=True)
        logsum_ref[part] = highest + jnp.log(totals)
        weights = (shifted * (1.0 / totals)).astype(low)
        heads_ref[part] = dot(weights, values).astype(low)


def attend_back_kernel(
    own_ref, other_ref, weight_ref, cosine_ref, sine_ref, column_ref, line_ref, qkv_ref, logsum_ref, slope_ref
):
    depth = cosine_ref.shape[1]
    scaling = depth**-0.5
    queries, key_rows, values = (qkv_ref[:, i * depth : (i + 1) * depth] for i in range(3))
    weight = weight_ref[:, 3 * depth :]
    head_grad = jnp.concatenate([dot(own_ref[...], weight), dot(other_ref[...], weight)], axis=0).astype(low)
    query_parts = []
    key_grad = value_grad = None
    for at in range(0, queries.shape[0], BLOCK):
        part = slice(at, at + BLOCK)
        scores = dot_last(queries[part], key_rows) * scaling
        scores = jnp.where(column_ref[part] >= line_ref[...], scores, masked_score)
        probable = jnp.exp(scores - logsum_ref[part])
        product = dot_last(head_grad[part], values)
        slopes = probable * (product - jnp.sum(probable * product, axis=1, keepdims=True))
        slopes = slopes.astype(low)
        query_parts.append(dot(slopes, key_rows) * scaling)
        key_part = dot_first(slopes, queries[part]) * scaling
        value_part = dot_first(probable.astype(low), head_grad[part])
        key_grad = key_part if at == 0 else key_grad + key_part
        value_grad = value_part if at == 0 else value_grad + value_part
    cosine, sine = cosine_ref[...], sine_ref[...]
    undo = lambda g: (g * cosine - turn(g * sine) * rope_sign(depth)).astype(low)
    slope_ref[:, :depth] = undo(jnp.concatenate(query_parts, axis=0))
    slope_ref[:, depth : 2 * depth] = undo(key_grad)
    slope_ref[:, 2 * depth :] = value_grad.astype(low)


def project_kernel(columns, *refs):
    lefts, weights = refs[: len(refs) // 2 - 1], refs[len(refs) // 2 - 1 : -2]
    part = sum(dot_last(left[...], weight[:, columns]) for left, weight in zip(lefts, weights)).astype(low)
    first = 2 * pl.program_id(0) < pl.num_programs(0)

    @pl.when(first)
    def _():
        refs[-2][...] = part

    @pl.when(jnp.logical_not(first))
    def _():
        refs[-1][...] = part


def project(name, columns, lefts, weights, tile=256):
    count, width = lefts[0].shape[0], weights[0].shape[0]
    last = count // tile // HALF - 1
    whole = lambda array: pl.BlockSpec(array.shape, lambda i: (0, 0), pipeline_mode=pl.Buffered(buffer_count=1))
    return pl.pallas_call(
        functools.partial(project_kernel, columns),
        grid=(count // tile,),
        in_specs=[pl.BlockSpec((tile, left.shape[1]), lambda i: (i, 0)) for left in lefts]
        + [whole(weight) for weight in weights],
        out_specs=[
            pl.BlockSpec((tile, width), lambda i: (jnp.minimum(i, last), 0)),
            pl.BlockSpec((tile, width), lambda i: (jnp.maximum(i - last - 1, 0), 0)),
        ],
        out_shape=[jax.ShapeDtypeStruct((count // HALF, width), low)] * HALF,
        compiler_params=pltpu.CompilerParams(vmem_limit_bytes=12 * 1024 * 1024),
        cost_estimate=CHEAP,
        name=name,
    )(*lefts, *weights)


def head_sum_kernel(rows_own, rows_other, middle_own, middle_other, slope_ref, attended_ref, out_ref):
    half = rows_own.shape[0]

    def product(own, other, right):
        return dot_first(own[...], right[:half]) + dot_first(other[...], right[half:])

    parts = [product(rows_own, rows_other, slope_ref), product(middle_own, middle_other, attended_ref)]
    out_ref[0] = jnp.concatenate(parts, axis=1).astype(low)


def gu_sum_kernel(blocks, *refs):
    parts = len(blocks)
    rows, slopes, out_refs = refs[:parts], refs[parts : 2 * parts], refs[2 * parts :]
    rows = [part[...] for part in rows]
    for n, out_ref in enumerate(out_refs):
        size = out_ref.shape[2]
        cuts = [slice(own[n] * size, (own[n] + 1) * size) for own in blocks]
        out_ref[0] = sum(dot_first(left, right[:, cut]) for left, right, cut in zip(rows, slopes, cuts)).astype(low)


def down_sum_kernel(blocks, *refs):
    parts = len(blocks)
    slopes, hiddens, out_refs = refs[:parts], refs[parts : 2 * parts], refs[2 * parts :]
    slopes = [part[...] for part in slopes]
    for n, out_ref in enumerate(out_refs):
        units = out_ref.shape[1]
        cuts = [slice(own[n] * units, (own[n] + 1) * units) for own in blocks]
        out_ref[0] = sum(dot_first(left[:, cut], right) for left, right, cut in zip(hiddens, slopes, cuts)).astype(low)


def call_blocks(kernel, name, cut, held, shapes):
    count = shapes[0][0]
    return pl.pallas_call(
        kernel,
        grid=(count,),
        in_specs=[pl.BlockSpec((array.shape[0], array.shape[1] // count), lambda i: (0, i)) for array in cut]
        + [pl.BlockSpec(array.shape, lambda i: (0, 0)) for array in held],
        out_specs=[pl.BlockSpec((1,) + shape[1:], lambda i: (i, 0, 0)) for shape in shapes],
        out_shape=[jax.ShapeDtypeStruct(shape, low) for shape in shapes],
        compiler_params=pltpu.CompilerParams(vmem_limit_bytes=12 * 1024 * 1024),
        cost_estimate=CHEAP,
        name=name,
    )(*cut, *held)


def assemble_kernel(x_ref, mine_ref, theirs_ref, query_ref, key_ref, value_ref, out_ref):
    line, block, depth = mine_ref.shape[0], mine_ref.shape[1], HEAD_DIM
    for i in range(line):
        for source, turned in ((mine_ref, x_ref[0]), (theirs_ref, 1 - x_ref[0])):
            place = pl.ds(pl.multiple_of((HALF * i + turned) * depth, depth), depth)
            for n, target in enumerate((query_ref, key_ref, value_ref)):
                target[:, place] = source[i, :, n * depth : (n + 1) * depth].astype(wide)
            out_ref[place, :] = source[i, :, 3 * depth :].astype(wide).T


def assemble(mine, theirs):
    line, block, _ = mine.shape
    shape = jax.ShapeDtypeStruct((block, block), wide)
    whole = pl.BlockSpec(memory_space=pltpu.VMEM)
    return pl.pallas_call(
        assemble_kernel,
        in_specs=[pl.BlockSpec(memory_space=pltpu.SMEM), whole, whole],
        out_specs=[whole] * 4,
        out_shape=[shape] * 4,
        cost_estimate=CHEAP,
        name="assemble",
    )(lax.axis_index("x")[None].astype(jnp.int32), mine, theirs)


def assemble_units_kernel(x_ref, mine_ref, theirs_ref, gate_ref, up_ref, down_ref):
    size, units = gate_ref.shape[0], down_ref.shape[0] // HALF
    mine, theirs = mine_ref[0].astype(wide), theirs_ref[0].astype(wide)
    first = jnp.where(x_ref[0] == 0, mine, theirs)
    second = jnp.where(x_ref[0] == 0, theirs, mine)
    gate_ref[...] = jnp.concatenate([first[:size, :units], second[:size, :units]], axis=1)
    up_ref[...] = jnp.concatenate([first[:size, units:], second[:size, units:]], axis=1)
    down_ref[...] = jnp.concatenate([first[size:], second[size:]], axis=0)


def assemble_units(mine, theirs):
    rows, height, size = mine.shape
    share = HALF * (height - size)
    arrived = pl.BlockSpec((1, height, size), lambda i, x: (i, 0, 0))
    columns = pl.BlockSpec((size, share), lambda i, x: (0, i))
    wide_shape = jax.ShapeDtypeStruct((size, rows * share), wide)
    return pl.pallas_call(
        assemble_units_kernel,
        grid_spec=pltpu.PrefetchScalarGridSpec(
            num_scalar_prefetch=1,
            grid=(rows,),
            in_specs=[arrived, arrived],
            out_specs=[columns, columns, pl.BlockSpec((share, size), lambda i, x: (i, 0))],
        ),
        out_shape=[wide_shape, wide_shape, jax.ShapeDtypeStruct((rows * share, size), wide)],
        compiler_params=pltpu.CompilerParams(vmem_limit_bytes=10 * 1024 * 1024),
        cost_estimate=CHEAP,
        name="assemble_units",
    )(lax.axis_index("x")[None].astype(jnp.int32), mine, theirs)


def call_whole(kernel, name, shapes, *arrays):
    whole = pl.BlockSpec(memory_space=pltpu.VMEM)
    return pl.pallas_call(
        kernel,
        in_specs=[whole] * len(arrays),
        out_specs=[whole] * len(shapes),
        out_shape=shapes,
        compiler_params=pltpu.CompilerParams(vmem_limit_bytes=18 * 1024 * 1024),
        cost_estimate=CHEAP,
        name=name,
    )(*arrays)


def dot_last(left, right):
    return lax.dot_general(left, right, (((1,), (1,)), ((), ())), preferred_element_type=wide)


def dot_first(left, right):
    return lax.dot_general(left, right, (((0,), (0,)), ((), ())), preferred_element_type=wide)


def swap(array, axis):
    return lax.ppermute(array, axis, [(0, 1), (1, 0)])


class Ring:
    def __init__(self, axes, line):
        self.axes = axes
        self.size = 2 * line
        self.half = line
        flat = [2 * n if n < line else 2 * (2 * line - 1 - n) + 1 for n in range(self.size)]
        self.upward = [(flat[i], flat[(i + 1) % self.size]) for i in range(self.size)]
        self.downward = [(b, a) for a, b in self.upward]

    def up(self, array):
        return lax.ppermute(array, self.axes, self.upward)

    def down(self, array):
        return lax.ppermute(array, self.axes, self.downward)

    def place(self):
        level, side = lax.axis_index(self.axes[:-1]), lax.axis_index(self.axes[-1])
        return jnp.where(side == 0, level, self.size - 1 - level)

    def gather(self, shard, waits={}):
        half, cut = self.half, shard.shape[0] // 2
        slots = [None] * self.size
        slots[half] = rising = falling = shard
        for step in range(1, half + 1):
            rising, falling = after((rising, falling), waits.get(step))
            if step == half:
                break
            slots[half - step] = rising = self.up(rising)
            slots[half + step] = falling = self.down(falling)
        slots[0] = jnp.concatenate([self.up(rising[:cut]), self.down(falling[cut:])], axis=0)
        return slots

    def scatter_start(self, parts):
        cut = parts[0].shape[0] // 2
        return self.up(parts[0][:cut]), self.down(parts[0][cut:])

    def scatter_step(self, parts, step, moving):
        rising, falling = moving
        cut = rising.shape[0]
        over, under = parts[self.size - step], parts[step]
        if step == 1:
            over = jnp.concatenate([add_low(over[:cut], rising), over[cut:]], axis=0)
            under = jnp.concatenate([under[:cut], add_low(under[cut:], falling)], axis=0)
        else:
            over, under = add_low(over, rising), add_low(under, falling)
        return self.up(over), self.down(under)

    def scatter_end(self, parts, moving):
        return sum(part.astype(wide) for part in (parts[self.half],) + moving)

    def scatter(self, parts):
        moving = self.scatter_start(parts)
        for step in range(1, self.half):
            moving = self.scatter_step(parts, step, moving)
        return self.scatter_end(parts, moving)


def add_low(left, right):
    return (left.astype(wide) + right.astype(wide)).astype(low)


def split_rows(array, count):
    rows = array.shape[0] // count
    return [array[i * rows : (i + 1) * rows] for i in range(count)]


def gather_group(slots):
    own = jnp.concatenate(slots, axis=0)
    return [own, swap(own, "core")]


def scatter_group(ring, own, other, awaited=None):
    total = after(add_low(own, swap(other, "core")), awaited)
    return ring.scatter(split_rows(total, ring.size))


def exchange_rows(array):
    return lax.all_to_all(array, ROW, 0, 0, tiled=True)


ROW = ("zhi", "zlo")


def to_shard(blocks):
    return jnp.transpose(blocks, (1, 0, 2)).reshape(blocks.shape[1], -1)


def from_shards(arrays, seqs):
    rows, count = lax.axis_size(ROW), len(arrays)
    tokens, width = arrays[0].shape[0], arrays[0].shape[1] // rows
    stacked = jnp.concatenate(arrays, axis=0).reshape(count * tokens, rows, width)
    got = exchange_rows(jnp.transpose(stacked, (1, 0, 2)))
    return [
        got[:, i * tokens : (i + 1) * tokens].reshape(seqs, rows * tokens // seqs, width)
        for i in range(count)
    ]


def together(*arrays):
    return lax.optimization_barrier(arrays)


def after(arrays, others):
    if others is None:
        return arrays
    return lax.optimization_barrier((arrays, others))[0]


def sum_pairs(array):
    return lax.psum(array, "pair") if lax.axis_size("pair") > 1 else array


def pack_kernel(x_ref, slope, query, key, value, out, gate, up, down, head, hidden):
    weight = jnp.concatenate([query[...], key[...], value[...], out[...].T], axis=1)
    head[0] = jnp.concatenate([weight, slope[0]], axis=0)
    hidden[0] = jnp.concatenate([jnp.concatenate([gate[...], up[...]], axis=1), down[...]], axis=0)


def pack(slope, query, key, value, out, gate, up, down, line):
    rows, shard, _ = slope.shape
    depth, block = HEAD_DIM, query.shape[0]
    units = gate.shape[1] // rows // HALF
    head_at = lambda r, x: HALF * (r % line) + x[0]
    head_in = pl.BlockSpec((block, depth), lambda r, x: (0, head_at(r, x)))
    out_in = pl.BlockSpec((depth, block), lambda r, x: (head_at(r, x), 0))
    unit_in = pl.BlockSpec((block, units), lambda r, x: (0, HALF * r + x[0]))
    down_in = pl.BlockSpec((units, block), lambda r, x: (HALF * r + x[0], 0))
    slope_in = pl.BlockSpec((1, shard, block), lambda r, x: (r, 0, 0))
    shapes = [(block + shard, 4 * depth), (block + units, block)]
    return pl.pallas_call(
        pack_kernel,
        grid_spec=pltpu.PrefetchScalarGridSpec(
            num_scalar_prefetch=1,
            grid=(rows,),
            in_specs=[slope_in, head_in, head_in, head_in, out_in, unit_in, unit_in, down_in],
            out_specs=[pl.BlockSpec((1,) + shape, lambda r, x: (r, 0, 0)) for shape in shapes],
        ),
        out_shape=[jax.ShapeDtypeStruct((rows,) + shape, low) for shape in shapes],
        name="pack_weights",
    )(lax.axis_index("x")[None].astype(jnp.int32), slope, query, key, value, out, gate, up, down)


def mlp_kernel(blocks, *refs):
    tiles, weights, rest = refs[:4], refs[4 : 4 + blocks], refs[4 + blocks :]
    earlier = rest[0] if len(rest) > 5 else None
    hidden_ref, gu_slope_ref, both_ref, rows_ref, slope_ref = rest[-5:]
    parts, height, span = weights[0].shape
    units = height - span
    rows_ref[...] = jnp.concatenate([tiles[0][...], tiles[2][...]], axis=0)
    slope_ref[...] = jnp.concatenate([tiles[1][...], tiles[3][...]], axis=0)
    cuts = [slice(k * span, (k + 1) * span) for k in range(parts)]
    totals, branches = [None] * parts, [None] * parts
    for i, weight in enumerate(weights):
        gate_up = sum(dot(rows_ref[:, cut], weight[k, :span]) for k, cut in enumerate(cuts))
        gate, up = gate_up[:, :units], gate_up[:, units:]
        sigmoid = 1.0 / (1.0 + jnp.exp(-gate))
        activated = gate * sigmoid
        hidden = (activated * up).astype(low)
        hidden_ref[:, i * units : (i + 1) * units] = hidden
        hidden_grad = sum(dot_last(slope_ref[:, cut], weight[k, span:]) for k, cut in enumerate(cuts))
        gate_slope = hidden_grad * up * sigmoid * (1.0 + gate * (1.0 - sigmoid))
        gu_slope = jnp.concatenate([gate_slope, hidden_grad * activated], axis=1).astype(low)
        gu_slope_ref[:, 2 * i * units : 2 * (i + 1) * units] = gu_slope
        for k in range(parts):
            part, branch = dot_last(gu_slope, weight[k, :span]), dot(hidden, weight[k, span:])
            totals[k] = part if i == 0 else totals[k] + part
            branches[k] = branch if i == 0 else branches[k] + branch
    tile = tiles[0].shape[0]
    for k, cut in enumerate(cuts):
        for n in range(2 * HALF):
            place = slice(n * tile, (n + 1) * tile)
            total = (branches if n % 2 else totals)[k][n // 2 * tile : (n // 2 + 1) * tile]
            if earlier is not None:
                total = total + earlier[place, cut].astype(wide)
            both_ref[place, cut] = total.astype(low)


def feed_forward(both, weights, tile, earlier=()):
    count, width = both.shape[0] // HALF, both.shape[1]
    parts, height, span = weights[0].shape
    blocks, units = len(weights), height - span
    steps = count // (HALF * tile)
    single = lambda n: pl.BlockSpec((tile, width), lambda i: (4 * i + n, 0))
    whole = lambda array: pl.BlockSpec(array.shape, lambda i: (0, 0, 0), pipeline_mode=pl.Buffered(buffer_count=1))
    shapes = [(count, size) for size in (blocks * units, 2 * blocks * units, width, width, width)]
    shapes[2] = both.shape
    return pl.pallas_call(
        functools.partial(mlp_kernel, blocks),
        grid=(steps,),
        in_specs=[single(n) for n in range(4)]
        + [whole(weight) for weight in weights]
        + [pl.BlockSpec((array.shape[0] // steps, width), lambda i: (i, 0)) for array in earlier],
        out_specs=[pl.BlockSpec((shape[0] // steps, shape[1]), lambda i: (i, 0)) for shape in shapes],
        out_shape=[jax.ShapeDtypeStruct(shape, low) for shape in shapes],
        compiler_params=pltpu.CompilerParams(vmem_limit_bytes=30 * 1024 * 1024),
        cost_estimate=CHEAP,
        name="feed_forward",
    )(*[both] * 4, *weights, *earlier)


def on_device(
    tokens,
    query_weight,
    key_weight,
    value_weight,
    out_weight,
    gate_weight,
    up_weight,
    down_weight,
    cotangent,
):
    depth = HEAD_DIM
    rows, line = lax.axis_size(ROW), lax.axis_size("zlo")
    small_ring = Ring(("zlo", "y"), line)
    large_ring = Ring(("zhi", "zlo", "y"), rows)
    seqs, width = tokens.shape[0], tokens.shape[2] * rows
    block = width // rows
    units = gate_weight.shape[1] // rows // HALF

    shard = seqs * tokens.shape[1] // rows
    pieces = [array.reshape(rows, shard, block) for array in (tokens, cotangent)]
    weights = (query_weight, key_weight, value_weight, out_weight, gate_weight, up_weight, down_weight)
    head_pieces, hidden_pieces = pack(pieces[1], *weights, line)
    got = exchange_rows(pieces[0])
    got, head_pieces, hidden_pieces = together(got, head_pieces, hidden_pieces)
    stream = to_shard(got).astype(wide)
    head_got = exchange_rows(head_pieces)

    place = jnp.arange(2 * small_ring.size)
    core = (lax.axis_index("core") + place // small_ring.size) % 2
    spot = (small_ring.place() + place % small_ring.size + small_ring.half) % small_ring.size
    slot_side = spot // line
    slot_level = jnp.where(slot_side == 0, spot, small_ring.size - 1 - spot)
    first = ((2 * slot_side + core) * line + slot_level) * shard
    places = (first[:, None] + jnp.arange(shard)[None, :]).reshape(-1)
    cosine, sine_table = rope_tables(places, depth)

    normed_one, inverse_one = layer_norm(stream)
    rows_slots = small_ring.gather(normed_one.astype(low))
    rows_slots, head_got, hidden_pieces = together(rows_slots, head_got, hidden_pieces)
    rows_one = gather_group(rows_slots)
    heads_weight = [head_got[:, :block].reshape(width, 4 * depth)]
    heads_weight.append(swap(heads_weight[0], "x"))
    slope_low = to_shard(head_got[:, block:])

    hidden_mine = exchange_rows(hidden_pieces)
    hidden_theirs = swap(hidden_mine, "x")
    length = HALF * rows_one[0].shape[0]
    seen = (cosine, sine_table, places[:, None], places[None, :])
    qkv_shape = jax.ShapeDtypeStruct((length, 3 * depth), low)
    kept = []
    for weight in heads_weight:
        shapes = [qkv_shape, jax.ShapeDtypeStruct((length, depth), low), jax.ShapeDtypeStruct((length, 1), wide)]
        kept.append(call_whole(attend_kernel, "attend", shapes, *rows_one, weight, *seen))
    heads = [part[1] for part in kept]
    out_parts = project("out_project", slice(3 * depth, 4 * depth), heads, heads_weight)
    middle = stream + scatter_group(small_ring, *out_parts, hidden_mine)
    normed_two, inverse_two = layer_norm(middle)
    both = jnp.concatenate([normed_two.astype(low), slope_low], axis=0)
    slots, size = [None] * large_ring.size, large_ring.half
    slots[size] = rising = falling = both
    hidden_mine = [hidden_mine, swap(hidden_mine, "core")]
    for step in range(1, size):
        slots[size - step] = rising = large_ring.up(rising)
        slots[size + step] = falling = large_ring.down(falling)
        if step < size - 1:
            rising, falling, hidden_mine = together(rising, falling, hidden_mine)
            slots[size - step], slots[size + step] = rising, falling
    inner = jnp.concatenate(slots[2:6], axis=0)
    inner_mine = feed_forward(inner, hidden_mine, shard)
    rising, falling, inner_mine, inner, hidden_theirs = together(rising, falling, inner_mine, inner, hidden_theirs)
    slots[size - step], slots[size + step] = rising, falling
    last = large_ring.up(rising[:shard]), large_ring.down(falling[shard:])
    hidden_theirs = [hidden_theirs, swap(hidden_theirs, "core")]
    inner_theirs = feed_forward(inner, hidden_theirs, shard, inner_mine[2:3])
    last, inner_theirs, hidden_mine, hidden_theirs = together(last, inner_theirs, hidden_mine, hidden_theirs)
    slots[0] = jnp.concatenate(last, axis=0)
    outer = feed_forward(jnp.concatenate([*slots[6:], *slots[:2]], axis=0), hidden_mine + hidden_theirs, shard)
    both_parts, rows_two, slope_all = [inner_theirs[2], outer[2]], [inner_mine[3], outer[3]], [inner_mine[4], outer[4]]

    def gu_sums(inner_part, outer_at, left):
        kernel = functools.partial(gu_sum_kernel, ((0, 1), (outer_at, outer_at + 1)))
        return call_blocks(kernel, "gu_sum", left, [inner_part[1], outer[1]], [(rows, block, 2 * units)] * 2)

    def down_sums(inner_part, outer_at, left):
        kernel = functools.partial(down_sum_kernel, ((0, 1), (outer_at, outer_at + 1)))
        return call_blocks(kernel, "down_sum", left, [inner_part[0], outer[0]], [(rows, units, block)] * 2)

    def slot_parts(inner, outer):
        outer = split_rows(outer, 4)
        return outer[2:] + split_rows(inner, 4) + outer[:2]

    moving = large_ring.scatter_start(slot_parts(*both_parts))
    gu_own, gu_other = gu_sums(inner_theirs, HALF, rows_two)
    moving, gu_own, gu_other, rows_two, slope_all, both_parts = together(
        moving, gu_own, gu_other, rows_two, slope_all, both_parts
    )
    parts = slot_parts(*both_parts)
    gu_other = swap(gu_other, "core")
    gu_theirs = [add_low(own, other) for own, other in zip(split_rows(gu_own, HALF), split_rows(gu_other, HALF))]
    moving, gu_theirs, rows_two, slope_all = together(moving, gu_theirs, rows_two, slope_all)

    chunks = [swap(gu_theirs[0], "x")]
    moving = large_ring.scatter_step(parts, 1, moving)
    gu_mine, gu_mine_other = gu_sums(inner_mine, 0, rows_two)
    down_own, down_other = down_sums(inner_theirs, HALF, slope_all)
    moving, chunks, gu_theirs, gu_mine, gu_mine_other, slope_all, down_own, down_other = together(
        moving, chunks, gu_theirs, gu_mine, gu_mine_other, slope_all, down_own, down_other
    )
    chunks.append(swap(gu_theirs[1], "x"))
    moving = large_ring.scatter_step(parts, 2, moving)
    down_other = swap(down_other, "core")
    down_mine, down_mine_other = down_sums(inner_mine, 0, slope_all)
    down_theirs = add_low(down_own, down_other)
    gu_mine_other = swap(gu_mine_other, "core")
    moving, chunks, gu_mine, gu_mine_other, down_theirs, down_mine, down_mine_other = together(
        moving, chunks, gu_mine, gu_mine_other, down_theirs, down_mine, down_mine_other
    )
    down_theirs = swap(down_theirs, "x")
    moving = large_ring.scatter_step(parts, 3, moving)
    down_mine = add_low(down_mine, swap(down_mine_other, "core"))
    gu_total = add_low(add_low(gu_mine, gu_mine_other), jnp.concatenate(chunks, axis=0))
    moving, gu_total, down_mine, down_theirs = together(moving, gu_total, down_mine, down_theirs)
    grad_two, branch = split_rows(large_ring.scatter_end(parts, moving), HALF)
    middle_grad = slope_low.astype(wide) + norm_backward(normed_two, inverse_two, grad_two)
    output_low = (middle + branch).astype(low)

    slots = small_ring.gather(middle_grad.astype(low))
    unit_total = jnp.concatenate([gu_total, add_low(down_mine, down_theirs)], axis=1)
    slots, unit_total = together(slots, unit_total)
    unit_got = exchange_rows(sum_pairs(unit_total))
    middle_all = gather_group(slots)

    def head_back(head):
        qkv, attended, logsums = kept[head]
        arrays = (*middle_all, heads_weight[head], *seen, qkv, logsums)
        (slope,) = call_whole(attend_back_kernel, "attend_back", [qkv_shape], *arrays)
        shape = (rows, block, 4 * depth)
        return slope, call_blocks(head_sum_kernel, "head_sum", rows_one + middle_all, [slope, attended], [shape])[0]

    theirs_slope, theirs_sum = head_back(1)
    middle_all, theirs_slope, theirs_sum = together(middle_all, theirs_slope, theirs_sum)
    head_chunks = [swap(theirs_sum[: rows // 2], "x")]
    mine_slope, mine_sum = head_back(0)
    back_parts = project("qkv_back", slice(0, 3 * depth), [mine_slope, theirs_slope], heads_weight)
    back_parts, mine_sum, head_chunks, theirs_sum = together(back_parts, mine_sum, head_chunks, theirs_sum)
    head_chunks.append(swap(theirs_sum[rows // 2 :], "x"))
    back_total = add_low(back_parts[0], swap(back_parts[1], "core"))
    back_total, mine_sum, head_chunks, unit_got = together(back_total, mine_sum, head_chunks, unit_got)

    head_got = exchange_rows(sum_pairs(add_low(mine_sum, jnp.concatenate(head_chunks, axis=0))))
    unit_theirs = swap(unit_got, "x")
    grad_one = small_ring.scatter(split_rows(back_total, small_ring.size))
    input_low = (middle_grad + norm_backward(normed_one, inverse_one, grad_one)).astype(low)
    head_got, unit_theirs, input_low, output_low, unit_got = together(
        head_got, unit_theirs, input_low, output_low, unit_got
    )
    head_got = head_got.reshape(rows // line, line, block, 4 * depth)
    head_mine = jnp.sum(head_got.astype(wide), axis=0).astype(low)
    head_theirs = swap(head_mine, "x")
    layer_out, input_grad = from_shards((output_low, input_low), seqs)
    gate_grad, up_grad, down_grad = assemble_units(unit_got, unit_theirs)
    layer_out, input_grad, head_mine, head_theirs = together(layer_out, input_grad, head_mine, head_theirs)
    input_grad = input_grad.astype(wide)
    query_grad, key_grad, value_grad, out_grad = assemble(head_mine, head_theirs)

    return (
        layer_out,
        input_grad,
        query_grad,
        key_grad,
        value_grad,
        out_grad,
        gate_grad,
        up_grad,
        down_grad,
    )


def solution(mesh):
    dp, rows, cols = (mesh.shape[name] for name in ("dp", "row", "col"))
    sizes = (dp // HALF, HALF, HALF, rows // HALF, cols // HALF, HALF)
    fine = Mesh(mesh.devices.reshape(sizes), ("pair", "x", "zhi", "zlo", "y", "core"))
    across, inner, tall = ("pair", "x"), ("y", "core"), ROW
    split = P(across, inner, tall)
    inward = P(tall, inner)
    outward = P(inner, tall)
    return jax.shard_map(
        on_device,
        mesh=fine,
        in_specs=(split, inward, inward, inward, outward, inward, inward, outward, split),
        out_specs=(split, split, inward, inward, inward, outward, inward, inward, outward),
        check_vma=False,
    )
```

```python
import functools

import jax
import jax.numpy as jnp
from jax import lax
from jax.experimental import pallas as pl
from jax.experimental.pallas import tpu as pltpu
from jax.sharding import Mesh
from jax.sharding import PartitionSpec as P

HEAD_DIM = 128
BLOCK = 512
HALF = 2

epsilon = 1e-05
rope_base = 10000.0
masked_score = -1e30
low = jnp.bfloat16
CHEAP = pl.CostEstimate(flops=1, transcendentals=0, bytes_accessed=1)
wide = jnp.float32


def rope_tables(places, head_depth):
    halfway = head_depth // 2
    position = places.astype(jnp.float32)[:, None]
    frequency = rope_base ** (-(2.0 * jnp.arange(halfway).astype(jnp.float32)) / head_depth)
    angles = position * frequency[None, :]
    cosine = jnp.concatenate([jnp.cos(angles), jnp.cos(angles)], axis=1)
    sine_table = jnp.concatenate([jnp.sin(angles), jnp.sin(angles)], axis=1)
    return (cosine, sine_table)


def dot(left, right):
    return jnp.dot(left, right, preferred_element_type=wide)


def layer_norm(stream):
    average = jnp.mean(stream, axis=1, keepdims=True)
    centered = stream - average
    inverse = lax.rsqrt(jnp.mean(centered * centered, axis=1, keepdims=True) + epsilon)
    return centered * inverse, inverse


def norm_backward(normed, inverse, gradient):
    average = jnp.mean(gradient, axis=1, keepdims=True)
    crossed = jnp.mean(gradient * normed, axis=1, keepdims=True)
    return inverse * (gradient - average - normed * crossed)


def turn(array):
    return pltpu.roll(array, array.shape[1] // 2, 1)


def rope_sign(depth):
    return jnp.where(lax.broadcasted_iota(jnp.int32, (1, depth), 1) < depth // 2, -1.0, 1.0)


def attend_kernel(own_ref, other_ref, weight_ref, cosine_ref, sine_ref, column_ref, line_ref, qkv_ref, heads_ref, logsum_ref):
    depth = heads_ref.shape[1]
    weight = weight_ref[:, : 3 * depth]
    qkv = jnp.concatenate([dot(own_ref[...], weight), dot(other_ref[...], weight)], axis=0)
    cosine, sine = cosine_ref[...], sine_ref[...] * rope_sign(depth)
    rope = lambda w: (w * cosine + turn(w) * sine).astype(low)
    queries, key_rows = rope(qkv[:, :depth]), rope(qkv[:, depth : 2 * depth])
    values = qkv[:, 2 * depth :].astype(low)
    qkv_ref[...] = jnp.concatenate([queries, key_rows, values], axis=1)
    for at in range(0, queries.shape[0], BLOCK):
        part = slice(at, at + BLOCK)
        scores = dot_last(queries[part], key_rows) * depth**-0.5
        scores = jnp.where(column_ref[part] >= line_ref[...], scores, masked_score)
        highest = jnp.max(scores, axis=1, keepdims=True)
        shifted = jnp.exp(scores - highest)
        totals = jnp.sum(shifted, axis=1, keepdims=True)
        logsum_ref[part] = highest + jnp.log(totals)
        weights = (shifted * (1.0 / totals)).astype(low)
        heads_ref[part] = dot(weights, values).astype(low)


def attend_back_kernel(
    own_ref, other_ref, weight_ref, cosine_ref, sine_ref, column_ref, line_ref, qkv_ref, logsum_ref, slope_ref
):
    depth = cosine_ref.shape[1]
    scaling = depth**-0.5
    queries, key_rows, values = (qkv_ref[:, i * depth : (i + 1) * depth] for i in range(3))
    weight = weight_ref[:, 3 * depth :]
    head_grad = jnp.concatenate([dot(own_ref[...], weight), dot(other_ref[...], weight)], axis=0).astype(low)
    query_parts = []
    key_grad = value_grad = None
    for at in range(0, queries.shape[0], BLOCK):
        part = slice(at, at + BLOCK)
        scores = dot_last(queries[part], key_rows) * scaling
        scores = jnp.where(column_ref[part] >= line_ref[...], scores, masked_score)
        probable = jnp.exp(scores - logsum_ref[part])
        product = dot_last(head_grad[part], values)
        slopes = probable * (product - jnp.sum(probable * product, axis=1, keepdims=True))
        slopes = slopes.astype(low)
        query_parts.append(dot(slopes, key_rows) * scaling)
        key_part = dot_first(slopes, queries[part]) * scaling
        value_part = dot_first(probable.astype(low), head_grad[part])
        key_grad = key_part if at == 0 else key_grad + key_part
        value_grad = value_part if at == 0 else value_grad + value_part
    cosine, sine = cosine_ref[...], sine_ref[...]
    undo = lambda g: (g * cosine - turn(g * sine) * rope_sign(depth)).astype(low)
    slope_ref[:, :depth] = undo(jnp.concatenate(query_parts, axis=0))
    slope_ref[:, depth : 2 * depth] = undo(key_grad)
    slope_ref[:, 2 * depth :] = value_grad.astype(low)


def project_kernel(columns, *refs):
    lefts, weights = refs[: len(refs) // 2 - 1], refs[len(refs) // 2 - 1 : -2]
    part = sum(dot_last(left[...], weight[:, columns]) for left, weight in zip(lefts, weights)).astype(low)
    first = 2 * pl.program_id(0) < pl.num_programs(0)

    @pl.when(first)
    def _():
        refs[-2][...] = part

    @pl.when(jnp.logical_not(first))
    def _():
        refs[-1][...] = part


def project(name, columns, lefts, weights, tile=256):
    count, width = lefts[0].shape[0], weights[0].shape[0]
    last = count // tile // HALF - 1
    whole = lambda array: pl.BlockSpec(array.shape, lambda i: (0, 0), pipeline_mode=pl.Buffered(buffer_count=1))
    return pl.pallas_call(
        functools.partial(project_kernel, columns),
        grid=(count // tile,),
        in_specs=[pl.BlockSpec((tile, left.shape[1]), lambda i: (i, 0)) for left in lefts]
        + [whole(weight) for weight in weights],
        out_specs=[
            pl.BlockSpec((tile, width), lambda i: (jnp.minimum(i, last), 0)),
            pl.BlockSpec((tile, width), lambda i: (jnp.maximum(i - last - 1, 0), 0)),
        ],
        out_shape=[jax.ShapeDtypeStruct((count // HALF, width), low)] * HALF,
        compiler_params=pltpu.CompilerParams(vmem_limit_bytes=9 * 1024 * 1024),
        cost_estimate=CHEAP,
        name=name,
    )(*lefts, *weights)


def head_sum_kernel(rows_own, rows_other, middle_own, middle_other, slope_ref, attended_ref, out_ref):
    half = rows_own.shape[0]

    def product(own, other, right):
        return dot_first(own[...], right[:half]) + dot_first(other[...], right[half:])

    parts = [product(rows_own, rows_other, slope_ref), product(middle_own, middle_other, attended_ref)]
    out_ref[0] = jnp.concatenate(parts, axis=1).astype(low)


def gu_sum_kernel(blocks, *refs):
    parts = len(blocks)
    rows, slopes, out_refs = refs[:parts], refs[parts : 2 * parts], refs[2 * parts :]
    rows = [part[...] for part in rows]
    for n, out_ref in enumerate(out_refs):
        size = out_ref.shape[2]
        cuts = [slice(own[n] * size, (own[n] + 1) * size) for own in blocks]
        out_ref[0] = sum(dot_first(left, right[:, cut]) for left, right, cut in zip(rows, slopes, cuts)).astype(low)


def down_sum_kernel(blocks, *refs):
    parts = len(blocks)
    slopes, hiddens, out_refs = refs[:parts], refs[parts : 2 * parts], refs[2 * parts :]
    slopes = [part[...] for part in slopes]
    for n, out_ref in enumerate(out_refs):
        units = out_ref.shape[1]
        cuts = [slice(own[n] * units, (own[n] + 1) * units) for own in blocks]
        out_ref[0] = sum(dot_first(left[:, cut], right) for left, right, cut in zip(hiddens, slopes, cuts)).astype(low)


def call_blocks(kernel, name, cut, held, shapes):
    count = shapes[0][0]
    return pl.pallas_call(
        kernel,
        grid=(count,),
        in_specs=[pl.BlockSpec((array.shape[0], array.shape[1] // count), lambda i: (0, i)) for array in cut]
        + [pl.BlockSpec(array.shape, lambda i: (0, 0)) for array in held],
        out_specs=[pl.BlockSpec((1,) + shape[1:], lambda i: (i, 0, 0)) for shape in shapes],
        out_shape=[jax.ShapeDtypeStruct(shape, low) for shape in shapes],
        compiler_params=pltpu.CompilerParams(vmem_limit_bytes=10 * 1024 * 1024),
        cost_estimate=CHEAP,
        name=name,
    )(*cut, *held)


def assemble_kernel(x_ref, mine_ref, theirs_ref, query_ref, key_ref, value_ref, out_ref):
    line, block, depth = mine_ref.shape[0], mine_ref.shape[1], HEAD_DIM
    for i in range(line):
        for source, turned in ((mine_ref, x_ref[0]), (theirs_ref, 1 - x_ref[0])):
            place = pl.ds(pl.multiple_of((HALF * i + turned) * depth, depth), depth)
            for n, target in enumerate((query_ref, key_ref, value_ref)):
                target[:, place] = source[i, :, n * depth : (n + 1) * depth].astype(wide)
            out_ref[place, :] = source[i, :, 3 * depth :].astype(wide).T


def assemble(mine, theirs):
    line, block, _ = mine.shape
    shape = jax.ShapeDtypeStruct((block, block), wide)
    whole = pl.BlockSpec(memory_space=pltpu.VMEM)
    return pl.pallas_call(
        assemble_kernel,
        in_specs=[pl.BlockSpec(memory_space=pltpu.SMEM), whole, whole],
        out_specs=[whole] * 4,
        out_shape=[shape] * 4,
        cost_estimate=CHEAP,
        name="assemble",
    )(lax.axis_index("x")[None].astype(jnp.int32), mine, theirs)


def assemble_units_kernel(x_ref, mine_ref, theirs_ref, gate_ref, up_ref, down_ref):
    size, units = gate_ref.shape[0], down_ref.shape[0] // HALF
    mine, theirs = mine_ref[0].astype(wide), theirs_ref[0].astype(wide)
    first = jnp.where(x_ref[0] == 0, mine, theirs)
    second = jnp.where(x_ref[0] == 0, theirs, mine)
    gate_ref[...] = jnp.concatenate([first[:size, :units], second[:size, :units]], axis=1)
    up_ref[...] = jnp.concatenate([first[:size, units:], second[:size, units:]], axis=1)
    down_ref[...] = jnp.concatenate([first[size:], second[size:]], axis=0)


def assemble_units(mine, theirs):
    rows, height, size = mine.shape
    share = HALF * (height - size)
    arrived = pl.BlockSpec((1, height, size), lambda i, x: (i, 0, 0))
    columns = pl.BlockSpec((size, share), lambda i, x: (0, i))
    wide_shape = jax.ShapeDtypeStruct((size, rows * share), wide)
    return pl.pallas_call(
        assemble_units_kernel,
        grid_spec=pltpu.PrefetchScalarGridSpec(
            num_scalar_prefetch=1,
            grid=(rows,),
            in_specs=[arrived, arrived],
            out_specs=[columns, columns, pl.BlockSpec((share, size), lambda i, x: (i, 0))],
        ),
        out_shape=[wide_shape, wide_shape, jax.ShapeDtypeStruct((rows * share, size), wide)],
        compiler_params=pltpu.CompilerParams(vmem_limit_bytes=10 * 1024 * 1024),
        cost_estimate=CHEAP,
        name="assemble_units",
    )(lax.axis_index("x")[None].astype(jnp.int32), mine, theirs)


def call_whole(kernel, name, shapes, *arrays):
    whole = pl.BlockSpec(memory_space=pltpu.VMEM)
    return pl.pallas_call(
        kernel,
        in_specs=[whole] * len(arrays),
        out_specs=[whole] * len(shapes),
        out_shape=shapes,
        compiler_params=pltpu.CompilerParams(vmem_limit_bytes=15 * 1024 * 1024),
        cost_estimate=CHEAP,
        name=name,
    )(*arrays)


def dot_last(left, right):
    return lax.dot_general(left, right, (((1,), (1,)), ((), ())), preferred_element_type=wide)


def dot_first(left, right):
    return lax.dot_general(left, right, (((0,), (0,)), ((), ())), preferred_element_type=wide)


def swap(array, axis):
    return lax.ppermute(array, axis, [(0, 1), (1, 0)])


class Ring:
    def __init__(self, axes, line):
        self.axes = axes
        self.size = 2 * line
        self.half = line
        flat = [2 * n if n < line else 2 * (2 * line - 1 - n) + 1 for n in range(self.size)]
        self.upward = [(flat[i], flat[(i + 1) % self.size]) for i in range(self.size)]
        self.downward = [(b, a) for a, b in self.upward]

    def up(self, array):
        return lax.ppermute(array, self.axes, self.upward)

    def down(self, array):
        return lax.ppermute(array, self.axes, self.downward)

    def place(self):
        level, side = lax.axis_index(self.axes[:-1]), lax.axis_index(self.axes[-1])
        return jnp.where(side == 0, level, self.size - 1 - level)

    def gather(self, shard, waits={}):
        half, cut = self.half, shard.shape[0] // 2
        slots = [None] * self.size
        slots[half] = rising = falling = shard
        for step in range(1, half + 1):
            rising, falling = after((rising, falling), waits.get(step))
            if step == half:
                break
            slots[half - step] = rising = self.up(rising)
            slots[half + step] = falling = self.down(falling)
        slots[0] = jnp.concatenate([self.up(rising[:cut]), self.down(falling[cut:])], axis=0)
        return slots

    def scatter_start(self, parts):
        cut = parts[0].shape[0] // 2
        return self.up(parts[0][:cut]), self.down(parts[0][cut:])

    def scatter_step(self, parts, step, moving):
        rising, falling = moving
        cut = rising.shape[0]
        over, under = parts[self.size - step], parts[step]
        if step == 1:
            over = jnp.concatenate([add_low(over[:cut], rising), over[cut:]], axis=0)
            under = jnp.concatenate([under[:cut], add_low(under[cut:], falling)], axis=0)
        else:
            over, under = add_low(over, rising), add_low(under, falling)
        return self.up(over), self.down(under)

    def scatter_end(self, parts, moving):
        return sum(part.astype(wide) for part in (parts[self.half],) + moving)

    def scatter(self, parts):
        moving = self.scatter_start(parts)
        for step in range(1, self.half):
            moving = self.scatter_step(parts, step, moving)
        return self.scatter_end(parts, moving)


def add_low(left, right):
    return (left.astype(wide) + right.astype(wide)).astype(low)


def split_rows(array, count):
    rows = array.shape[0] // count
    return [array[i * rows : (i + 1) * rows] for i in range(count)]


def gather_group(slots):
    own = jnp.concatenate(slots, axis=0)
    return [own, swap(own, "core")]


def scatter_group(ring, own, other, awaited=None):
    total = after(add_low(own, swap(other, "core")), awaited)
    return ring.scatter(split_rows(total, ring.size))


def exchange_rows(array):
    return lax.all_to_all(array, ROW, 0, 0, tiled=True)


ROW = ("zhi", "zlo")


def to_shard(blocks):
    return jnp.transpose(blocks, (1, 0, 2)).reshape(blocks.shape[1], -1)


def from_shards(arrays, seqs):
    rows, count = lax.axis_size(ROW), len(arrays)
    tokens, width = arrays[0].shape[0], arrays[0].shape[1] // rows
    stacked = jnp.concatenate(arrays, axis=0).reshape(count * tokens, rows, width)
    got = exchange_rows(jnp.transpose(stacked, (1, 0, 2)))
    return [
        got[:, i * tokens : (i + 1) * tokens].reshape(seqs, rows * tokens // seqs, width)
        for i in range(count)
    ]


def together(*arrays):
    return lax.optimization_barrier(arrays)


def after(arrays, others):
    if others is None:
        return arrays
    return lax.optimization_barrier((arrays, others))[0]


def sum_pairs(array):
    return lax.psum(array, "pair") if lax.axis_size("pair") > 1 else array


def pack_kernel(x_ref, slope, query, key, value, out, gate, up, down, head, hidden):
    weight = jnp.concatenate([query[...], key[...], value[...], out[...].T], axis=1)
    head[0] = jnp.concatenate([weight, slope[0]], axis=0)
    hidden[0] = jnp.concatenate([jnp.concatenate([gate[...], up[...]], axis=1), down[...]], axis=0)


def pack(slope, query, key, value, out, gate, up, down, line):
    rows, shard, _ = slope.shape
    depth, block = HEAD_DIM, query.shape[0]
    units = gate.shape[1] // rows // HALF
    head_at = lambda r, x: HALF * (r % line) + x[0]
    head_in = pl.BlockSpec((block, depth), lambda r, x: (0, head_at(r, x)))
    out_in = pl.BlockSpec((depth, block), lambda r, x: (head_at(r, x), 0))
    unit_in = pl.BlockSpec((block, units), lambda r, x: (0, HALF * r + x[0]))
    down_in = pl.BlockSpec((units, block), lambda r, x: (HALF * r + x[0], 0))
    slope_in = pl.BlockSpec((1, shard, block), lambda r, x: (r, 0, 0))
    shapes = [(block + shard, 4 * depth), (block + units, block)]
    return pl.pallas_call(
        pack_kernel,
        grid_spec=pltpu.PrefetchScalarGridSpec(
            num_scalar_prefetch=1,
            grid=(rows,),
            in_specs=[slope_in, head_in, head_in, head_in, out_in, unit_in, unit_in, down_in],
            out_specs=[pl.BlockSpec((1,) + shape, lambda r, x: (r, 0, 0)) for shape in shapes],
        ),
        out_shape=[jax.ShapeDtypeStruct((rows,) + shape, low) for shape in shapes],
        name="pack_weights",
    )(lax.axis_index("x")[None].astype(jnp.int32), slope, query, key, value, out, gate, up, down)


def mlp_kernel(blocks, *refs):
    tiles, weights, rest = refs[:4], refs[4 : 4 + blocks], refs[4 + blocks :]
    earlier = rest[0] if len(rest) > 5 else None
    hidden_ref, gu_slope_ref, both_ref, rows_ref, slope_ref = rest[-5:]
    parts, height, span = weights[0].shape
    units = height - span
    rows_ref[...] = jnp.concatenate([tiles[0][...], tiles[2][...]], axis=0)
    slope_ref[...] = jnp.concatenate([tiles[1][...], tiles[3][...]], axis=0)
    cuts = [slice(k * span, (k + 1) * span) for k in range(parts)]
    totals, branches = [None] * parts, [None] * parts
    for i, weight in enumerate(weights):
        gate_up = sum(dot(rows_ref[:, cut], weight[k, :span]) for k, cut in enumerate(cuts))
        gate, up = gate_up[:, :units], gate_up[:, units:]
        sigmoid = 1.0 / (1.0 + jnp.exp(-gate))
        activated = gate * sigmoid
        hidden = (activated * up).astype(low)
        hidden_ref[:, i * units : (i + 1) * units] = hidden
        hidden_grad = sum(dot_last(slope_ref[:, cut], weight[k, span:]) for k, cut in enumerate(cuts))
        gate_slope = hidden_grad * up * sigmoid * (1.0 + gate * (1.0 - sigmoid))
        gu_slope = jnp.concatenate([gate_slope, hidden_grad * activated], axis=1).astype(low)
        gu_slope_ref[:, 2 * i * units : 2 * (i + 1) * units] = gu_slope
        for k in range(parts):
            part, branch = dot_last(gu_slope, weight[k, :span]), dot(hidden, weight[k, span:])
            totals[k] = part if i == 0 else totals[k] + part
            branches[k] = branch if i == 0 else branches[k] + branch
    tile = tiles[0].shape[0]
    for k, cut in enumerate(cuts):
        for n in range(2 * HALF):
            place = slice(n * tile, (n + 1) * tile)
            total = (branches if n % 2 else totals)[k][n // 2 * tile : (n // 2 + 1) * tile]
            if earlier is not None:
                total = total + earlier[place, cut].astype(wide)
            both_ref[place, cut] = total.astype(low)


def feed_forward(both, weights, tile, earlier=()):
    count, width = both.shape[0] // HALF, both.shape[1]
    parts, height, span = weights[0].shape
    blocks, units = len(weights), height - span
    steps = count // (HALF * tile)
    single = lambda n: pl.BlockSpec((tile, width), lambda i: (4 * i + n, 0))
    whole = lambda array: pl.BlockSpec(array.shape, lambda i: (0, 0, 0), pipeline_mode=pl.Buffered(buffer_count=1))
    shapes = [(count, size) for size in (blocks * units, 2 * blocks * units, width, width, width)]
    shapes[2] = both.shape
    return pl.pallas_call(
        functools.partial(mlp_kernel, blocks),
        grid=(steps,),
        in_specs=[single(n) for n in range(4)]
        + [whole(weight) for weight in weights]
        + [pl.BlockSpec((array.shape[0] // steps, width), lambda i: (i, 0)) for array in earlier],
        out_specs=[pl.BlockSpec((shape[0] // steps, shape[1]), lambda i: (i, 0)) for shape in shapes],
        out_shape=[jax.ShapeDtypeStruct(shape, low) for shape in shapes],
        compiler_params=pltpu.CompilerParams(vmem_limit_bytes=22 * 1024 * 1024),
        cost_estimate=CHEAP,
        name="feed_forward",
    )(*[both] * 4, *weights, *earlier)


def on_device(
    tokens,
    query_weight,
    key_weight,
    value_weight,
    out_weight,
    gate_weight,
    up_weight,
    down_weight,
    cotangent,
):
    depth = HEAD_DIM
    rows, line = lax.axis_size(ROW), lax.axis_size("zlo")
    small_ring = Ring(("zlo", "y"), line)
    large_ring = Ring(("zhi", "zlo", "y"), rows)
    seqs, width = tokens.shape[0], tokens.shape[2] * rows
    block = width // rows
    units = gate_weight.shape[1] // rows // HALF

    shard = seqs * tokens.shape[1] // rows
    pieces = [array.reshape(rows, shard, block) for array in (tokens, cotangent)]
    weights = (query_weight, key_weight, value_weight, out_weight, gate_weight, up_weight, down_weight)
    head_pieces, hidden_pieces = pack(pieces[1], *weights, line)
    got = exchange_rows(pieces[0])
    got, head_pieces, hidden_pieces = together(got, head_pieces, hidden_pieces)
    stream = to_shard(got).astype(wide)
    head_got = exchange_rows(head_pieces)

    place = jnp.arange(2 * small_ring.size)
    core = (lax.axis_index("core") + place // small_ring.size) % 2
    spot = (small_ring.place() + place % small_ring.size + small_ring.half) % small_ring.size
    slot_side = spot // line
    slot_level = jnp.where(slot_side == 0, spot, small_ring.size - 1 - spot)
    first = ((2 * slot_side + core) * line + slot_level) * shard
    places = (first[:, None] + jnp.arange(shard)[None, :]).reshape(-1)
    cosine, sine_table = rope_tables(places, depth)

    normed_one, inverse_one = layer_norm(stream)
    rows_slots = small_ring.gather(normed_one.astype(low))
    rows_slots, head_got, hidden_pieces = together(rows_slots, head_got, hidden_pieces)
    rows_one = gather_group(rows_slots)
    heads_weight = [head_got[:, :block].reshape(width, 4 * depth)]
    heads_weight.append(swap(heads_weight[0], "x"))
    slope_low = to_shard(head_got[:, block:])

    hidden_mine = exchange_rows(hidden_pieces)
    hidden_theirs = swap(hidden_mine, "x")
    length = HALF * rows_one[0].shape[0]
    seen = (cosine, sine_table, places[:, None], places[None, :])
    qkv_shape = jax.ShapeDtypeStruct((length, 3 * depth), low)
    kept = []
    for weight in heads_weight:
        shapes = [qkv_shape, jax.ShapeDtypeStruct((length, depth), low), jax.ShapeDtypeStruct((length, 1), wide)]
        kept.append(call_whole(attend_kernel, "attend", shapes, *rows_one, weight, *seen))
    heads = [part[1] for part in kept]
    out_parts = project("out_project", slice(3 * depth, 4 * depth), heads, heads_weight)
    middle = stream + scatter_group(small_ring, *out_parts, hidden_mine)
    normed_two, inverse_two = layer_norm(middle)
    both = jnp.concatenate([normed_two.astype(low), slope_low], axis=0)
    slots, size = [None] * large_ring.size, large_ring.half
    slots[size] = rising = falling = both
    hidden_mine = [hidden_mine, swap(hidden_mine, "core")]
    for step in range(1, size):
        slots[size - step] = rising = large_ring.up(rising)
        slots[size + step] = falling = large_ring.down(falling)
        if step < size - 1:
            rising, falling, hidden_mine = together(rising, falling, hidden_mine)
            slots[size - step], slots[size + step] = rising, falling
    inner = jnp.concatenate(slots[2:6], axis=0)
    inner_mine = feed_forward(inner, hidden_mine, shard)
    rising, falling, inner_mine, inner, hidden_theirs = together(rising, falling, inner_mine, inner, hidden_theirs)
    slots[size - step], slots[size + step] = rising, falling
    last = large_ring.up(rising[:shard]), large_ring.down(falling[shard:])
    hidden_theirs = [hidden_theirs, swap(hidden_theirs, "core")]
    inner_theirs = feed_forward(inner, hidden_theirs, shard, inner_mine[2:3])
    last, inner_theirs, hidden_mine, hidden_theirs = together(last, inner_theirs, hidden_mine, hidden_theirs)
    slots[0] = jnp.concatenate(last, axis=0)
    outer = feed_forward(jnp.concatenate([*slots[6:], *slots[:2]], axis=0), hidden_mine + hidden_theirs, shard)
    both_parts, rows_two, slope_all = [inner_theirs[2], outer[2]], [inner_mine[3], outer[3]], [inner_mine[4], outer[4]]

    def gu_sums(inner_part, outer_at, left):
        kernel = functools.partial(gu_sum_kernel, ((0, 1), (outer_at, outer_at + 1)))
        return call_blocks(kernel, "gu_sum", left, [inner_part[1], outer[1]], [(rows, block, 2 * units)] * 2)

    def down_sums(inner_part, outer_at, left):
        kernel = functools.partial(down_sum_kernel, ((0, 1), (outer_at, outer_at + 1)))
        return call_blocks(kernel, "down_sum", left, [inner_part[0], outer[0]], [(rows, units, block)] * 2)

    def slot_parts(inner, outer):
        outer = split_rows(outer, 4)
        return outer[2:] + split_rows(inner, 4) + outer[:2]

    moving = large_ring.scatter_start(slot_parts(*both_parts))
    gu_own, gu_other = gu_sums(inner_theirs, HALF, rows_two)
    moving, gu_own, gu_other, rows_two, slope_all, both_parts = together(
        moving, gu_own, gu_other, rows_two, slope_all, both_parts
    )
    parts = slot_parts(*both_parts)
    gu_other = swap(gu_other, "core")
    gu_theirs = [add_low(own, other) for own, other in zip(split_rows(gu_own, HALF), split_rows(gu_other, HALF))]
    moving, gu_theirs, rows_two, slope_all = together(moving, gu_theirs, rows_two, slope_all)

    chunks = [swap(gu_theirs[0], "x")]
    moving = large_ring.scatter_step(parts, 1, moving)
    gu_mine, gu_mine_other = gu_sums(inner_mine, 0, rows_two)
    down_own, down_other = down_sums(inner_theirs, HALF, slope_all)
    moving, chunks, gu_theirs, gu_mine, gu_mine_other, slope_all, down_own, down_other = together(
        moving, chunks, gu_theirs, gu_mine, gu_mine_other, slope_all, down_own, down_other
    )
    chunks.append(swap(gu_theirs[1], "x"))
    moving = large_ring.scatter_step(parts, 2, moving)
    down_other = swap(down_other, "core")
    down_mine, down_mine_other = down_sums(inner_mine, 0, slope_all)
    down_theirs = add_low(down_own, down_other)
    gu_mine_other = swap(gu_mine_other, "core")
    moving, chunks, gu_mine, gu_mine_other, down_theirs, down_mine, down_mine_other = together(
        moving, chunks, gu_mine, gu_mine_other, down_theirs, down_mine, down_mine_other
    )
    down_theirs = swap(down_theirs, "x")
    moving = large_ring.scatter_step(parts, 3, moving)
    down_mine = add_low(down_mine, swap(down_mine_other, "core"))
    gu_total = add_low(add_low(gu_mine, gu_mine_other), jnp.concatenate(chunks, axis=0))
    moving, gu_total, down_mine, down_theirs = together(moving, gu_total, down_mine, down_theirs)
    grad_two, branch = split_rows(large_ring.scatter_end(parts, moving), HALF)
    middle_grad = slope_low.astype(wide) + norm_backward(normed_two, inverse_two, grad_two)
    output_low = (middle + branch).astype(low)

    slots = small_ring.gather(middle_grad.astype(low))
    unit_total = jnp.concatenate([gu_total, add_low(down_mine, down_theirs)], axis=1)
    slots, unit_total = together(slots, unit_total)
    unit_got = exchange_rows(sum_pairs(unit_total))
    middle_all = gather_group(slots)

    def head_back(head):
        qkv, attended, logsums = kept[head]
        arrays = (*middle_all, heads_weight[head], *seen, qkv, logsums)
        (slope,) = call_whole(attend_back_kernel, "attend_back", [qkv_shape], *arrays)
        shape = (rows, block, 4 * depth)
        return slope, call_blocks(head_sum_kernel, "head_sum", rows_one + middle_all, [slope, attended], [shape])[0]

    theirs_slope, theirs_sum = head_back(1)
    middle_all, theirs_slope, theirs_sum = together(middle_all, theirs_slope, theirs_sum)
    head_chunks = [swap(theirs_sum[: rows // 2], "x")]
    mine_slope, mine_sum = head_back(0)
    back_parts = project("qkv_back", slice(0, 3 * depth), [mine_slope, theirs_slope], heads_weight)
    back_parts, mine_sum, head_chunks, theirs_sum = together(back_parts, mine_sum, head_chunks, theirs_sum)
    head_chunks.append(swap(theirs_sum[rows // 2 :], "x"))
    back_total = add_low(back_parts[0], swap(back_parts[1], "core"))
    back_total, mine_sum, head_chunks, unit_got = together(back_total, mine_sum, head_chunks, unit_got)

    head_got = exchange_rows(sum_pairs(add_low(mine_sum, jnp.concatenate(head_chunks, axis=0))))
    unit_theirs = swap(unit_got, "x")
    grad_one = small_ring.scatter(split_rows(back_total, small_ring.size))
    input_low = (middle_grad + norm_backward(normed_one, inverse_one, grad_one)).astype(low)
    head_got, unit_theirs, input_low, output_low, unit_got = together(
        head_got, unit_theirs, input_low, output_low, unit_got
    )
    head_got = head_got.reshape(rows // line, line, block, 4 * depth)
    head_mine = jnp.sum(head_got.astype(wide), axis=0).astype(low)
    head_theirs = swap(head_mine, "x")
    layer_out, input_grad = from_shards((output_low, input_low), seqs)
    gate_grad, up_grad, down_grad = assemble_units(unit_got, unit_theirs)
    layer_out, input_grad, head_mine, head_theirs = together(layer_out, input_grad, head_mine, head_theirs)
    input_grad = input_grad.astype(wide)
    query_grad, key_grad, value_grad, out_grad = assemble(head_mine, head_theirs)

    return (
        layer_out,
        input_grad,
        query_grad,
        key_grad,
        value_grad,
        out_grad,
        gate_grad,
        up_grad,
        down_grad,
    )


def solution(mesh):
    dp, rows, cols = (mesh.shape[name] for name in ("dp", "row", "col"))
    sizes = (dp // HALF, HALF, HALF, rows // HALF, cols // HALF, HALF)
    fine = Mesh(mesh.devices.reshape(sizes), ("pair", "x", "zhi", "zlo", "y", "core"))
    across, inner, tall = ("pair", "x"), ("y", "core"), ROW
    split = P(across, inner, tall)
    inward = P(tall, inner)
    outward = P(inner, tall)
    return jax.shard_map(
        on_device,
        mesh=fine,
        in_specs=(split, inward, inward, inward, outward, inward, inward, outward, split),
        out_specs=(split, split, inward, inward, inward, outward, inward, inward, outward),
        check_vma=False,
    )
```

```python
import functools

import jax
import jax.numpy as jnp
from jax import lax
from jax.experimental import pallas as pl
from jax.experimental.pallas import tpu as pltpu
from jax.sharding import Mesh
from jax.sharding import PartitionSpec as P

HEAD_DIM = 128
BLOCK = 256
HALF = 2

epsilon = 1e-05
rope_base = 10000.0
masked_score = -1e30
low = jnp.bfloat16
CHEAP = pl.CostEstimate(flops=1, transcendentals=0, bytes_accessed=1)
wide = jnp.float32


def rope_tables(places, head_depth):
    halfway = head_depth // 2
    position = places.astype(jnp.float32)[:, None]
    frequency = rope_base ** (-(2.0 * jnp.arange(halfway).astype(jnp.float32)) / head_depth)
    angles = position * frequency[None, :]
    cosine = jnp.concatenate([jnp.cos(angles), jnp.cos(angles)], axis=1)
    sine_table = jnp.concatenate([jnp.sin(angles), jnp.sin(angles)], axis=1)
    return (cosine, sine_table)


def dot(left, right):
    return jnp.dot(left, right, preferred_element_type=wide)


def layer_norm(stream):
    average = jnp.mean(stream, axis=1, keepdims=True)
    centered = stream - average
    inverse = lax.rsqrt(jnp.mean(centered * centered, axis=1, keepdims=True) + epsilon)
    return centered * inverse, inverse


def norm_backward(normed, inverse, gradient):
    average = jnp.mean(gradient, axis=1, keepdims=True)
    crossed = jnp.mean(gradient * normed, axis=1, keepdims=True)
    return inverse * (gradient - average - normed * crossed)


def turn(array):
    return pltpu.roll(array, array.shape[1] // 2, 1)


def rope_sign(depth):
    return jnp.where(lax.broadcasted_iota(jnp.int32, (1, depth), 1) < depth // 2, -1.0, 1.0)


def attend_kernel(own_ref, other_ref, weight_ref, cosine_ref, sine_ref, column_ref, line_ref, qkv_ref, heads_ref, logsum_ref):
    depth = heads_ref.shape[1]
    weight = weight_ref[:, : 3 * depth]
    qkv = jnp.concatenate([dot(own_ref[...], weight), dot(other_ref[...], weight)], axis=0)
    cosine, sine = cosine_ref[...], sine_ref[...] * rope_sign(depth)
    rope = lambda w: (w * cosine + turn(w) * sine).astype(low)
    queries, key_rows = rope(qkv[:, :depth]), rope(qkv[:, depth : 2 * depth])
    values = qkv[:, 2 * depth :].astype(low)
    qkv_ref[...] = jnp.concatenate([queries, key_rows, values], axis=1)
    for at in range(0, queries.shape[0], BLOCK):
        part = slice(at, at + BLOCK)
        scores = dot_last(queries[part], key_rows) * depth**-0.5
        scores = jnp.where(column_ref[part] >= line_ref[...], scores, masked_score)
        highest = jnp.max(scores, axis=1, keepdims=True)
        shifted = jnp.exp(scores - highest)
        totals = jnp.sum(shifted, axis=1, keepdims=True)
        logsum_ref[part] = highest + jnp.log(totals)
        weights = (shifted * (1.0 / totals)).astype(low)
        heads_ref[part] = dot(weights, values).astype(low)


def attend_back_kernel(
    own_ref, other_ref, weight_ref, cosine_ref, sine_ref, column_ref, line_ref, qkv_ref, logsum_ref, slope_ref
):
    depth = cosine_ref.shape[1]
    scaling = depth**-0.5
    queries, key_rows, values = (qkv_ref[:, i * depth : (i + 1) * depth] for i in range(3))
    weight = weight_ref[:, 3 * depth :]
    head_grad = jnp.concatenate([dot(own_ref[...], weight), dot(other_ref[...], weight)], axis=0).astype(low)
    query_parts = []
    key_grad = value_grad = None
    for at in range(0, queries.shape[0], BLOCK):
        part = slice(at, at + BLOCK)
        scores = dot_last(queries[part], key_rows) * scaling
        scores = jnp.where(column_ref[part] >= line_ref[...], scores, masked_score)
        probable = jnp.exp(scores - logsum_ref[part])
        product = dot_last(head_grad[part], values)
        slopes = probable * (product - jnp.sum(probable * product, axis=1, keepdims=True))
        slopes = slopes.astype(low)
        query_parts.append(dot(slopes, key_rows) * scaling)
        key_part = dot_first(slopes, queries[part]) * scaling
        value_part = dot_first(probable.astype(low), head_grad[part])
        key_grad = key_part if at == 0 else key_grad + key_part
        value_grad = value_part if at == 0 else value_grad + value_part
    cosine, sine = cosine_ref[...], sine_ref[...]
    undo = lambda g: (g * cosine - turn(g * sine) * rope_sign(depth)).astype(low)
    slope_ref[:, :depth] = undo(jnp.concatenate(query_parts, axis=0))
    slope_ref[:, depth : 2 * depth] = undo(key_grad)
    slope_ref[:, 2 * depth :] = value_grad.astype(low)


def project_kernel(columns, *refs):
    lefts, weights = refs[: len(refs) // 2 - 1], refs[len(refs) // 2 - 1 : -2]
    part = sum(dot_last(left[...], weight[:, columns]) for left, weight in zip(lefts, weights)).astype(low)
    first = 2 * pl.program_id(0) < pl.num_programs(0)

    @pl.when(first)
    def _():
        refs[-2][...] = part

    @pl.when(jnp.logical_not(first))
    def _():
        refs[-1][...] = part


def project(name, columns, lefts, weights, tile=256):
    count, width = lefts[0].shape[0], weights[0].shape[0]
    last = count // tile // HALF - 1
    whole = lambda array: pl.BlockSpec(array.shape, lambda i: (0, 0), pipeline_mode=pl.Buffered(buffer_count=1))
    return pl.pallas_call(
        functools.partial(project_kernel, columns),
        grid=(count // tile,),
        in_specs=[pl.BlockSpec((tile, left.shape[1]), lambda i: (i, 0)) for left in lefts]
        + [whole(weight) for weight in weights],
        out_specs=[
            pl.BlockSpec((tile, width), lambda i: (jnp.minimum(i, last), 0)),
            pl.BlockSpec((tile, width), lambda i: (jnp.maximum(i - last - 1, 0), 0)),
        ],
        out_shape=[jax.ShapeDtypeStruct((count // HALF, width), low)] * HALF,
        compiler_params=pltpu.CompilerParams(vmem_limit_bytes=9 * 1024 * 1024),
        cost_estimate=CHEAP,
        name=name,
    )(*lefts, *weights)


def head_sum_kernel(rows_own, rows_other, middle_own, middle_other, slope_ref, attended_ref, out_ref):
    half = rows_own.shape[0]

    def product(own, other, right):
        return dot_first(own[...], right[:half]) + dot_first(other[...], right[half:])

    parts = [product(rows_own, rows_other, slope_ref), product(middle_own, middle_other, attended_ref)]
    out_ref[0] = jnp.concatenate(parts, axis=1).astype(low)


def gu_sum_kernel(blocks, *refs):
    parts = len(blocks)
    rows, slopes, out_refs = refs[:parts], refs[parts : 2 * parts], refs[2 * parts :]
    rows = [part[...] for part in rows]
    for n, out_ref in enumerate(out_refs):
        size = out_ref.shape[2]
        cuts = [slice(own[n] * size, (own[n] + 1) * size) for own in blocks]
        out_ref[0] = sum(dot_first(left, right[:, cut]) for left, right, cut in zip(rows, slopes, cuts)).astype(low)


def down_sum_kernel(blocks, *refs):
    parts = len(blocks)
    slopes, hiddens, out_refs = refs[:parts], refs[parts : 2 * parts], refs[2 * parts :]
    slopes = [part[...] for part in slopes]
    for n, out_ref in enumerate(out_refs):
        units = out_ref.shape[1]
        cuts = [slice(own[n] * units, (own[n] + 1) * units) for own in blocks]
        out_ref[0] = sum(dot_first(left[:, cut], right) for left, right, cut in zip(hiddens, slopes, cuts)).astype(low)


def call_blocks(kernel, name, cut, held, shapes):
    count = shapes[0][0]
    return pl.pallas_call(
        kernel,
        grid=(count,),
        in_specs=[pl.BlockSpec((array.shape[0], array.shape[1] // count), lambda i: (0, i)) for array in cut]
        + [pl.BlockSpec(array.shape, lambda i: (0, 0)) for array in held],
        out_specs=[pl.BlockSpec((1,) + shape[1:], lambda i: (i, 0, 0)) for shape in shapes],
        out_shape=[jax.ShapeDtypeStruct(shape, low) for shape in shapes],
        compiler_params=pltpu.CompilerParams(vmem_limit_bytes=10 * 1024 * 1024),
        cost_estimate=CHEAP,
        name=name,
    )(*cut, *held)


def assemble_kernel(x_ref, mine_ref, theirs_ref, query_ref, key_ref, value_ref, out_ref):
    line, block, depth = mine_ref.shape[0], mine_ref.shape[1], HEAD_DIM
    for i in range(line):
        for source, turned in ((mine_ref, x_ref[0]), (theirs_ref, 1 - x_ref[0])):
            place = pl.ds(pl.multiple_of((HALF * i + turned) * depth, depth), depth)
            for n, target in enumerate((query_ref, key_ref, value_ref)):
                target[:, place] = source[i, :, n * depth : (n + 1) * depth].astype(wide)
            out_ref[place, :] = source[i, :, 3 * depth :].astype(wide).T


def assemble(mine, theirs):
    line, block, _ = mine.shape
    shape = jax.ShapeDtypeStruct((block, block), wide)
    whole = pl.BlockSpec(memory_space=pltpu.VMEM)
    return pl.pallas_call(
        assemble_kernel,
        in_specs=[pl.BlockSpec(memory_space=pltpu.SMEM), whole, whole],
        out_specs=[whole] * 4,
        out_shape=[shape] * 4,
        cost_estimate=CHEAP,
        name="assemble",
    )(lax.axis_index("x")[None].astype(jnp.int32), mine, theirs)


def assemble_units_kernel(x_ref, mine_ref, theirs_ref, gate_ref, up_ref, down_ref):
    size, units = gate_ref.shape[0], down_ref.shape[0] // HALF
    mine, theirs = mine_ref[0].astype(wide), theirs_ref[0].astype(wide)
    first = jnp.where(x_ref[0] == 0, mine, theirs)
    second = jnp.where(x_ref[0] == 0, theirs, mine)
    gate_ref[...] = jnp.concatenate([first[:size, :units], second[:size, :units]], axis=1)
    up_ref[...] = jnp.concatenate([first[:size, units:], second[:size, units:]], axis=1)
    down_ref[...] = jnp.concatenate([first[size:], second[size:]], axis=0)


def assemble_units(mine, theirs):
    rows, height, size = mine.shape
    share = HALF * (height - size)
    arrived = pl.BlockSpec((1, height, size), lambda i, x: (i, 0, 0))
    columns = pl.BlockSpec((size, share), lambda i, x: (0, i))
    wide_shape = jax.ShapeDtypeStruct((size, rows * share), wide)
    return pl.pallas_call(
        assemble_units_kernel,
        grid_spec=pltpu.PrefetchScalarGridSpec(
            num_scalar_prefetch=1,
            grid=(rows,),
            in_specs=[arrived, arrived],
            out_specs=[columns, columns, pl.BlockSpec((share, size), lambda i, x: (i, 0))],
        ),
        out_shape=[wide_shape, wide_shape, jax.ShapeDtypeStruct((rows * share, size), wide)],
        compiler_params=pltpu.CompilerParams(vmem_limit_bytes=10 * 1024 * 1024),
        cost_estimate=CHEAP,
        name="assemble_units",
    )(lax.axis_index("x")[None].astype(jnp.int32), mine, theirs)


def call_whole(kernel, name, shapes, *arrays):
    whole = pl.BlockSpec(memory_space=pltpu.VMEM)
    return pl.pallas_call(
        kernel,
        in_specs=[whole] * len(arrays),
        out_specs=[whole] * len(shapes),
        out_shape=shapes,
        compiler_params=pltpu.CompilerParams(vmem_limit_bytes=12 * 1024 * 1024),
        cost_estimate=CHEAP,
        name=name,
    )(*arrays)


def dot_last(left, right):
    return lax.dot_general(left, right, (((1,), (1,)), ((), ())), preferred_element_type=wide)


def dot_first(left, right):
    return lax.dot_general(left, right, (((0,), (0,)), ((), ())), preferred_element_type=wide)


def swap(array, axis):
    return lax.ppermute(array, axis, [(0, 1), (1, 0)])


class Ring:
    def __init__(self, axes, line):
        self.axes = axes
        self.size = 2 * line
        self.half = line
        flat = [2 * n if n < line else 2 * (2 * line - 1 - n) + 1 for n in range(self.size)]
        self.upward = [(flat[i], flat[(i + 1) % self.size]) for i in range(self.size)]
        self.downward = [(b, a) for a, b in self.upward]

    def up(self, array):
        return lax.ppermute(array, self.axes, self.upward)

    def down(self, array):
        return lax.ppermute(array, self.axes, self.downward)

    def place(self):
        level, side = lax.axis_index(self.axes[:-1]), lax.axis_index(self.axes[-1])
        return jnp.where(side == 0, level, self.size - 1 - level)

    def gather(self, shard, waits={}):
        half, cut = self.half, shard.shape[0] // 2
        slots = [None] * self.size
        slots[half] = rising = falling = shard
        for step in range(1, half + 1):
            rising, falling = after((rising, falling), waits.get(step))
            if step == half:
                break
            slots[half - step] = rising = self.up(rising)
            slots[half + step] = falling = self.down(falling)
        slots[0] = jnp.concatenate([self.up(rising[:cut]), self.down(falling[cut:])], axis=0)
        return slots

    def scatter_start(self, parts):
        cut = parts[0].shape[0] // 2
        return self.up(parts[0][:cut]), self.down(parts[0][cut:])

    def scatter_step(self, parts, step, moving):
        rising, falling = moving
        cut = rising.shape[0]
        over, under = parts[self.size - step], parts[step]
        if step == 1:
            over = jnp.concatenate([add_low(over[:cut], rising), over[cut:]], axis=0)
            under = jnp.concatenate([under[:cut], add_low(under[cut:], falling)], axis=0)
        else:
            over, under = add_low(over, rising), add_low(under, falling)
        return self.up(over), self.down(under)

    def scatter_end(self, parts, moving):
        return sum(part.astype(wide) for part in (parts[self.half],) + moving)

    def scatter(self, parts):
        moving = self.scatter_start(parts)
        for step in range(1, self.half):
            moving = self.scatter_step(parts, step, moving)
        return self.scatter_end(parts, moving)


def add_low(left, right):
    return (left.astype(wide) + right.astype(wide)).astype(low)


def split_rows(array, count):
    rows = array.shape[0] // count
    return [array[i * rows : (i + 1) * rows] for i in range(count)]


def gather_group(slots):
    own = jnp.concatenate(slots, axis=0)
    return [own, swap(own, "core")]


def scatter_group(ring, own, other, awaited=None):
    total = after(add_low(own, swap(other, "core")), awaited)
    return ring.scatter(split_rows(total, ring.size))


def exchange_rows(array):
    return lax.all_to_all(array, ROW, 0, 0, tiled=True)


ROW = ("zhi", "zlo")


def to_shard(blocks):
    return jnp.transpose(blocks, (1, 0, 2)).reshape(blocks.shape[1], -1)


def from_shards(arrays, seqs):
    rows, count = lax.axis_size(ROW), len(arrays)
    tokens, width = arrays[0].shape[0], arrays[0].shape[1] // rows
    stacked = jnp.concatenate(arrays, axis=0).reshape(count * tokens, rows, width)
    got = exchange_rows(jnp.transpose(stacked, (1, 0, 2)))
    return [
        got[:, i * tokens : (i + 1) * tokens].reshape(seqs, rows * tokens // seqs, width)
        for i in range(count)
    ]


def together(*arrays):
    return lax.optimization_barrier(arrays)


def after(arrays, others):
    if others is None:
        return arrays
    return lax.optimization_barrier((arrays, others))[0]


def sum_pairs(array):
    return lax.psum(array, "pair") if lax.axis_size("pair") > 1 else array


def pack_kernel(x_ref, slope, query, key, value, out, gate, up, down, head, hidden):
    weight = jnp.concatenate([query[...], key[...], value[...], out[...].T], axis=1)
    head[0] = jnp.concatenate([weight, slope[0]], axis=0)
    hidden[0] = jnp.concatenate([jnp.concatenate([gate[...], up[...]], axis=1), down[...]], axis=0)


def pack(slope, query, key, value, out, gate, up, down, line):
    rows, shard, _ = slope.shape
    depth, block = HEAD_DIM, query.shape[0]
    units = gate.shape[1] // rows // HALF
    head_at = lambda r, x: HALF * (r % line) + x[0]
    head_in = pl.BlockSpec((block, depth), lambda r, x: (0, head_at(r, x)))
    out_in = pl.BlockSpec((depth, block), lambda r, x: (head_at(r, x), 0))
    unit_in = pl.BlockSpec((block, units), lambda r, x: (0, HALF * r + x[0]))
    down_in = pl.BlockSpec((units, block), lambda r, x: (HALF * r + x[0], 0))
    slope_in = pl.BlockSpec((1, shard, block), lambda r, x: (r, 0, 0))
    shapes = [(block + shard, 4 * depth), (block + units, block)]
    return pl.pallas_call(
        pack_kernel,
        grid_spec=pltpu.PrefetchScalarGridSpec(
            num_scalar_prefetch=1,
            grid=(rows,),
            in_specs=[slope_in, head_in, head_in, head_in, out_in, unit_in, unit_in, down_in],
            out_specs=[pl.BlockSpec((1,) + shape, lambda r, x: (r, 0, 0)) for shape in shapes],
        ),
        out_shape=[jax.ShapeDtypeStruct((rows,) + shape, low) for shape in shapes],
        name="pack_weights",
    )(lax.axis_index("x")[None].astype(jnp.int32), slope, query, key, value, out, gate, up, down)


def mlp_kernel(blocks, *refs):
    tiles, weights, rest = refs[:4], refs[4 : 4 + blocks], refs[4 + blocks :]
    earlier = rest[0] if len(rest) > 5 else None
    hidden_ref, gu_slope_ref, both_ref, rows_ref, slope_ref = rest[-5:]
    parts, height, span = weights[0].shape
    units = height - span
    rows_ref[...] = jnp.concatenate([tiles[0][...], tiles[2][...]], axis=0)
    slope_ref[...] = jnp.concatenate([tiles[1][...], tiles[3][...]], axis=0)
    cuts = [slice(k * span, (k + 1) * span) for k in range(parts)]
    totals, branches = [None] * parts, [None] * parts
    for i, weight in enumerate(weights):
        gate_up = sum(dot(rows_ref[:, cut], weight[k, :span]) for k, cut in enumerate(cuts))
        gate, up = gate_up[:, :units], gate_up[:, units:]
        sigmoid = 1.0 / (1.0 + jnp.exp(-gate))
        activated = gate * sigmoid
        hidden = (activated * up).astype(low)
        hidden_ref[:, i * units : (i + 1) * units] = hidden
        hidden_grad = sum(dot_last(slope_ref[:, cut], weight[k, span:]) for k, cut in enumerate(cuts))
        gate_slope = hidden_grad * up * sigmoid * (1.0 + gate * (1.0 - sigmoid))
        gu_slope = jnp.concatenate([gate_slope, hidden_grad * activated], axis=1).astype(low)
        gu_slope_ref[:, 2 * i * units : 2 * (i + 1) * units] = gu_slope
        for k in range(parts):
            part, branch = dot_last(gu_slope, weight[k, :span]), dot(hidden, weight[k, span:])
            totals[k] = part if i == 0 else totals[k] + part
            branches[k] = branch if i == 0 else branches[k] + branch
    tile = tiles[0].shape[0]
    for k, cut in enumerate(cuts):
        for n in range(2 * HALF):
            place = slice(n * tile, (n + 1) * tile)
            total = (branches if n % 2 else totals)[k][n // 2 * tile : (n // 2 + 1) * tile]
            if earlier is not None:
                total = total + earlier[place, cut].astype(wide)
            both_ref[place, cut] = total.astype(low)


def feed_forward(both, weights, tile, earlier=()):
    count, width = both.shape[0] // HALF, both.shape[1]
    parts, height, span = weights[0].shape
    blocks, units = len(weights), height - span
    steps = count // (HALF * tile)
    single = lambda n: pl.BlockSpec((tile, width), lambda i: (4 * i + n, 0))
    whole = lambda array: pl.BlockSpec(array.shape, lambda i: (0, 0, 0), pipeline_mode=pl.Buffered(buffer_count=1))
    shapes = [(count, size) for size in (blocks * units, 2 * blocks * units, width, width, width)]
    shapes[2] = both.shape
    return pl.pallas_call(
        functools.partial(mlp_kernel, blocks),
        grid=(steps,),
        in_specs=[single(n) for n in range(4)]
        + [whole(weight) for weight in weights]
        + [pl.BlockSpec((array.shape[0] // steps, width), lambda i: (i, 0)) for array in earlier],
        out_specs=[pl.BlockSpec((shape[0] // steps, shape[1]), lambda i: (i, 0)) for shape in shapes],
        out_shape=[jax.ShapeDtypeStruct(shape, low) for shape in shapes],
        compiler_params=pltpu.CompilerParams(vmem_limit_bytes=22 * 1024 * 1024),
        cost_estimate=CHEAP,
        name="feed_forward",
    )(*[both] * 4, *weights, *earlier)


def on_device(
    tokens,
    query_weight,
    key_weight,
    value_weight,
    out_weight,
    gate_weight,
    up_weight,
    down_weight,
    cotangent,
):
    depth = HEAD_DIM
    rows, line = lax.axis_size(ROW), lax.axis_size("zlo")
    small_ring = Ring(("zlo", "y"), line)
    large_ring = Ring(("zhi", "zlo", "y"), rows)
    seqs, width = tokens.shape[0], tokens.shape[2] * rows
    block = width // rows
    units = gate_weight.shape[1] // rows // HALF

    shard = seqs * tokens.shape[1] // rows
    pieces = [array.reshape(rows, shard, block) for array in (tokens, cotangent)]
    weights = (query_weight, key_weight, value_weight, out_weight, gate_weight, up_weight, down_weight)
    head_pieces, hidden_pieces = pack(pieces[1], *weights, line)
    got = exchange_rows(pieces[0])
    got, head_pieces, hidden_pieces = together(got, head_pieces, hidden_pieces)
    stream = to_shard(got).astype(wide)
    head_got = exchange_rows(head_pieces)

    place = jnp.arange(2 * small_ring.size)
    core = (lax.axis_index("core") + place // small_ring.size) % 2
    spot = (small_ring.place() + place % small_ring.size + small_ring.half) % small_ring.size
    slot_side = spot // line
    slot_level = jnp.where(slot_side == 0, spot, small_ring.size - 1 - spot)
    first = ((2 * slot_side + core) * line + slot_level) * shard
    places = (first[:, None] + jnp.arange(shard)[None, :]).reshape(-1)
    cosine, sine_table = rope_tables(places, depth)

    normed_one, inverse_one = layer_norm(stream)
    rows_slots = small_ring.gather(normed_one.astype(low))
    rows_slots, head_got, hidden_pieces = together(rows_slots, head_got, hidden_pieces)
    rows_one = gather_group(rows_slots)
    heads_weight = [head_got[:, :block].reshape(width, 4 * depth)]
    heads_weight.append(swap(heads_weight[0], "x"))
    slope_low = to_shard(head_got[:, block:])

    hidden_mine = exchange_rows(hidden_pieces)
    hidden_theirs = swap(hidden_mine, "x")
    length = HALF * rows_one[0].shape[0]
    seen = (cosine, sine_table, places[:, None], places[None, :])
    qkv_shape = jax.ShapeDtypeStruct((length, 3 * depth), low)
    kept = []
    for weight in heads_weight:
        shapes = [qkv_shape, jax.ShapeDtypeStruct((length, depth), low), jax.ShapeDtypeStruct((length, 1), wide)]
        kept.append(call_whole(attend_kernel, "attend", shapes, *rows_one, weight, *seen))
    heads = [part[1] for part in kept]
    out_parts = project("out_project", slice(3 * depth, 4 * depth), heads, heads_weight)
    middle = stream + scatter_group(small_ring, *out_parts, hidden_mine)
    normed_two, inverse_two = layer_norm(middle)
    both = jnp.concatenate([normed_two.astype(low), slope_low], axis=0)
    slots, size = [None] * large_ring.size, large_ring.half
    slots[size] = rising = falling = both
    hidden_mine = [hidden_mine, swap(hidden_mine, "core")]
    for step in range(1, size):
        slots[size - step] = rising = large_ring.up(rising)
        slots[size + step] = falling = large_ring.down(falling)
        if step < size - 1:
            rising, falling, hidden_mine = together(rising, falling, hidden_mine)
            slots[size - step], slots[size + step] = rising, falling
    inner = jnp.concatenate(slots[2:6], axis=0)
    inner_mine = feed_forward(inner, hidden_mine, shard)
    rising, falling, inner_mine, inner, hidden_theirs = together(rising, falling, inner_mine, inner, hidden_theirs)
    slots[size - step], slots[size + step] = rising, falling
    last = large_ring.up(rising[:shard]), large_ring.down(falling[shard:])
    hidden_theirs = [hidden_theirs, swap(hidden_theirs, "core")]
    inner_theirs = feed_forward(inner, hidden_theirs, shard, inner_mine[2:3])
    last, inner_theirs, hidden_mine, hidden_theirs = together(last, inner_theirs, hidden_mine, hidden_theirs)
    slots[0] = jnp.concatenate(last, axis=0)
    outer = feed_forward(jnp.concatenate([*slots[6:], *slots[:2]], axis=0), hidden_mine + hidden_theirs, shard)
    both_parts, rows_two, slope_all = [inner_theirs[2], outer[2]], [inner_mine[3], outer[3]], [inner_mine[4], outer[4]]

    def gu_sums(inner_part, outer_at, left):
        kernel = functools.partial(gu_sum_kernel, ((0, 1), (outer_at, outer_at + 1)))
        return call_blocks(kernel, "gu_sum", left, [inner_part[1], outer[1]], [(rows, block, 2 * units)] * 2)

    def down_sums(inner_part, outer_at, left):
        kernel = functools.partial(down_sum_kernel, ((0, 1), (outer_at, outer_at + 1)))
        return call_blocks(kernel, "down_sum", left, [inner_part[0], outer[0]], [(rows, units, block)] * 2)

    def slot_parts(inner, outer):
        outer = split_rows(outer, 4)
        return outer[2:] + split_rows(inner, 4) + outer[:2]

    moving = large_ring.scatter_start(slot_parts(*both_parts))
    gu_own, gu_other = gu_sums(inner_theirs, HALF, rows_two)
    moving, gu_own, gu_other, rows_two, slope_all, both_parts = together(
        moving, gu_own, gu_other, rows_two, slope_all, both_parts
    )
    parts = slot_parts(*both_parts)
    gu_other = swap(gu_other, "core")
    gu_theirs = [add_low(own, other) for own, other in zip(split_rows(gu_own, HALF), split_rows(gu_other, HALF))]
    moving, gu_theirs, rows_two, slope_all = together(moving, gu_theirs, rows_two, slope_all)

    chunks = [swap(gu_theirs[0], "x")]
    moving = large_ring.scatter_step(parts, 1, moving)
    gu_mine, gu_mine_other = gu_sums(inner_mine, 0, rows_two)
    down_own, down_other = down_sums(inner_theirs, HALF, slope_all)
    moving, chunks, gu_theirs, gu_mine, gu_mine_other, slope_all, down_own, down_other = together(
        moving, chunks, gu_theirs, gu_mine, gu_mine_other, slope_all, down_own, down_other
    )
    chunks.append(swap(gu_theirs[1], "x"))
    moving = large_ring.scatter_step(parts, 2, moving)
    down_other = swap(down_other, "core")
    down_mine, down_mine_other = down_sums(inner_mine, 0, slope_all)
    down_theirs = add_low(down_own, down_other)
    gu_mine_other = swap(gu_mine_other, "core")
    moving, chunks, gu_mine, gu_mine_other, down_theirs, down_mine, down_mine_other = together(
        moving, chunks, gu_mine, gu_mine_other, down_theirs, down_mine, down_mine_other
    )
    down_theirs = swap(down_theirs, "x")
    moving = large_ring.scatter_step(parts, 3, moving)
    down_mine = add_low(down_mine, swap(down_mine_other, "core"))
    gu_total = add_low(add_low(gu_mine, gu_mine_other), jnp.concatenate(chunks, axis=0))
    moving, gu_total, down_mine, down_theirs = together(moving, gu_total, down_mine, down_theirs)
    grad_two, branch = split_rows(large_ring.scatter_end(parts, moving), HALF)
    middle_grad = slope_low.astype(wide) + norm_backward(normed_two, inverse_two, grad_two)
    output_low = (middle + branch).astype(low)

    slots = small_ring.gather(middle_grad.astype(low))
    unit_total = jnp.concatenate([gu_total, add_low(down_mine, down_theirs)], axis=1)
    slots, unit_total = together(slots, unit_total)
    unit_got = exchange_rows(sum_pairs(unit_total))
    middle_all = gather_group(slots)

    def head_back(head):
        qkv, attended, logsums = kept[head]
        arrays = (*middle_all, heads_weight[head], *seen, qkv, logsums)
        (slope,) = call_whole(attend_back_kernel, "attend_back", [qkv_shape], *arrays)
        shape = (rows, block, 4 * depth)
        return slope, call_blocks(head_sum_kernel, "head_sum", rows_one + middle_all, [slope, attended], [shape])[0]

    theirs_slope, theirs_sum = head_back(1)
    middle_all, theirs_slope, theirs_sum = together(middle_all, theirs_slope, theirs_sum)
    head_chunks = [swap(theirs_sum[: rows // 2], "x")]
    mine_slope, mine_sum = head_back(0)
    back_parts = project("qkv_back", slice(0, 3 * depth), [mine_slope, theirs_slope], heads_weight)
    back_parts, mine_sum, head_chunks, theirs_sum = together(back_parts, mine_sum, head_chunks, theirs_sum)
    head_chunks.append(swap(theirs_sum[rows // 2 :], "x"))
    back_total = add_low(back_parts[0], swap(back_parts[1], "core"))
    back_total, mine_sum, head_chunks, unit_got = together(back_total, mine_sum, head_chunks, unit_got)

    head_got = exchange_rows(sum_pairs(add_low(mine_sum, jnp.concatenate(head_chunks, axis=0))))
    unit_theirs = swap(unit_got, "x")
    grad_one = small_ring.scatter(split_rows(back_total, small_ring.size))
    input_low = (middle_grad + norm_backward(normed_one, inverse_one, grad_one)).astype(low)
    head_got, unit_theirs, input_low, output_low, unit_got = together(
        head_got, unit_theirs, input_low, output_low, unit_got
    )
    head_got = head_got.reshape(rows // line, line, block, 4 * depth)
    head_mine = jnp.sum(head_got.astype(wide), axis=0).astype(low)
    head_theirs = swap(head_mine, "x")
    layer_out, input_grad = from_shards((output_low, input_low), seqs)
    gate_grad, up_grad, down_grad = assemble_units(unit_got, unit_theirs)
    layer_out, input_grad, head_mine, head_theirs = together(layer_out, input_grad, head_mine, head_theirs)
    input_grad = input_grad.astype(wide)
    query_grad, key_grad, value_grad, out_grad = assemble(head_mine, head_theirs)

    return (
        layer_out,
        input_grad,
        query_grad,
        key_grad,
        value_grad,
        out_grad,
        gate_grad,
        up_grad,
        down_grad,
    )


def solution(mesh):
    dp, rows, cols = (mesh.shape[name] for name in ("dp", "row", "col"))
    sizes = (dp // HALF, HALF, HALF, rows // HALF, cols // HALF, HALF)
    fine = Mesh(mesh.devices.reshape(sizes), ("pair", "x", "zhi", "zlo", "y", "core"))
    across, inner, tall = ("pair", "x"), ("y", "core"), ROW
    split = P(across, inner, tall)
    inward = P(tall, inner)
    outward = P(inner, tall)
    return jax.shard_map(
        on_device,
        mesh=fine,
        in_specs=(split, inward, inward, inward, outward, inward, inward, outward, split),
        out_specs=(split, split, inward, inward, inward, outward, inward, inward, outward),
        check_vma=False,
    )
```
